32 devices in a mesh: grp: 8 (over z, y), rep: 2 (over core), tp: 2 (over x).
Axes of the slice: x: 2, y: 2, z: 4, core: 2. Of those that a mesh axis runs over, the one named last changes fastest.
Arguments:
- hidden: bfloat16 [8, 768, 8192], P('grp', 'rep'), may hold values from -6 to 6
- decode_hidden: bfloat16 [8, 2, 2, 32, 8192], P('grp', 'rep'), may hold values from -6 to 6
- norm_gain: bfloat16 [8192], replicated, may hold values from 0.25 to 1.75
- qkv_weight: bfloat16 [8192, 10240], P('grp', 'tp'), may hold values from -0.0625 to 0.0625
- qkv_bias: bfloat16 [10240], P('tp'), may hold values from -32 to 32
- lengths: int32 [8], replicated, may hold values from 12 to 768, as said below
Outputs:
- prefill_out: bfloat16 [8, 768, 8192], P('grp', 'rep', 'tp')
- decode_out: bfloat16 [8, 2, 2, 32, 8192], P('grp', 'rep', None, None, 'tp')
The draws below stay inside these ranges and needn't reach their ends.
Inputs may be any that keep to these rules, and one draw needn't show every extreme that they name: `lengths`: some prompt is 768 tokens long.
All inputs are finite; a program needn't handle non-finite values.
Results may differ from the reference program's by a relative error of at most 0.012.
The reference program's roundings to bfloat16 on the way count: a program that leaves them out, or rounds other values in their place, can miss the bound.
Values may be sent and summed in bfloat16 or wider, within the bound.
A program may use at most 256 MiB of HBM per device.

```python
import jax
import jax.numpy as jnp
from jax import lax

D = 8192
KVH = 8
HD = 128
QPK = 8
PROMPT = 768
SAMP = 8
STEPS = 4
PROMPTS = 8
N_REP = 2


def draw_qkv_bias(key, part):
    base_bias = jnp.clip(jax.random.normal(jax.random.fold_in(key, 11), (KVH, QPK + 2, HD), jnp.float32), -4.0, 4.0) * 0.5
    return base_bias.reshape(KVH * (QPK + 2) * HD).astype(jnp.bfloat16)


def draw_lengths(key, part):
    shortest = max(1, PROMPT // 64)
    random_lengths = jax.random.randint(jax.random.fold_in(key, 21), (PROMPTS,), shortest, PROMPT + 1)
    longest = jax.random.randint(jax.random.fold_in(key, 22), (), 0, PROMPTS)
    return jnp.where(jnp.arange(PROMPTS) == longest, PROMPT, random_lengths).astype(jnp.int32)


def levels(stream_key, dims, pieces, low, largest):
    level, own = 1.0, jax.random.fold_in(stream_key, 6)
    for dim, parts in pieces:
        heights = jnp.exp(jax.random.uniform(jax.random.fold_in(own, dim), (parts,), jnp.float32, low / len(pieces), largest / len(pieces)))
        level = level * jnp.repeat(heights, dims[dim] // parts).reshape([-1 if axis == dim else 1 for axis in range(len(dims))])
    return level


def gaussian(key, dims, width, reach, pieces=(), held_as=jnp.bfloat16):
    values = jax.random.normal(key, dims, jnp.float32) * width
    if len(pieces) > 0:
        values = levels(key, dims, pieces, -0.22, 0.18) * values
    return jnp.clip(values, min=-reach, max=reach).astype(held_as)


def setup_inputs(seed: int = 0) -> dict:
    seeds = jax.random.split(jax.random.key(seed), 7)
    hidden = gaussian(seeds[0], (PROMPTS, PROMPT, D), 1.0, 6.0, ((0, 8), (1, 2)))
    decode_hidden = gaussian(seeds[1], (PROMPTS, N_REP, 2, SAMP * STEPS, D), 1.0, 6.0, ((0, 8), (1, 2)))
    norm_gain = jnp.clip(1.0 + 0.15 * jax.random.normal(seeds[2], (D,), jnp.float32), 0.25, 1.75).astype(jnp.bfloat16)
    qkv_weight = gaussian(seeds[3], (D, KVH * (QPK + 2) * HD), D ** -0.5, 0.0625, ((0, 8), (1, 2)))
    qkv_bias = draw_qkv_bias(jax.random.fold_in(seeds[6], 71), 0)
    lengths = draw_lengths(jax.random.fold_in(seeds[6], 71), 0)
    return dict(hidden=hidden, decode_hidden=decode_hidden, norm_gain=norm_gain, qkv_weight=qkv_weight, qkv_bias=qkv_bias, lengths=lengths)


THETA = 1000000.0
EPSILON = 1e-06
NEGATIVE = -1e+30

def normalize(row_block, gain_row):
    widened = row_block.astype(jnp.float32)
    factor = lax.rsqrt(lax.optimization_barrier(jnp.mean(widened * widened, axis=-1, keepdims=True)) + EPSILON)
    return (widened * factor * gain_row.astype(jnp.float32)).astype(jnp.bfloat16)

def rope_tables(positions):
    half_size = HD // 2
    frequency = THETA ** (-(jnp.arange(half_size, dtype=jnp.float32) * 2.0 / HD))
    angle = positions.astype(jnp.float32)[:, None] * frequency[None, :]
    return (jnp.cos(angle), jnp.sin(angle))

def rotate(vector, cosine, sine_part):
    half_size = vector.shape[-1] // 2
    first_half = vector[..., :half_size]
    second = vector[..., half_size:]
    return jnp.concatenate([first_half * cosine - second * sine_part, second * cosine + first_half * sine_part], axis=-1)

def qkv_rows(row_block, positions, norm_gain, qkv_weight, qkv_bias):
    normed = normalize(row_block, norm_gain)
    projected = jnp.dot(normed, qkv_weight, preferred_element_type=jnp.float32) + qkv_bias.astype(jnp.float32)
    projected = projected.reshape(row_block.shape[0], KVH, QPK + 2, HD)
    cosine, sine_part = rope_tables(positions)
    query_matrix = rotate(projected[:, :, :QPK], cosine[:, None, None, :], sine_part[:, None, None, :]).astype(jnp.bfloat16)
    key_matrix_rows = rotate(projected[:, :, QPK], cosine[:, None, :], sine_part[:, None, :]).astype(jnp.bfloat16)
    value_matrix = projected[:, :, QPK + 1].astype(jnp.bfloat16)
    return (query_matrix, key_matrix_rows, value_matrix)

def attend(head_query, head_keys, per_head_value_rows, allowed):
    scores = jnp.einsum('nqd,md->qnm', head_query.astype(jnp.float32), head_keys.astype(jnp.float32)) * HD ** (-0.5)
    highest = lax.optimization_barrier(jnp.max(jnp.where(allowed[None], scores, NEGATIVE), axis=-1, keepdims=True))
    exponent = jnp.where(allowed[None], jnp.exp(scores - highest), 0.0)
    running = lax.optimization_barrier(jnp.sum(exponent, axis=-1, keepdims=True))
    weight_matrix = (exponent / running).astype(jnp.bfloat16)
    return jnp.einsum('qnm,md->nqd', weight_matrix.astype(jnp.float32), per_head_value_rows.astype(jnp.float32))

def heads_attend(query_matrix, key_matrix_rows, value_matrix, allowed):

    def single_head(item_tuple):
        head_query, head_keys, per_head_value_rows = item_tuple
        return attend(head_query, head_keys, per_head_value_rows, allowed)
    result = lax.map(single_head, (jnp.swapaxes(query_matrix, 0, 1), jnp.swapaxes(key_matrix_rows, 0, 1), jnp.swapaxes(value_matrix, 0, 1)))
    return jnp.swapaxes(result, 0, 1)

def reference(hidden, decode_hidden, norm_gain, qkv_weight, qkv_bias, lengths):

    def prefill_one(item_tuple):
        row_block, valid_len = item_tuple
        positions = jnp.arange(PROMPT, dtype=jnp.int32)
        query_matrix, key_matrix_rows, value_matrix = qkv_rows(row_block, positions, norm_gain, qkv_weight, qkv_bias)
        allowed = (positions[None, :] <= positions[:, None]) & (positions[None, :] < valid_len)
        result = heads_attend(query_matrix, key_matrix_rows, value_matrix, allowed)
        return (result.astype(jnp.bfloat16).reshape(PROMPT, KVH * QPK * HD), key_matrix_rows, value_matrix)
    prefill_out, keys_all, values_all = lax.map(prefill_one, (hidden, lengths))

    def decode_group(row_block, prompt_keys, prompt_values, valid_len):
        row_ids = jnp.arange(SAMP * STEPS, dtype=jnp.int32)
        step_ids = row_ids % STEPS
        sample_ids = row_ids // STEPS
        positions = valid_len + step_ids
        query_matrix, key_matrix_rows, value_matrix = qkv_rows(row_block, positions, norm_gain, qkv_weight, qkv_bias)
        all_keys = jnp.concatenate([prompt_keys, key_matrix_rows], axis=0)
        all_values = jnp.concatenate([prompt_values, value_matrix], axis=0)
        prompt_allowed = jnp.broadcast_to((jnp.arange(PROMPT, dtype=jnp.int32) < valid_len)[None, :], (SAMP * STEPS, PROMPT))
        own_allowed = (sample_ids[None, :] == sample_ids[:, None]) & (step_ids[None, :] <= step_ids[:, None])
        allowed = jnp.concatenate([prompt_allowed, own_allowed], axis=1)
        result = heads_attend(query_matrix, all_keys, all_values, allowed)
        return result.astype(jnp.bfloat16).reshape(SAMP * STEPS, KVH * QPK * HD)

    def decode_one(item_tuple):
        grp_index, rows_all = item_tuple
        results = []
        for rep_index in range(N_REP):
            pair_list = []
            for side_index in range(2):
                prompt = (grp_index + side_index * (PROMPTS // 2)) % PROMPTS
                pair_list.append(decode_group(rows_all[rep_index, side_index], keys_all[prompt], values_all[prompt], lengths[prompt]))
            results.append(jnp.stack(pair_list))
        return jnp.stack(results)
    decode_out = lax.map(decode_one, (jnp.arange(PROMPTS, dtype=jnp.int32), decode_hidden))
    return (prefill_out, decode_out)
```

```python
import jax
import jax.numpy as jnp
from jax import lax
from jax.experimental import pallas as pl
from jax.experimental.pallas import tpu as pltpu
from jax.sharding import PartitionSpec as P
import functools
import math

HD = 128
QPK = 8
STEPS = 4


THETA = 1000000.0
EPSILON = 1e-06
NEGATIVE = -1e30


def shifted(block, axis, distance):
    devices = range(lax.axis_size(axis))
    route = [((i - distance) % len(devices), i) for i in devices]
    return lax.ppermute(block, axis, route)


def normalize(row_block, gain_row):
    widened = row_block.astype(jnp.float32)
    factor = lax.rsqrt(jnp.mean(widened * widened, axis=-1, keepdims=True) + EPSILON)
    return (widened * factor * gain_row.astype(jnp.float32)).astype(jnp.bfloat16)


def rope_tables(positions, head_size):
    half_size = head_size // 2
    frequency = THETA ** (-(jnp.arange(half_size, dtype=jnp.float32) * 2.0 / head_size))
    angle = positions.astype(jnp.float32)[:, None] * frequency[None, :]
    return (jnp.cos(angle), jnp.sin(angle))


def rotate(vector, cosine, sine_part):
    half_size = vector.shape[-1] // 2
    first_half = vector[..., :half_size]
    second = vector[..., half_size:]
    return jnp.concatenate(
        [first_half * cosine - second * sine_part, second * cosine + first_half * sine_part],
        axis=-1,
    )


def masked_max(scores, allowed):
    return jnp.max(jnp.where(allowed, scores, NEGATIVE), axis=-1, keepdims=True)


def combine_values(weight_matrix, value_matrix):
    return jnp.einsum(
        "aprk,kaz->rapz",
        weight_matrix.astype(jnp.bfloat16),
        value_matrix,
        preferred_element_type=jnp.float32,
    )


def pair_scores(query_matrix, key_matrix_rows, score_scale):
    return (
        jnp.einsum(
            "wjro,ujo->jrwu", query_matrix, key_matrix_rows, preferred_element_type=jnp.float32
        )
        * score_scale
    )


def decode_pair(
    query_matrix,
    own_keys,
    own_values,
    prompt_keys,
    prompt_values,
    valid_len,
    local_allowed,
    score_scale,
):
    key_slot_index = jnp.arange(prompt_keys.shape[0], dtype=jnp.int32)
    prompt_allowed = (key_slot_index < valid_len)[None, None, None, :]
    far_scores = pair_scores(query_matrix, prompt_keys, score_scale)
    near_scores = pair_scores(query_matrix, own_keys, score_scale)
    highest = jnp.maximum(
        masked_max(far_scores, prompt_allowed), masked_max(near_scores, local_allowed)
    )
    far_exp = jnp.where(prompt_allowed, jnp.exp(far_scores - highest), 0.0)
    near_exp = jnp.where(local_allowed, jnp.exp(near_scores - highest), 0.0)
    running = jnp.sum(far_exp, axis=-1, keepdims=True) + jnp.sum(near_exp, axis=-1, keepdims=True)
    return combine_values(far_exp / running, prompt_values) + combine_values(
        near_exp / running, own_values
    )


def plain_device(hidden, decode_hidden, norm_gain, qkv_weight, qkv_bias, lengths):
    prompt_count = lax.axis_size("grp")
    rep_count = lax.axis_size("rep")
    half_cycle = prompt_count // 2
    grp_here = lax.axis_index("grp")
    rep_here = lax.axis_index("rep")
    span_rows = hidden.shape[1]
    model_width = hidden.shape[2]
    head_block = (QPK + 2) * HD
    heads_here = qkv_bias.shape[0] // head_block
    decode_rows = decode_hidden.shape[3]
    score_scale = HD ** (-0.5)
    prefill_normed = normalize(hidden[0], norm_gain)
    decode_normed = normalize(decode_hidden.reshape(2 * decode_rows, model_width), norm_gain)
    normed = jnp.concatenate([prefill_normed, decode_normed], axis=0)
    share_cols = qkv_weight.shape[1] // rep_count
    own_cols = lax.dynamic_slice_in_dim(qkv_weight, rep_here * share_cols, share_cols, 1)
    columns = lax.all_gather(own_cols, "grp", axis=0, tiled=True)
    complete = lax.all_gather(columns, "rep", axis=1, tiled=True)
    projected = jnp.dot(normed, complete, preferred_element_type=jnp.float32)
    projected = (projected + qkv_bias.astype(jnp.float32)).reshape(
        normed.shape[0], heads_here, QPK + 2, HD
    )
    index_table = jnp.arange(prompt_count, dtype=jnp.int32)

    def length_of(prompt):
        return jnp.sum(jnp.where(index_table == prompt, lengths, 0))

    own_len = length_of(grp_here)
    far_len = length_of((grp_here + half_cycle) % prompt_count)
    row_position = rep_here * span_rows + jnp.arange(span_rows, dtype=jnp.int32)
    local_ids = jnp.arange(decode_rows, dtype=jnp.int32)
    step_ids = local_ids % STEPS
    sample_ids = local_ids // STEPS
    positions = jnp.concatenate([row_position, own_len + step_ids, far_len + step_ids])
    cosine, sine_part = rope_tables(positions, HD)
    query_matrix = rotate(
        projected[:, :, :QPK], cosine[:, None, None, :], sine_part[:, None, None, :]
    ).astype(jnp.bfloat16)
    key_matrix_rows = rotate(
        projected[:, :, QPK], cosine[:, None, :], sine_part[:, None, :]
    ).astype(jnp.bfloat16)
    value_matrix = projected[:, :, QPK + 1].astype(jnp.bfloat16)
    cache_keys, cache_values = (
        lax.all_gather(key_matrix_rows[:span_rows], "rep", axis=0, tiled=True),
        lax.all_gather(value_matrix[:span_rows], "rep", axis=0, tiled=True),
    )
    key_pos = jnp.arange(cache_keys.shape[0], dtype=jnp.int32)
    allowed = ((key_pos[None, :] <= row_position[:, None]) & (key_pos[None, :] < own_len))[
        None, None
    ]
    scores = pair_scores(query_matrix[:span_rows], cache_keys, score_scale)
    highest = masked_max(scores, allowed)
    exponent = jnp.where(allowed, jnp.exp(scores - highest), 0.0)
    weight_matrix = exponent / jnp.sum(exponent, axis=-1, keepdims=True)
    attended = combine_values(weight_matrix, cache_values)
    prefill_out = attended.astype(jnp.bfloat16).reshape(1, span_rows, heads_here * QPK * HD)
    decode_queries = query_matrix[span_rows:].reshape(2, decode_rows, heads_here, QPK, HD)
    decode_keys = key_matrix_rows[span_rows:].reshape(2, decode_rows, heads_here, HD)
    decode_values = value_matrix[span_rows:].reshape(2, decode_rows, heads_here, HD)
    local_allowed = (
        (sample_ids[None, :] == sample_ids[:, None]) & (step_ids[None, :] <= step_ids[:, None])
    )[None, None]
    near_out = decode_pair(
        decode_queries[0],
        decode_keys[0],
        decode_values[0],
        cache_keys,
        cache_values,
        own_len,
        local_allowed,
        score_scale,
    )
    far_keys, far_values = shifted((cache_keys, cache_values), "grp", half_cycle)
    far_out = decode_pair(
        decode_queries[1],
        decode_keys[1],
        decode_values[1],
        far_keys,
        far_values,
        far_len,
        local_allowed,
        score_scale,
    )
    decode_out = (
        jnp.stack([near_out, far_out])
        .astype(jnp.bfloat16)
        .reshape(1, 1, 2, decode_rows, heads_here * QPK * HD)
    )
    return (prefill_out, decode_out)


MESH = pl.DeviceIdType.MESH
SUBS = 2
GROUPS = QPK // 2 + 1
WIDE = 2 * HD


def gather_kernel(
    hidden_ref, decode_ref, gain_ref, w_ref,
    acc_ref, wbuf_ref, land_ref,
    xh_ref, nv_ref, wt_ref, accp_ref, pb_ref,
    wi_s, wo_s, wb_s, wy_s, w_r,
    xa_s, xb_s, xc_s, xd_s, xf_s, x_r,
    p_s, p_r, l_s, t_s,
):
    g = lax.axis_index("grp")
    r = lax.axis_index("rep")
    x = lax.axis_index("tp")
    z = g // 2
    y = g % 2
    hi = z // 2
    zin = z + 1 - 2 * hi
    zout = z - 1 + 2 * hi
    mid = (z == 1) | (z == 2)
    end = (z == 0) | (z == 3)
    home = r == y
    away = r != y
    span = hidden_ref.shape[1]
    drows = decode_ref.shape[3]
    share = w_ref.shape[0]
    cols = acc_ref.shape[1]
    head = cols // 2
    half = xh_ref.shape[2]
    rows_all = acc_ref.shape[0]
    sub = span // SUBS
    sides = 4

    barrier = pltpu.get_barrier_semaphore()

    def greet(grp, rep, tp):
        pl.semaphore_signal(
            barrier, inc=1, device_id={"grp": grp, "rep": rep, "tp": tp}, device_id_type=MESH
        )

    pair = 2 * z + 1 - y
    greet(g, 1 - r, x)
    greet(g, r, 1 - x)
    for c in (0, 1):
        greet(pair, c, x)
        greet((g + 4) % 8, c, x)
        greet(2 * zin + y, c, x)

    @pl.when(mid)
    def _():
        for c in (0, 1):
            greet(2 * zout + y, c, x)
        pl.semaphore_wait(barrier, 10)

    @pl.when(end)
    def _():
        pl.semaphore_wait(barrier, 8)

    def offset(k):
        return ((k + GROUPS - 1) % GROUPS) * WIDE

    def own_cols(line, h, k):
        return w_ref.at[:, pl.ds(pl.multiple_of(line * cols + h * head + offset(k), 128), WIDE)]

    def remote(src, dst, ssem, rsem, **device):
        return pltpu.make_async_remote_copy(
            src, dst, ssem, rsem, device_id=device, device_id_type=MESH
        )

    def w_copy(o, k, own, kind):
        src = own_cols(y, r, k) if own else wbuf_ref.at[o, k, r]
        dst = wbuf_ref.at[o, k, r]
        if kind == 0:
            return remote(src, dst, wi_s.at[o, k], w_r.at[o, k, r], grp=2 * zin + y)
        if kind == 1:
            return remote(src, dst, wo_s.at[o, k], w_r.at[o, k, r], grp=2 * zout + y)
        return remote(src, dst, wb_s.at[o, k], w_r.at[o, k, r], rep=1 - r)

    def w_cross(k):
        return remote(own_cols(1 - y, r, k), wbuf_ref.at[g, k, r], wy_s.at[k], w_r.at[g, k, r], grp=pair)

    def w_arrived(o, k, h):
        remote(wbuf_ref.at[o, k, h], wbuf_ref.at[o, k, h], wb_s.at[o, k], w_r.at[o, k, h], rep=1 - r).wait_recv()

    def own_sends(k):
        w_cross(k).start()
        w_copy(g, k, True, 0).start()

        @pl.when(mid)
        def _():
            w_copy(g, k, True, 1).start()

    own_sends(0)
    own_sends(1)

    raw = [
        pltpu.make_async_copy(decode_ref.at[0, 0, 1], nv_ref.at[pl.ds(span + drows, drows), :], l_s.at[0]),
        pltpu.make_async_copy(decode_ref.at[0, 0, 0], nv_ref.at[pl.ds(span, drows), :], l_s.at[1]),
        pltpu.make_async_copy(hidden_ref.at[0], nv_ref.at[pl.ds(0, span), :], l_s.at[2]),
    ]
    for copy in raw:
        copy.start()

    @pl.loop(0, rows_all // 16)
    def _(i):
        acc_ref[pl.ds(pl.multiple_of(i * 16, 16), 16), :] = jnp.zeros((16, cols), jnp.float32)

    gain = gain_ref[...].astype(jnp.float32)

    def norm(first, n):
        @pl.loop(0, n // 16)
        def _(i):
            rows = pl.ds(pl.multiple_of(first + i * 16, 16), 16)
            wide = nv_ref[rows, :].astype(jnp.float32)
            factor = lax.rsqrt(jnp.mean(wide * wide, axis=-1, keepdims=True) + EPSILON)
            nv_ref[rows, :] = (wide * factor * gain).astype(jnp.bfloat16)

    def place(piece, rr):
        if piece < SUBS:
            return pl.multiple_of(rr * span + piece * sub, 16), sub
        return pl.multiple_of(2 * span + ((piece - SUBS) * 2 + rr) * drows, 16), drows

    def source(piece, k_half):
        start, n = (piece * sub, sub) if piece < SUBS else (span + (piece - SUBS) * drows, drows)
        return nv_ref.at[pl.ds(start, n), pl.ds(pl.multiple_of(k_half * half, 128), half)]

    def spot(slot, piece, rr):
        start, n = place(piece, rr)
        return xh_ref.at[slot, pl.ds(start, n), :]

    near_half = hi
    far_half = 1 - hi
    far_layer = (z + 2) % 4

    def x_to_home(piece, slot, k_half):
        return remote(source(piece, k_half), spot(slot, piece, r), xa_s.at[slot, piece], x_r.at[slot, piece, r], rep=y)

    def x_local(piece, slot, k_half):
        return pltpu.make_async_copy(source(piece, k_half), spot(slot, piece, r), x_r.at[slot, piece, r])

    def x_to_away(piece):
        slot = jnp.where(mid, x, 0)
        k_half = hi + slot * (1 - 2 * hi)
        return remote(source(piece, k_half), spot(slot, piece, r), xb_s.at[piece], x_r.at[slot, piece, r], grp=pair, rep=y)

    def x_to_mid(piece):
        return remote(
            source(piece, far_half), spot(2, piece, r), xc_s.at[piece], x_r.at[2, piece, r], grp=2 * zin + y, rep=y
        )

    FAR = SUBS + 1
    NEAR = SUBS

    def x_far(which):
        if which == 0:
            return remote(
                source(FAR, far_half), spot(0, FAR, r), xd_s.at[0], x_r.at[0, FAR, r], grp=(g + 4) % 8, rep=y
            )
        slot = jnp.where(mid, 2, 1)
        layer = jnp.where(mid, zin, far_layer)
        return remote(
            source(FAR, near_half), spot(slot, FAR, r), xd_s.at[1], x_r.at[slot, FAR, r], grp=2 * layer + y, rep=y
        )

    def send_piece(piece):
        x_to_away(piece).start()

        @pl.when(end)
        def _():
            x_to_mid(piece).start()

        @pl.when(home)
        def _():
            x_local(piece, 0, near_half).start()

            @pl.when(mid)
            def _():
                x_local(piece, 1, far_half).start()

        @pl.when(away)
        def _():
            x_to_home(piece, 0, near_half).start()

            @pl.when(mid)
            def _():
                x_to_home(piece, 1, far_half).start()

    raw[0].wait()
    norm(span + drows, drows)
    x_far(0).start()
    x_far(1).start()
    raw[1].wait()
    norm(span, drows)
    send_piece(NEAR)
    raw[2].wait()
    for s in range(SUBS):
        norm(s * sub, sub)
        send_piece(s)

    def x_forward(slot, piece, rr, **device):
        return remote(
            spot(slot, piece, rr), spot(slot, piece, rr), xf_s.at[slot, piece, rr], x_r.at[slot, piece, rr], **device
        )

    def x_arrived(slot, piece, rr):
        x_forward(slot, piece, rr, rep=1 - r).wait_recv()

    def pass_on(slot, pieces, device, act):
        for piece in pieces:
            for rr in (0, 1):
                act(slot, piece, rr, device)

    def relay(slot, piece, rr, device):
        x_arrived(slot, piece, rr)
        x_forward(slot, piece, rr, **device).start()

    def settle(slot, piece, rr, device):
        x_forward(slot, piece, rr, **device).wait_send()

    across = {"grp": pair}
    beside = {"tp": 1 - x}

    def forward_x(stage, act):
        pieces = [stage]
        fars = []
        if stage == 0:
            pieces = [NEAR, 0]
            fars = [FAR]

        @pl.when(home)
        def _():
            pass_on(0, fars, across, act)

            @pl.when(mid)
            def _():
                pass_on(1, fars, across, act)
                pass_on(2, fars + pieces, across, act)

        @pl.when(away & mid)
        def _():
            pass_on(x, pieces, beside, act)

    def wait_x():
        main = [NEAR] + list(range(SUBS))

        @pl.when(home)
        def _():
            def both(slot, k_half):
                for piece in main:
                    x_local(piece, slot, k_half).wait()
                    x_arrived(slot, piece, 1 - r)

            both(0, near_half)

            @pl.when(mid)
            def _():
                both(1, far_half)

        @pl.when(away)
        def _():
            def every(slot, pieces):
                for piece in pieces:
                    for rr in (0, 1):
                        x_arrived(slot, piece, rr)

            every(0, [FAR])

            @pl.when(mid)
            def _():
                every(1 - x, main)
                every(1, [FAR])
                every(2, main + [FAR])

            @pl.when(end)
            def _():
                every(0, main)

    def relay_w(k):
        other = pair
        w_arrived(other, k, r)
        w_copy(other, k, False, 0).start()

        @pl.when(mid)
        def _():
            w_copy(other, k, False, 1).start()

        w_copy(other, k, False, 2).start()

        @pl.when(mid)
        def _():
            for yy in (y, 1 - y):
                o = 2 * zout + yy
                w_arrived(o, k, r)
                w_copy(o, k, False, 0).start()
                w_copy(o, k, False, 2).start()
            for layer in (zin, zin + 1 - 2 * hi):
                for yy in (y, 1 - y):
                    o = 2 * layer + yy
                    w_arrived(o, k, r)
                    w_copy(o, k, False, 2).start()
            for yy in (0, 1):
                w_arrived(2 * zout + yy, k, 1 - r)
            for i in range(sides):
                w_arrived(sides * (1 - hi) + i, k, 1 - r)

        @pl.when(end)
        def _():
            for yy in (y, 1 - y):
                o = 2 * zin + yy
                w_arrived(o, k, r)
                w_copy(o, k, False, 2).start()
            for yy in (0, 1):
                w_arrived(2 * zin + yy, k, 1 - r)

        w_arrived(other, k, 1 - r)

    def p_copy(k):
        return remote(pb_ref.at[k % 2], land_ref.at[k], p_s.at[k], p_r.at[k], grp=2 * zout + y)

    def fetch(k, o, slot):
        for h in (0, 1):
            dst = wt_ref.at[slot, h]

            @pl.when(o == g)
            def _():
                pltpu.make_async_copy(own_cols(y, h, k), dst, t_s.at[slot, h]).start()

            @pl.when(o != g)
            def _():
                pltpu.make_async_copy(wbuf_ref.at[o, k, h], dst, t_s.at[slot, h]).start()

    def compute(k):
        @pl.when(mid)
        def _():
            @pl.loop(0, rows_all // 16)
            def _(i):
                accp_ref[pl.ds(pl.multiple_of(i * 16, 16), 16), :] = jnp.zeros((16, 2 * WIDE), jnp.float32)

            fetch(k, sides * (1 - hi), 0)

        @pl.when(end)
        def _():
            fetch(k, sides * hi, 0)

        @pl.loop(0, 2 * sides)
        def _(j):
            o = (sides * (1 - hi) + j) % (2 * sides)
            slot = j % 2

            @pl.when((j >= sides) | mid)
            def _():
                @pl.when(j + 1 < 2 * sides)
                def _():
                    fetch(k, (sides * (1 - hi) + j + 1) % (2 * sides), (j + 1) % 2)

                for h in (0, 1):
                    pltpu.make_async_copy(wbuf_ref.at[0, 0, h], wt_ref.at[slot, h], t_s.at[slot, h]).wait()
                span_k = pl.ds(pl.multiple_of((o % sides) * share, 128), share)
                which = 1 - j // sides
                for h in (0, 1):
                    place_h = pl.ds(pl.multiple_of(h * head + offset(k), 128), WIDE)
                    acc_ref[:, place_h] += jnp.dot(
                        xh_ref[which, :, span_k], wt_ref[slot, h], preferred_element_type=jnp.float32
                    )

                @pl.when(j < sides)
                def _():
                    for h in (0, 1):
                        accp_ref[:, h * WIDE:(h + 1) * WIDE] += jnp.dot(
                            xh_ref[2, :, span_k], wt_ref[slot, h], preferred_element_type=jnp.float32
                        )

                @pl.when(j == sides - 1)
                def _():
                    @pl.when(k >= 2)
                    def _():
                        p_copy(k - 2).wait_send()

                    @pl.loop(0, rows_all // 16)
                    def _(i):
                        rows = pl.ds(pl.multiple_of(i * 16, 16), 16)
                        pb_ref[k % 2, rows, :] = accp_ref[rows, :].astype(jnp.bfloat16)

                    p_copy(k).start()

    @pl.loop(0, GROUPS)
    def _(k):
        @pl.when(k + 2 < GROUPS)
        def _():
            own_sends(k + 2)

        relay_w(k)
        for stage in range(SUBS):
            @pl.when(k == stage)
            def _():
                forward_x(stage, relay)

        @pl.when(k == 1)
        def _():
            wait_x()

        @pl.loop(0, GROUPS)
        def _(c):
            @pl.when(((k == 1) & (c <= 1)) | ((k >= 2) & (c == k)))
            def _():
                compute(c)

    @pl.when(end)
    def _():
        @pl.loop(0, GROUPS)
        def _(k):
            remote(pb_ref.at[0], land_ref.at[k], p_s.at[k], p_r.at[k], grp=2 * zin + y).wait_recv()
            take = pltpu.make_async_copy(land_ref.at[k], pb_ref.at[0], l_s.at[3])
            take.start()
            take.wait()

            @pl.loop(0, rows_all // 16)
            def _(i):
                rows = pl.ds(pl.multiple_of(i * 16, 16), 16)
                for h in (0, 1):
                    place_h = pl.ds(pl.multiple_of(h * head + offset(k), 128), WIDE)
                    acc_ref[rows, place_h] += pb_ref[0, rows, h * WIDE:(h + 1) * WIDE].astype(jnp.float32)

    @pl.when(mid)
    def _():
        p_copy(GROUPS - 2).wait_send()
        p_copy(GROUPS - 1).wait_send()

    x_far(0).wait_send()
    x_far(1).wait_send()
    for piece in [NEAR] + list(range(SUBS)):
        x_to_away(piece).wait_send()

        @pl.when(end)
        def _():
            x_to_mid(piece).wait_send()

        @pl.when(away)
        def _():
            x_to_home(piece, 0, near_half).wait_send()

            @pl.when(mid)
            def _():
                x_to_home(piece, 1, far_half).wait_send()

    for stage in range(SUBS):
        forward_x(stage, settle)

    @pl.loop(0, GROUPS)
    def _(k):
        w_cross(k).wait_send()
        for o in (g, pair):
            w_copy(o, k, False, 0).wait_send()

            @pl.when(mid)
            def _():
                w_copy(o, k, False, 1).wait_send()

        w_copy(pair, k, False, 2).wait_send()

        @pl.when(mid)
        def _():
            for yy in (0, 1):
                w_copy(2 * zout + yy, k, False, 0).wait_send()
                w_copy(2 * zout + yy, k, False, 2).wait_send()
            for i in range(sides):
                w_copy(sides * (1 - hi) + i, k, False, 2).wait_send()

        @pl.when(end)
        def _():
            for yy in (0, 1):
                w_copy(2 * zin + yy, k, False, 2).wait_send()


def gather_project(hidden, decode_hidden, norm_gain, qkv_weight):
    reps = 2
    count = lax.axis_size("grp")
    rows = reps * (hidden.shape[1] + 2 * decode_hidden.shape[3])
    own_rows = hidden.shape[1] + 2 * decode_hidden.shape[3]
    share = qkv_weight.shape[0]
    width = hidden.shape[2]
    cols = qkv_weight.shape[1] // 2
    hbm = pl.BlockSpec(memory_space=pl.ANY)
    vmem = pl.BlockSpec(memory_space=pltpu.VMEM)
    dma = pltpu.SemaphoreType.DMA
    return pl.pallas_call(
        gather_kernel,
        out_shape=(
            jax.ShapeDtypeStruct((rows, cols), jnp.float32),
            jax.ShapeDtypeStruct((count, GROUPS, 2, share, WIDE), jnp.bfloat16),
            jax.ShapeDtypeStruct((GROUPS, rows, 2 * WIDE), jnp.bfloat16),
        ),
        in_specs=[hbm, hbm, vmem, hbm],
        out_specs=(vmem, hbm, hbm),
        scratch_shapes=[
            pltpu.VMEM((3, rows, width // 2), jnp.bfloat16),
            pltpu.VMEM((own_rows, width), jnp.bfloat16),
            pltpu.VMEM((2, 2, share, WIDE), jnp.bfloat16),
            pltpu.VMEM((rows, 2 * WIDE), jnp.float32),
            pltpu.VMEM((2, rows, 2 * WIDE), jnp.bfloat16),
            dma((count, GROUPS)), dma((count, GROUPS)), dma((count, GROUPS)), dma((GROUPS,)),
            dma((count, GROUPS, 2)),
            dma((2, SUBS + 1)), dma((SUBS + 1,)), dma((SUBS + 1,)), dma((2,)),
            dma((3, SUBS + 2, 2)), dma((3, SUBS + 2, 2)),
            dma((GROUPS,)), dma((GROUPS,)), dma((4,)), dma((2, 2)),
        ],
        compiler_params=pltpu.CompilerParams(
            collective_id=0, has_side_effects=True, vmem_limit_bytes=58 << 20
        ),
        name="gather_project",
    )(hidden, decode_hidden, norm_gain.reshape(1, width), qkv_weight)[0]


def attend_kernel(
    heads, block, len_ref, proj_ref, bias_ref, cos_ref, sin_ref, prefill_ref, decode_ref,
    q_ref, k_ref, v_ref, m_ref, out_ref, ss, rs, ls,
):
    rows = proj_ref.shape[0]
    h = pl.program_id(0)
    g = lax.axis_index("grp")
    r = lax.axis_index("rep")
    y = g % 2
    pair = g + 1 - 2 * y
    far = (g + 4) % 8
    prompt = g - y + r
    span = prefill_ref.shape[1]
    drows = decode_ref.shape[3]
    prompt_rows = rows - 4 * drows
    width = QPK * HD
    barrier = pltpu.get_barrier_semaphore()

    @pl.when(h == 0)
    def _():
        def greet(grp, rep):
            pl.semaphore_signal(barrier, inc=1, device_id={"grp": grp, "rep": rep}, device_id_type=MESH)

        greet(g, 1 - r)
        for c in (0, 1):
            greet(pair, c)
            greet(far, c)
            greet(far + 1 - 2 * y, c)

    starts = (0, prompt_rows, prompt_rows + 2 * drows)
    sizes = (span, drows, drows)

    def target(i, c, line):
        at = pl.ds(pl.multiple_of((line * heads + i) * width, 128), width)
        return (prefill_ref.at[0, :, at], decode_ref.at[0, 0, 0, :, at], decode_ref.at[0, 0, 1, :, at])[c]

    def piece(i, c, rr):
        start = pl.multiple_of(starts[c] + rr * sizes[c], 16)
        return out_ref.at[i, pl.ds(start, sizes[c]), :]

    def send(i, c, rr):
        grp = (prompt + 4) % 8 if c == 2 else prompt
        return pltpu.make_async_remote_copy(
            piece(i, c, rr), target(i, c, y), ss.at[i, c, rr], rs.at[i, c, y],
            device_id={"grp": grp, "rep": rr}, device_id_type=MESH,
        )

    def keep(i, c):
        return pltpu.make_async_copy(piece(i, c, r), target(i, c, y), ls.at[i, c])

    def receive(i, c, line):
        return pltpu.make_async_remote_copy(
            piece(i, c, 0), target(i, c, line), ss.at[i, c, 0], rs.at[i, c, line],
            device_id={"rep": 1 - r}, device_id_type=MESH,
        )

    def each(i, c, act, keep_act):
        if c == 2:
            act(send(i, c, 0))
            act(send(i, c, 1))
            return

        @pl.when(r == y)
        def _():
            keep_act(keep(i, c))
            act(send(i, c, 1 - r))

        @pl.when(r != y)
        def _():
            act(send(i, c, 0))
            act(send(i, c, 1))

    cosine = cos_ref[...]
    sine = sin_ref[...]
    factor = HD ** (-0.5) * math.log2(math.e)
    valid = len_ref[0]

    def part(j):
        cols = slice(j * HD, (j + 1) * HD)
        return proj_ref[:, cols] + bias_ref[:, cols]

    def turned(x):
        return x * cosine + pltpu.roll(x, HD // 2, 1) * sine

    for j in range(QPK):
        q_ref[j] = (turned(part(j)) * factor).astype(jnp.bfloat16)
    k_ref[...] = turned(part(QPK)).astype(jnp.bfloat16)
    v_ref[...] = part(QPK + 1).astype(jnp.bfloat16)

    def run(start, size, keys):
        shape = (size, keys)
        row = lax.broadcasted_iota(jnp.int32, shape, 0) + start
        col = lax.broadcasted_iota(jnp.int32, shape, 1)
        if start < prompt_rows:
            allowed = (col <= row) & (col < valid)
        else:
            same = ((row - prompt_rows) // STEPS == (col - prompt_rows) // STEPS) & (col <= row)
            allowed = (col < jnp.minimum(valid, prompt_rows)) | ((col >= prompt_rows) & same)
        m_ref[:size, :keys] = jnp.where(allowed, 0.0, NEGATIVE)

        for j in range(QPK):
            s = lax.dot_general(
                q_ref[j, start:start + size, :], k_ref[:keys, :], (((1,), (1,)), ((), ())),
                preferred_element_type=jnp.float32,
            ) + m_ref[:size, :keys]
            top = jnp.max(s, axis=-1, keepdims=True)
            p = jnp.exp2(s - top)
            total = jnp.sum(p, axis=-1, keepdims=True)
            o = jnp.dot(p.astype(jnp.bfloat16), v_ref[:keys, :], preferred_element_type=jnp.float32)
            out_ref[h, start:start + size, j * HD:(j + 1) * HD] = (o / total).astype(jnp.bfloat16)

    run(prompt_rows, rows - prompt_rows, rows)
    run(0, block, block)

    @pl.when(h == 0)
    def _():
        pl.semaphore_wait(barrier, 7)

    def begin(copy):
        copy.start()

    each(h, 2, begin, begin)
    each(h, 1, begin, begin)
    for start in range(block, prompt_rows, block):
        run(start, block, start + block)
    each(h, 0, begin, begin)

    @pl.when(h == heads - 1)
    def _():
        def sent(copy):
            copy.wait_send()

        def kept(copy):
            copy.wait()

        for i in range(heads):
            for c in range(3):
                each(i, c, sent, kept)
                if c == 2:
                    receive(i, c, 0).wait_recv()
                    receive(i, c, 1).wait_recv()
                else:
                    receive(i, c, 1 - y).wait_recv()

                    @pl.when(r != y)
                    def _():
                        receive(i, c, y).wait_recv()


def attend(proj, bias_row, cosine, sine, valid, hidden, decode_hidden):
    rows, cols = proj.shape
    head = (QPK + 2) * HD
    heads = cols // head
    prompt_rows = 2 * hidden.shape[1]
    block = 256 if prompt_rows % 256 == 0 else prompt_rows
    size = max(block, rows - prompt_rows)
    width = 2 * heads * QPK * HD
    dma = pltpu.SemaphoreType.DMA
    hbm = pl.BlockSpec(memory_space=pl.ANY)
    return pl.pallas_call(
        functools.partial(attend_kernel, heads, block),
        out_shape=(
            jax.ShapeDtypeStruct(hidden.shape[:2] + (width,), jnp.bfloat16),
            jax.ShapeDtypeStruct(decode_hidden.shape[:4] + (width,), jnp.bfloat16),
        ),
        grid=(heads,),
        in_specs=[
            pl.BlockSpec(memory_space=pltpu.SMEM),
            pl.BlockSpec((rows, head), lambda h: (0, h)),
            pl.BlockSpec((1, head), lambda h: (0, h)),
            pl.BlockSpec((rows, HD), lambda h: (0, 0)),
            pl.BlockSpec((rows, HD), lambda h: (0, 0)),
        ],
        out_specs=(hbm, hbm),
        scratch_shapes=[
            pltpu.VMEM((QPK, rows, HD), jnp.bfloat16),
            pltpu.VMEM((rows, HD), jnp.bfloat16),
            pltpu.VMEM((rows, HD), jnp.bfloat16),
            pltpu.VMEM((size, rows), jnp.float32),
            pltpu.VMEM((heads, rows, QPK * HD), jnp.bfloat16),
            dma((heads, 3, 2)), dma((heads, 3, 2)), dma((heads, 3)),
        ],
        compiler_params=pltpu.CompilerParams(
            collective_id=1, has_side_effects=True, vmem_limit_bytes=48 << 20
        ),
        name="attend",
    )(valid.reshape(1), proj, bias_row, cosine, sine)


def on_device(hidden, decode_hidden, norm_gain, qkv_weight, qkv_bias, lengths):
    count = lax.axis_size("grp")
    reps = lax.axis_size("rep")
    head_block = (QPK + 2) * HD
    heads_here = qkv_bias.shape[0] // head_block
    if reps != 2 or count != 8 or lax.axis_size("tp") != 2 or heads_here != 4 or decode_hidden.shape[1] != 1:
        return plain_device(hidden, decode_hidden, norm_gain, qkv_weight, qkv_bias, lengths)
    g = lax.axis_index("grp")
    r = lax.axis_index("rep")
    y = g % 2
    prompt = g - y + r
    cols = qkv_weight.shape[1] // 2
    drows = decode_hidden.shape[3]
    prompt_rows = reps * hidden.shape[1]
    proj = gather_project(hidden, decode_hidden, norm_gain, qkv_weight)

    index_table = jnp.arange(count, dtype=jnp.int32)
    own_len = jnp.sum(jnp.where(index_table == prompt, lengths, 0))
    steps = jnp.arange(2 * reps * drows, dtype=jnp.int32) % STEPS
    positions = jnp.concatenate([jnp.arange(prompt_rows, dtype=jnp.int32), own_len + steps])
    cosine, sine = rope_tables(positions, HD)
    cosine = jnp.concatenate([cosine, cosine], axis=-1)
    sine = jnp.concatenate([-sine, sine], axis=-1)
    bias_row = lax.dynamic_slice_in_dim(qkv_bias, y * cols, cols, 0).astype(jnp.float32).reshape(1, cols)
    return attend(proj, bias_row, cosine, sine, own_len, hidden, decode_hidden)


def solution(mesh):
    return jax.shard_map(
        on_device,
        mesh=mesh,
        in_specs=(
            P("grp", "rep", None),
            P("grp", "rep", None, None, None),
            P(),
            P("grp", "tp"),
            P("tp"),
            P(),
        ),
        out_specs=(P("grp", "rep", "tp"), P("grp", "rep", None, None, "tp")),
        check_vma=False,
    )
```

```python
import jax
import jax.numpy as jnp
from jax import lax
from jax.experimental import pallas as pl
from jax.experimental.pallas import tpu as pltpu
from jax.sharding import PartitionSpec as P
import functools
import math

HD = 128
QPK = 8
STEPS = 4


THETA = 1000000.0
EPSILON = 1e-06
NEGATIVE = -1e30


def shifted(block, axis, distance):
    devices = range(lax.axis_size(axis))
    route = [((i - distance) % len(devices), i) for i in devices]
    return lax.ppermute(block, axis, route)


def normalize(row_block, gain_row):
    widened = row_block.astype(jnp.float32)
    factor = lax.rsqrt(jnp.mean(widened * widened, axis=-1, keepdims=True) + EPSILON)
    return (widened * factor * gain_row.astype(jnp.float32)).astype(jnp.bfloat16)


def rope_tables(positions, head_size):
    half_size = head_size // 2
    frequency = THETA ** (-(jnp.arange(half_size, dtype=jnp.float32) * 2.0 / head_size))
    angle = positions.astype(jnp.float32)[:, None] * frequency[None, :]
    return (jnp.cos(angle), jnp.sin(angle))


def rotate(vector, cosine, sine_part):
    half_size = vector.shape[-1] // 2
    first_half = vector[..., :half_size]
    second = vector[..., half_size:]
    return jnp.concatenate(
        [first_half * cosine - second * sine_part, second * cosine + first_half * sine_part],
        axis=-1,
    )


def masked_max(scores, allowed):
    return jnp.max(jnp.where(allowed, scores, NEGATIVE), axis=-1, keepdims=True)


def combine_values(weight_matrix, value_matrix):
    return jnp.einsum(
        "aprk,kaz->rapz",
        weight_matrix.astype(jnp.bfloat16),
        value_matrix,
        preferred_element_type=jnp.float32,
    )


def pair_scores(query_matrix, key_matrix_rows, score_scale):
    return (
        jnp.einsum(
            "wjro,ujo->jrwu", query_matrix, key_matrix_rows, preferred_element_type=jnp.float32
        )
        * score_scale
    )


def decode_pair(
    query_matrix,
    own_keys,
    own_values,
    prompt_keys,
    prompt_values,
    valid_len,
    local_allowed,
    score_scale,
):
    key_slot_index = jnp.arange(prompt_keys.shape[0], dtype=jnp.int32)
    prompt_allowed = (key_slot_index < valid_len)[None, None, None, :]
    far_scores = pair_scores(query_matrix, prompt_keys, score_scale)
    near_scores = pair_scores(query_matrix, own_keys, score_scale)
    highest = jnp.maximum(
        masked_max(far_scores, prompt_allowed), masked_max(near_scores, local_allowed)
    )
    far_exp = jnp.where(prompt_allowed, jnp.exp(far_scores - highest), 0.0)
    near_exp = jnp.where(local_allowed, jnp.exp(near_scores - highest), 0.0)
    running = jnp.sum(far_exp, axis=-1, keepdims=True) + jnp.sum(near_exp, axis=-1, keepdims=True)
    return combine_values(far_exp / running, prompt_values) + combine_values(
        near_exp / running, own_values
    )


def plain_device(hidden, decode_hidden, norm_gain, qkv_weight, qkv_bias, lengths):
    prompt_count = lax.axis_size("grp")
    rep_count = lax.axis_size("rep")
    half_cycle = prompt_count // 2
    grp_here = lax.axis_index("grp")
    rep_here = lax.axis_index("rep")
    span_rows = hidden.shape[1]
    model_width = hidden.shape[2]
    head_block = (QPK + 2) * HD
    heads_here = qkv_bias.shape[0] // head_block
    decode_rows = decode_hidden.shape[3]
    score_scale = HD ** (-0.5)
    prefill_normed = normalize(hidden[0], norm_gain)
    decode_normed = normalize(decode_hidden.reshape(2 * decode_rows, model_width), norm_gain)
    normed = jnp.concatenate([prefill_normed, decode_normed], axis=0)
    share_cols = qkv_weight.shape[1] // rep_count
    own_cols = lax.dynamic_slice_in_dim(qkv_weight, rep_here * share_cols, share_cols, 1)
    columns = lax.all_gather(own_cols, "grp", axis=0, tiled=True)
    complete = lax.all_gather(columns, "rep", axis=1, tiled=True)
    projected = jnp.dot(normed, complete, preferred_element_type=jnp.float32)
    projected = (projected + qkv_bias.astype(jnp.float32)).reshape(
        normed.shape[0], heads_here, QPK + 2, HD
    )
    index_table = jnp.arange(prompt_count, dtype=jnp.int32)

    def length_of(prompt):
        return jnp.sum(jnp.where(index_table == prompt, lengths, 0))

    own_len = length_of(grp_here)
    far_len = length_of((grp_here + half_cycle) % prompt_count)
    row_position = rep_here * span_rows + jnp.arange(span_rows, dtype=jnp.int32)
    local_ids = jnp.arange(decode_rows, dtype=jnp.int32)
    step_ids = local_ids % STEPS
    sample_ids = local_ids // STEPS
    positions = jnp.concatenate([row_position, own_len + step_ids, far_len + step_ids])
    cosine, sine_part = rope_tables(positions, HD)
    query_matrix = rotate(
        projected[:, :, :QPK], cosine[:, None, None, :], sine_part[:, None, None, :]
    ).astype(jnp.bfloat16)
    key_matrix_rows = rotate(
        projected[:, :, QPK], cosine[:, None, :], sine_part[:, None, :]
    ).astype(jnp.bfloat16)
    value_matrix = projected[:, :, QPK + 1].astype(jnp.bfloat16)
    cache_keys, cache_values = (
        lax.all_gather(key_matrix_rows[:span_rows], "rep", axis=0, tiled=True),
        lax.all_gather(value_matrix[:span_rows], "rep", axis=0, tiled=True),
    )
    key_pos = jnp.arange(cache_keys.shape[0], dtype=jnp.int32)
    allowed = ((key_pos[None, :] <= row_position[:, None]) & (key_pos[None, :] < own_len))[
        None, None
    ]
    scores = pair_scores(query_matrix[:span_rows], cache_keys, score_scale)
    highest = masked_max(scores, allowed)
    exponent = jnp.where(allowed, jnp.exp(scores - highest), 0.0)
    weight_matrix = exponent / jnp.sum(exponent, axis=-1, keepdims=True)
    attended = combine_values(weight_matrix, cache_values)
    prefill_out = attended.astype(jnp.bfloat16).reshape(1, span_rows, heads_here * QPK * HD)
    decode_queries = query_matrix[span_rows:].reshape(2, decode_rows, heads_here, QPK, HD)
    decode_keys = key_matrix_rows[span_rows:].reshape(2, decode_rows, heads_here, HD)
    decode_values = value_matrix[span_rows:].reshape(2, decode_rows, heads_here, HD)
    local_allowed = (
        (sample_ids[None, :] == sample_ids[:, None]) & (step_ids[None, :] <= step_ids[:, None])
    )[None, None]
    near_out = decode_pair(
        decode_queries[0],
        decode_keys[0],
        decode_values[0],
        cache_keys,
        cache_values,
        own_len,
        local_allowed,
        score_scale,
    )
    far_keys, far_values = shifted((cache_keys, cache_values), "grp", half_cycle)
    far_out = decode_pair(
        decode_queries[1],
        decode_keys[1],
        decode_values[1],
        far_keys,
        far_values,
        far_len,
        local_allowed,
        score_scale,
    )
    decode_out = (
        jnp.stack([near_out, far_out])
        .astype(jnp.bfloat16)
        .reshape(1, 1, 2, decode_rows, heads_here * QPK * HD)
    )
    return (prefill_out, decode_out)


MESH = pl.DeviceIdType.MESH
SUBS = 2
GROUPS = QPK // 2 + 1
WIDE = 2 * HD


def fused_kernel(
    len_ref, hidden_ref, decode_ref, gain_ref, w_ref, bias_ref, cos_ref, sin_ref,
    prefill_ref, out_decode_ref, wbuf_ref, land_ref,
    acc_ref, xh_ref, nv_ref, wt_ref, accp_ref, pb_ref, q_ref, k_ref, v_ref, m_ref, out_ref,
    wi_s, wo_s, wb_s, wy_s, w_r,
    xa_s, xb_s, xc_s, xd_s, xf_s, x_r,
    p_s, p_r, l_s, t_s, o_s, o_r, o_l,
):
    g = lax.axis_index("grp")
    r = lax.axis_index("rep")
    x = lax.axis_index("tp")
    z = g // 2
    y = g % 2
    hi = z // 2
    zin = z + 1 - 2 * hi
    zout = z - 1 + 2 * hi
    mid = (z == 1) | (z == 2)
    end = (z == 0) | (z == 3)
    mid_count = (z // 2 + z % 2) % 2
    home = r == y
    away = r != y
    span = hidden_ref.shape[1]
    drows = decode_ref.shape[3]
    share = w_ref.shape[0]
    cols = acc_ref.shape[1]
    head = cols // 2
    half = xh_ref.shape[2]
    quarter = half // 2
    rows_all = acc_ref.shape[0]
    sub = span // SUBS
    sides = 4

    barrier = pltpu.get_barrier_semaphore()

    def greet(grp, rep, tp):
        pl.semaphore_signal(
            barrier, inc=1, device_id={"grp": grp, "rep": rep, "tp": tp}, device_id_type=MESH
        )

    pair = 2 * z + 1 - y
    greet(g, 1 - r, x)
    greet(g, r, 1 - x)
    for c in (0, 1):
        greet(pair, c, x)
        greet((g + 4) % 8, c, x)
        greet((g + 4) % 8 + 1 - 2 * y, c, x)
        greet(2 * zin + y, c, x)

    @pl.when(mid)
    def _():
        for c in (0, 1):
            greet(2 * zout + y, c, x)
        pl.semaphore_wait(barrier, 12)

    @pl.when(end)
    def _():
        pl.semaphore_wait(barrier, 10)

    def offset(k):
        return ((k + GROUPS - 1) % GROUPS) * WIDE

    def own_cols(line, h, k):
        return w_ref.at[:, pl.ds(pl.multiple_of(line * cols + h * head + offset(k), 128), WIDE)]

    def remote(src, dst, ssem, rsem, **device):
        return pltpu.make_async_remote_copy(
            src, dst, ssem, rsem, device_id=device, device_id_type=MESH
        )

    def w_copy(o, k, own, kind):
        src = own_cols(y, r, k) if own else wbuf_ref.at[o, k, r]
        dst = wbuf_ref.at[o, k, r]
        if kind == 0:
            return remote(src, dst, wi_s.at[o, k], w_r.at[o, k, r], grp=2 * zin + y)
        if kind == 1:
            return remote(src, dst, wo_s.at[o, k], w_r.at[o, k, r], grp=2 * zout + y)
        return remote(src, dst, wb_s.at[o, k], w_r.at[o, k, r], rep=1 - r)

    def w_cross(k):
        return remote(own_cols(1 - y, r, k), wbuf_ref.at[g, k, r], wy_s.at[k], w_r.at[g, k, r], grp=pair)

    def w_arrived(o, k, h):
        remote(wbuf_ref.at[o, k, h], wbuf_ref.at[o, k, h], wb_s.at[o, k], w_r.at[o, k, h], rep=1 - r).wait_recv()

    def own_sends(k):
        w_cross(k).start()

        @pl.when(mid)
        def _():
            w_copy(g, k, True, 1).start()

        @pl.when(end)
        def _():
            w_copy(g, k, True, 0).start()

    own_sends(0)
    own_sends(1)

    @pl.when(mid)
    def _():
        for k in range(GROUPS):
            w_copy(g, k, True, 0).start()

    raw = [
        pltpu.make_async_copy(decode_ref.at[0, 0, 1], nv_ref.at[pl.ds(span + drows, drows), :], l_s.at[0]),
        pltpu.make_async_copy(decode_ref.at[0, 0, 0], nv_ref.at[pl.ds(span, drows), :], l_s.at[1]),
        pltpu.make_async_copy(hidden_ref.at[0], nv_ref.at[pl.ds(0, span), :], l_s.at[2]),
    ]
    for copy in raw:
        copy.start()

    @pl.loop(0, rows_all // 16)
    def _(i):
        acc_ref[pl.ds(pl.multiple_of(i * 16, 16), 16), :] = jnp.zeros((16, cols), jnp.float32)

    gain = gain_ref[...].astype(jnp.float32)

    def norm(first, n):
        @pl.loop(0, n // 16)
        def _(i):
            rows = pl.ds(pl.multiple_of(first + i * 16, 16), 16)
            wide = nv_ref[rows, :].astype(jnp.float32)
            factor = lax.rsqrt(jnp.mean(wide * wide, axis=-1, keepdims=True) + EPSILON)
            nv_ref[rows, :] = (wide * factor * gain).astype(jnp.bfloat16)

    def place(piece, rr):
        if piece < SUBS:
            return pl.multiple_of(rr * span + piece * sub, 16), sub
        return pl.multiple_of(2 * span + ((piece - SUBS) * 2 + rr) * drows, 16), drows

    def source(piece, k_half, part=None):
        start, n = (piece * sub, sub) if piece < SUBS else (span + (piece - SUBS) * drows, drows)
        if part is None:
            return nv_ref.at[pl.ds(start, n), pl.ds(pl.multiple_of(k_half * half, 128), half)]
        return nv_ref.at[pl.ds(start, n), pl.ds(pl.multiple_of(k_half * half + part * quarter, 128), quarter)]

    def spot(slot, piece, rr):
        start, n = place(piece, rr)
        return xh_ref.at[slot, pl.ds(start, n), :]

    def spot_part(part, piece, rr):
        start, n = place(piece, rr)
        return xh_ref.at[2, pl.ds(start, n), pl.ds(pl.multiple_of(part * quarter, 128), quarter)]

    near_half = hi
    far_half = 1 - hi

    def x_to_home(piece, slot, k_half):
        return remote(source(piece, k_half), spot(slot, piece, r), xa_s.at[slot, piece], x_r.at[slot, piece, r], rep=y)

    def x_local(piece, slot, k_half):
        return pltpu.make_async_copy(source(piece, k_half), spot(slot, piece, r), x_r.at[slot, piece, r])

    def x_to_away(piece):
        slot = jnp.where(mid, x, 0)
        k_half = hi + slot * (1 - 2 * hi)
        return remote(source(piece, k_half), spot(slot, piece, r), xb_s.at[piece], x_r.at[slot, piece, r], grp=pair, rep=y)

    def x_to_mid(piece):
        return remote(
            source(piece, far_half, x), spot_part(x, piece, r), xc_s.at[piece], x_r.at[2 + x, piece, r],
            grp=2 * zin + y, rep=y,
        )

    FAR = SUBS + 1
    NEAR = SUBS
    far_g = (g + 4) % 8

    def far_from_end():
        k_half = far_half + x * (1 - 2 * far_half)
        return remote(source(FAR, k_half), spot(x, FAR, r), xd_s.at[0], x_r.at[x, FAR, r], grp=far_g, rep=y)

    def far_to_end():
        return remote(source(FAR, far_half), spot(0, FAR, r), xd_s.at[0], x_r.at[0, FAR, r], grp=far_g, rep=y)

    def far_to_mid():
        return remote(
            source(FAR, near_half, x), spot_part(x, FAR, r), xd_s.at[1], x_r.at[2 + x, FAR, r],
            grp=2 * zin + y, rep=y,
        )

    def send_piece(piece):
        x_to_away(piece).start()

        @pl.when(end)
        def _():
            x_to_mid(piece).start()

        @pl.when(home)
        def _():
            x_local(piece, 0, near_half).start()

            @pl.when(mid)
            def _():
                x_local(piece, 1, far_half).start()

        @pl.when(away)
        def _():
            x_to_home(piece, 0, near_half).start()

            @pl.when(mid)
            def _():
                x_to_home(piece, 1, far_half).start()

    raw[0].wait()
    norm(span + drows, drows)

    @pl.when(mid)
    def _():
        far_to_end().start()
        far_to_mid().start()

    @pl.when(end)
    def _():
        far_from_end().start()

    raw[1].wait()
    norm(span, drows)
    send_piece(NEAR)
    raw[2].wait()
    for s in range(SUBS):
        norm(s * sub, sub)
        send_piece(s)

    across = {"grp": pair}
    beside = {"tp": 1 - x}
    MAIN = [NEAR] + list(range(SUBS))

    def x_forward(slot, piece, rr, way, device):
        where = spot(slot, piece, rr)
        return remote(where, where, xf_s.at[way, slot, piece, rr], x_r.at[slot, piece, rr], **device)

    def part_forward(part, piece, rr, way, device):
        where = spot_part(part, piece, rr)
        return remote(where, where, xf_s.at[way, 2 + part, piece, rr], x_r.at[2 + part, piece, rr], **device)

    def arrived(make, slot, piece, rr):
        make(slot, piece, rr, 0, {"rep": 1 - r}).wait_recv()

    def relay(make, slot, piece, ways):
        for rr in (0, 1):
            arrived(make, slot, piece, rr)
            for way in ways:
                make(slot, piece, rr, way, (across, beside)[way]).start()

    def settle(make, slot, piece, ways):
        for rr in (0, 1):
            for way in ways:
                make(slot, piece, rr, way, (across, beside)[way]).wait_send()

    def forward_x(stage, act):
        pieces = [NEAR, 0] if stage == 0 else [stage]
        fars = [FAR] if stage == 0 else []

        @pl.when(home & end)
        def _():
            for piece in fars:
                act(x_forward, 0, piece, (0,))

        @pl.when(home & mid)
        def _():
            for piece in fars:
                act(x_forward, x, piece, (0, 1))
            for piece in fars + pieces:
                act(part_forward, x, piece, (0, 1))

        @pl.when(away & mid)
        def _():
            for piece in pieces:
                act(x_forward, x, piece, (1,))

    def forward_late(act):
        @pl.when(away & mid)
        def _():
            act(x_forward, x, FAR, (1,))

    def forward_part(act):
        @pl.when(away & mid)
        def _():
            for piece in [FAR] + MAIN:
                act(part_forward, x, piece, (1,))

    def wait_x():
        @pl.when(home)
        def _():
            def both(slot, k_half):
                for piece in MAIN:
                    x_local(piece, slot, k_half).wait()
                    arrived(x_forward, slot, piece, 1 - r)

            both(0, near_half)

            @pl.when(mid)
            def _():
                both(1, far_half)
                for rr in (0, 1):
                    arrived(x_forward, 1 - x, FAR, rr)

        @pl.when(away)
        def _():
            slot = jnp.where(mid, 1 - x, 0)
            for piece in MAIN + [FAR]:
                for rr in (0, 1):
                    arrived(x_forward, slot, piece, rr)

    def wait_part():
        @pl.when(mid)
        def _():
            for piece in MAIN + [FAR]:
                for rr in (0, 1):
                    arrived(part_forward, 1 - x, piece, rr)

    def pass_w(k):
        w_arrived(pair, k, r)
        w_copy(pair, k, False, 0).start()

        @pl.when(mid)
        def _():
            w_copy(pair, k, False, 1).start()

        w_copy(pair, k, False, 2).start()

        @pl.when(mid)
        def _():
            for yy in (y, 1 - y):
                o = 2 * zout + yy
                w_arrived(o, k, r)
                w_copy(o, k, False, 0).start()
                w_copy(o, k, False, 2).start()

    def take_w(k):
        def over(layer):
            for yy in (y, 1 - y):
                o = 2 * layer + yy
                w_arrived(o, k, r)
                w_copy(o, k, False, 2).start()

        over(zin)

        @pl.when(mid)
        def _():
            over(zin + 1 - 2 * hi)
            for yy in (0, 1):
                w_arrived(2 * zout + yy, k, 1 - r)
            for i in range(sides):
                w_arrived(sides * (1 - hi) + i, k, 1 - r)

        @pl.when(end)
        def _():
            for yy in (0, 1):
                w_arrived(2 * zin + yy, k, 1 - r)

        w_arrived(pair, k, 1 - r)

    def p_copy(k):
        return remote(pb_ref.at[k % 2], land_ref.at[k], p_s.at[k], p_r.at[k], grp=2 * zout + y)

    def fetch(k, o, slot):
        for h in (0, 1):
            dst = wt_ref.at[slot, h]

            @pl.when(o == g)
            def _():
                pltpu.make_async_copy(own_cols(y, h, k), dst, t_s.at[slot, h]).start()

            @pl.when(o != g)
            def _():
                pltpu.make_async_copy(wbuf_ref.at[o, k, h], dst, t_s.at[slot, h]).start()

    def tile_done(slot):
        for h in (0, 1):
            pltpu.make_async_copy(wbuf_ref.at[0, 0, h], wt_ref.at[slot, h], t_s.at[slot, h]).wait()

    def slice_at(j):
        return (sides * (1 - hi) + j) % (2 * sides)

    def columns_of(o):
        return pl.ds(pl.multiple_of((o % sides) * share, 128), share)

    def compute(k):
        @pl.when(mid)
        def _():
            fetch(k, slice_at(0), 0)

        @pl.when(end)
        def _():
            fetch(k, slice_at(sides), 0)

        @pl.loop(0, 2 * sides)
        def _(j):
            o = slice_at(j)
            slot = j % 2

            @pl.when((j >= sides) | mid)
            def _():
                @pl.when(j + 1 < 2 * sides)
                def _():
                    fetch(k, slice_at(j + 1), (j + 1) % 2)

                tile_done(slot)
                for h in (0, 1):
                    place_h = pl.ds(pl.multiple_of(h * head + offset(k), 128), WIDE)
                    acc_ref[:, place_h] += jnp.dot(
                        xh_ref[1 - j // sides, :, columns_of(o)], wt_ref[slot, h], preferred_element_type=jnp.float32
                    )

    def partial(k):
        @pl.loop(0, rows_all // 16)
        def _(i):
            accp_ref[pl.ds(pl.multiple_of(i * 16, 16), 16), :] = jnp.zeros((16, 2 * WIDE), jnp.float32)

        fetch(k, slice_at(0), 0)

        @pl.loop(0, sides)
        def _(j):
            o = slice_at(j)
            slot = j % 2

            @pl.when(j + 1 < sides)
            def _():
                fetch(k, slice_at(j + 1), (j + 1) % 2)

            tile_done(slot)
            for h in (0, 1):
                accp_ref[:, h * WIDE:(h + 1) * WIDE] += jnp.dot(
                    xh_ref[2, :, columns_of(o)], wt_ref[slot, h], preferred_element_type=jnp.float32
                )

        @pl.when(k >= 2)
        def _():
            p_copy(k - 2).wait_send()

        @pl.loop(0, rows_all // 16)
        def _(i):
            rows = pl.ds(pl.multiple_of(i * 16, 16), 16)
            pb_ref[k % 2, rows, :] = accp_ref[rows, :].astype(jnp.bfloat16)

        p_copy(k).start()

    def add_partial(k):
        remote(pb_ref.at[0], land_ref.at[k], p_s.at[k], p_r.at[k], grp=2 * zin + y).wait_recv()
        take = pltpu.make_async_copy(land_ref.at[k], pb_ref.at[0], l_s.at[3])
        take.start()
        take.wait()

        @pl.loop(0, rows_all // 16)
        def _(i):
            rows = pl.ds(pl.multiple_of(i * 16, 16), 16)
            for h in (0, 1):
                place_h = pl.ds(pl.multiple_of(h * head + offset(k), 128), WIDE)
                acc_ref[rows, place_h] += pb_ref[0, rows, h * WIDE:(h + 1) * WIDE].astype(jnp.float32)

    prompt = g - y + r
    prompt_rows = 2 * span
    valid = len_ref[0]
    block = 256 if prompt_rows % 256 == 0 else prompt_rows
    blocks = [(prompt_rows, rows_all - prompt_rows, rows_all)]
    blocks += [(start, block, start + block) for start in range(0, prompt_rows, block)]
    starts = (0, prompt_rows, prompt_rows + 2 * drows)
    sizes = (span, drows, drows)
    width = QPK * HD

    def mask_place(index):
        top = 0
        for start, size, keys in blocks[:index]:
            top += size
        return slice(top, top + blocks[index][1]), slice(0, blocks[index][2])

    def make_masks():
        for index, (start, size, keys) in enumerate(blocks):
            shape = (size, keys)
            row = lax.broadcasted_iota(jnp.int32, shape, 0) + start
            col = lax.broadcasted_iota(jnp.int32, shape, 1)
            if start < prompt_rows:
                allowed = (col <= row) & (col < valid)
            else:
                same = ((row - prompt_rows) // STEPS == (col - prompt_rows) // STEPS) & (col <= row)
                allowed = (col < jnp.minimum(valid, prompt_rows)) | ((col >= prompt_rows) & same)
            m_ref[mask_place(index)] = jnp.where(allowed, 0.0, NEGATIVE)

    def target(f, h, c, line):
        at = pl.ds(pl.multiple_of((line * 2 + h) * width + offset(f), 128), WIDE)
        return (prefill_ref.at[0, :, at], out_decode_ref.at[0, 0, 0, :, at], out_decode_ref.at[0, 0, 1, :, at])[c]

    def out_piece(f, h, c, rr):
        start = pl.multiple_of(starts[c] + rr * sizes[c], 16)
        return out_ref.at[f - 1, h, pl.ds(start, sizes[c]), :]

    def out_send(f, h, c, rr):
        grp = (prompt + 4) % 8 if c == 2 else prompt
        return remote(
            out_piece(f, h, c, rr), target(f, h, c, y), o_s.at[f - 1, h, c, rr], o_r.at[f - 1, h, c, y],
            grp=grp, rep=rr,
        )

    def out_keep(f, h, c):
        return pltpu.make_async_copy(out_piece(f, h, c, r), target(f, h, c, y), o_l.at[f - 1, h, c])

    def out_receive(f, h, c, line):
        remote(
            out_piece(f, h, c, 0), target(f, h, c, line), o_s.at[f - 1, h, c, 0], o_r.at[f - 1, h, c, line], rep=1 - r
        ).wait_recv()

    def each_out(f, h, c, act, keep_act):
        if c == 2:
            act(out_send(f, h, c, 0))
            act(out_send(f, h, c, 1))
            return

        @pl.when(home)
        def _():
            keep_act(out_keep(f, h, c))
            act(out_send(f, h, c, 1 - r))

        @pl.when(away)
        def _():
            act(out_send(f, h, c, 0))
            act(out_send(f, h, c, 1))

    def begin(copy):
        copy.start()

    def sent(copy):
        copy.wait_send()

    def kept(copy):
        copy.wait()

    def finish(f):
        factor = HD ** (-0.5) * math.log2(math.e)

        def part(h, first):
            at = pl.ds(pl.multiple_of(h * head + first, 128), HD)
            return acc_ref[:, at] + bias_ref[:, at]

        def turned(v):
            return v * cos_ref[...] + pltpu.roll(v, HD // 2, 1) * sin_ref[...]

        @pl.when(f == 0)
        def _():
            for h in (0, 1):
                k_ref[h] = turned(part(h, QPK * HD)).astype(jnp.bfloat16)
                v_ref[h] = part(h, (QPK + 1) * HD).astype(jnp.bfloat16)

        @pl.when(f > 0)
        def _():
            @pl.loop(0, 2)
            def _(h):
                for j in (0, 1):
                    q_ref[j] = (turned(part(h, offset(f) + j * HD)) * factor).astype(jnp.bfloat16)
                for index, (start, size, keys) in enumerate(blocks):
                    for j in (0, 1):
                        s = lax.dot_general(
                            q_ref[j, start:start + size, :], k_ref[h, :keys, :], (((1,), (1,)), ((), ())),
                            preferred_element_type=jnp.float32,
                        ) + m_ref[mask_place(index)]
                        top = jnp.max(s, axis=-1, keepdims=True)
                        p = jnp.exp2(s - top)
                        total = jnp.sum(p, axis=-1, keepdims=True)
                        o = jnp.dot(p.astype(jnp.bfloat16), v_ref[h, :keys, :], preferred_element_type=jnp.float32)
                        out_ref[f - 1, h, start:start + size, j * HD:(j + 1) * HD] = (o / total).astype(jnp.bfloat16)
                    if index == 0:
                        each_out(f, h, 2, begin, begin)
                        each_out(f, h, 1, begin, begin)
                each_out(f, h, 0, begin, begin)

    @pl.loop(0, GROUPS + 4)
    def _(t):
        @pl.when(t + 2 < GROUPS)
        def _():
            own_sends(t + 2)

        @pl.when(t < GROUPS)
        def _():
            pass_w(t)

        for stage in range(SUBS):
            @pl.when(t == stage)
            def _():
                forward_x(stage, relay)

        @pl.when(t == 2)
        def _():
            forward_late(relay)
            make_masks()
            wait_x()

        @pl.when((t >= 2) & (t < GROUPS + 2))
        def _():
            take_w(t - 2)

            @pl.when(mid & (t >= 4))
            def _():
                partial(t - 2)

            compute(t - 2)

        @pl.when(t == 2)
        def _():
            forward_part(relay)

        @pl.when(mid & (t == 3))
        def _():
            wait_part()

            @pl.loop(0, 2)
            def _(k):
                partial(k)

        f = t - 4 + 2 * mid_count

        @pl.when((f >= 0) & (f < GROUPS))
        def _():
            @pl.when(end)
            def _():
                add_partial(f)

            finish(f)

    @pl.loop(1, GROUPS)
    def _(f):
        for h in (0, 1):
            for c in range(3):
                each_out(f, h, c, sent, kept)
                if c == 2:
                    out_receive(f, h, c, 0)
                    out_receive(f, h, c, 1)
                else:
                    out_receive(f, h, c, 1 - y)

                    @pl.when(away)
                    def _():
                        out_receive(f, h, c, y)

    @pl.when(mid)
    def _():
        p_copy(GROUPS - 2).wait_send()
        p_copy(GROUPS - 1).wait_send()

    @pl.when(mid)
    def _():
        far_to_end().wait_send()
        far_to_mid().wait_send()

    @pl.when(end)
    def _():
        far_from_end().wait_send()

    for piece in [NEAR] + list(range(SUBS)):
        x_to_away(piece).wait_send()

        @pl.when(end)
        def _():
            x_to_mid(piece).wait_send()

        @pl.when(away)
        def _():
            x_to_home(piece, 0, near_half).wait_send()

            @pl.when(mid)
            def _():
                x_to_home(piece, 1, far_half).wait_send()

    for stage in range(SUBS):
        forward_x(stage, settle)
    forward_late(settle)
    forward_part(settle)

    @pl.loop(0, GROUPS)
    def _(k):
        w_cross(k).wait_send()
        for o in (g, pair):
            w_copy(o, k, False, 0).wait_send()

            @pl.when(mid)
            def _():
                w_copy(o, k, False, 1).wait_send()

        w_copy(pair, k, False, 2).wait_send()

        @pl.when(mid)
        def _():
            for yy in (0, 1):
                w_copy(2 * zout + yy, k, False, 0).wait_send()
                w_copy(2 * zout + yy, k, False, 2).wait_send()
            for i in range(sides):
                w_copy(sides * (1 - hi) + i, k, False, 2).wait_send()

        @pl.when(end)
        def _():
            for yy in (0, 1):
                w_copy(2 * zin + yy, k, False, 2).wait_send()


def fused(hidden, decode_hidden, norm_gain, qkv_weight, bias_row, cosine, sine, valid):
    count = lax.axis_size("grp")
    own_rows = hidden.shape[1] + 2 * decode_hidden.shape[3]
    rows = 2 * own_rows
    share = qkv_weight.shape[0]
    width = hidden.shape[2]
    cols = qkv_weight.shape[1] // 2
    out_width = 4 * QPK * HD
    pieces = SUBS + 2
    hbm = pl.BlockSpec(memory_space=pl.ANY)
    vmem = pl.BlockSpec(memory_space=pltpu.VMEM)
    smem = pl.BlockSpec(memory_space=pltpu.SMEM)
    dma = pltpu.SemaphoreType.DMA
    outs = GROUPS - 1
    return pl.pallas_call(
        fused_kernel,
        out_shape=(
            jax.ShapeDtypeStruct(hidden.shape[:2] + (out_width,), jnp.bfloat16),
            jax.ShapeDtypeStruct(decode_hidden.shape[:4] + (out_width,), jnp.bfloat16),
            jax.ShapeDtypeStruct((count, GROUPS, 2, share, WIDE), jnp.bfloat16),
            jax.ShapeDtypeStruct((GROUPS, rows, 2 * WIDE), jnp.bfloat16),
        ),
        in_specs=[smem, hbm, hbm, vmem, hbm, vmem, vmem, vmem],
        out_specs=(hbm, hbm, hbm, hbm),
        scratch_shapes=[
            pltpu.VMEM((rows, cols), jnp.float32),
            pltpu.VMEM((3, rows, width // 2), jnp.bfloat16),
            pltpu.VMEM((own_rows, width), jnp.bfloat16),
            pltpu.VMEM((2, 2, share, WIDE), jnp.bfloat16),
            pltpu.VMEM((rows, 2 * WIDE), jnp.float32),
            pltpu.VMEM((2, rows, 2 * WIDE), jnp.bfloat16),
            pltpu.VMEM((2, rows, HD), jnp.bfloat16),
            pltpu.VMEM((2, rows, HD), jnp.bfloat16),
            pltpu.VMEM((2, rows, HD), jnp.bfloat16),
            pltpu.VMEM((rows, rows), jnp.float32),
            pltpu.VMEM((outs, 2, rows, WIDE), jnp.bfloat16),
            dma((count, GROUPS)), dma((count, GROUPS)), dma((count, GROUPS)), dma((GROUPS,)),
            dma((count, GROUPS, 2)),
            dma((2, SUBS + 1)), dma((SUBS + 1,)), dma((SUBS + 1,)), dma((2,)),
            dma((2, 4, pieces, 2)), dma((4, pieces, 2)),
            dma((GROUPS,)), dma((GROUPS,)), dma((4,)), dma((2, 2)),
            dma((outs, 2, 3, 2)), dma((outs, 2, 3, 2)), dma((outs, 2, 3)),
        ],
        compiler_params=pltpu.CompilerParams(
            collective_id=0, has_side_effects=True, vmem_limit_bytes=60 << 20
        ),
        name="fused",
    )(valid.reshape(1), hidden, decode_hidden, norm_gain.reshape(1, width), qkv_weight, bias_row, cosine, sine)[:2]


def on_device(hidden, decode_hidden, norm_gain, qkv_weight, qkv_bias, lengths):
    count = lax.axis_size("grp")
    reps = lax.axis_size("rep")
    head_block = (QPK + 2) * HD
    heads_here = qkv_bias.shape[0] // head_block
    if reps != 2 or count != 8 or lax.axis_size("tp") != 2 or heads_here != 4 or decode_hidden.shape[1] != 1:
        return plain_device(hidden, decode_hidden, norm_gain, qkv_weight, qkv_bias, lengths)
    g = lax.axis_index("grp")
    r = lax.axis_index("rep")
    y = g % 2
    prompt = g - y + r
    cols = qkv_weight.shape[1] // 2
    drows = decode_hidden.shape[3]
    prompt_rows = reps * hidden.shape[1]
    index_table = jnp.arange(count, dtype=jnp.int32)
    own_len = jnp.sum(jnp.where(index_table == prompt, lengths, 0))
    steps = jnp.arange(2 * reps * drows, dtype=jnp.int32) % STEPS
    positions = jnp.concatenate([jnp.arange(prompt_rows, dtype=jnp.int32), own_len + steps])
    cosine, sine = rope_tables(positions, HD)
    cosine = jnp.concatenate([cosine, cosine], axis=-1)
    sine = jnp.concatenate([-sine, sine], axis=-1)
    bias_row = lax.dynamic_slice_in_dim(qkv_bias, y * cols, cols, 0).astype(jnp.float32).reshape(1, cols)
    return fused(hidden, decode_hidden, norm_gain, qkv_weight, bias_row, cosine, sine, own_len)


def solution(mesh):
    return jax.shard_map(
        on_device,
        mesh=mesh,
        in_specs=(
            P("grp", "rep", None),
            P("grp", "rep", None, None, None),
            P(),
            P("grp", "tp"),
            P("tp"),
            P(),
        ),
        out_specs=(P("grp", "rep", "tp"), P("grp", "rep", None, None, "tp")),
        check_vma=False,
    )
```

```python
import jax
import jax.numpy as jnp
from jax import lax
from jax.experimental import pallas as pl
from jax.experimental.pallas import tpu as pltpu
from jax.sharding import PartitionSpec as P
import functools
import math

HD = 128
QPK = 8
STEPS = 4


THETA = 1000000.0
EPSILON = 1e-06
NEGATIVE = -1e30


def shifted(block, axis, distance):
    devices = range(lax.axis_size(axis))
    route = [((i - distance) % len(devices), i) for i in devices]
    return lax.ppermute(block, axis, route)


def normalize(row_block, gain_row):
    widened = row_block.astype(jnp.float32)
    factor = lax.rsqrt(jnp.mean(widened * widened, axis=-1, keepdims=True) + EPSILON)
    return (widened * factor * gain_row.astype(jnp.float32)).astype(jnp.bfloat16)


def rope_tables(positions, head_size):
    half_size = head_size // 2
    frequency = THETA ** (-(jnp.arange(half_size, dtype=jnp.float32) * 2.0 / head_size))
    angle = positions.astype(jnp.float32)[:, None] * frequency[None, :]
    return (jnp.cos(angle), jnp.sin(angle))


def rotate(vector, cosine, sine_part):
    half_size = vector.shape[-1] // 2
    first_half = vector[..., :half_size]
    second = vector[..., half_size:]
    return jnp.concatenate(
        [first_half * cosine - second * sine_part, second * cosine + first_half * sine_part],
        axis=-1,
    )


def masked_max(scores, allowed):
    return jnp.max(jnp.where(allowed, scores, NEGATIVE), axis=-1, keepdims=True)


def combine_values(weight_matrix, value_matrix):
    return jnp.einsum(
        "aprk,kaz->rapz",
        weight_matrix.astype(jnp.bfloat16),
        value_matrix,
        preferred_element_type=jnp.float32,
    )


def pair_scores(query_matrix, key_matrix_rows, score_scale):
    return (
        jnp.einsum(
            "wjro,ujo->jrwu", query_matrix, key_matrix_rows, preferred_element_type=jnp.float32
        )
        * score_scale
    )


def decode_pair(
    query_matrix,
    own_keys,
    own_values,
    prompt_keys,
    prompt_values,
    valid_len,
    local_allowed,
    score_scale,
):
    key_slot_index = jnp.arange(prompt_keys.shape[0], dtype=jnp.int32)
    prompt_allowed = (key_slot_index < valid_len)[None, None, None, :]
    far_scores = pair_scores(query_matrix, prompt_keys, score_scale)
    near_scores = pair_scores(query_matrix, own_keys, score_scale)
    highest = jnp.maximum(
        masked_max(far_scores, prompt_allowed), masked_max(near_scores, local_allowed)
    )
    far_exp = jnp.where(prompt_allowed, jnp.exp(far_scores - highest), 0.0)
    near_exp = jnp.where(local_allowed, jnp.exp(near_scores - highest), 0.0)
    running = jnp.sum(far_exp, axis=-1, keepdims=True) + jnp.sum(near_exp, axis=-1, keepdims=True)
    return combine_values(far_exp / running, prompt_values) + combine_values(
        near_exp / running, own_values
    )


def plain_device(hidden, decode_hidden, norm_gain, qkv_weight, qkv_bias, lengths):
    prompt_count = lax.axis_size("grp")
    rep_count = lax.axis_size("rep")
    half_cycle = prompt_count // 2
    grp_here = lax.axis_index("grp")
    rep_here = lax.axis_index("rep")
    span_rows = hidden.shape[1]
    model_width = hidden.shape[2]
    head_block = (QPK + 2) * HD
    heads_here = qkv_bias.shape[0] // head_block
    decode_rows = decode_hidden.shape[3]
    score_scale = HD ** (-0.5)
    prefill_normed = normalize(hidden[0], norm_gain)
    decode_normed = normalize(decode_hidden.reshape(2 * decode_rows, model_width), norm_gain)
    normed = jnp.concatenate([prefill_normed, decode_normed], axis=0)
    share_cols = qkv_weight.shape[1] // rep_count
    own_cols = lax.dynamic_slice_in_dim(qkv_weight, rep_here * share_cols, share_cols, 1)
    columns = lax.all_gather(own_cols, "grp", axis=0, tiled=True)
    complete = lax.all_gather(columns, "rep", axis=1, tiled=True)
    projected = jnp.dot(normed, complete, preferred_element_type=jnp.float32)
    projected = (projected + qkv_bias.astype(jnp.float32)).reshape(
        normed.shape[0], heads_here, QPK + 2, HD
    )
    index_table = jnp.arange(prompt_count, dtype=jnp.int32)

    def length_of(prompt):
        return jnp.sum(jnp.where(index_table == prompt, lengths, 0))

    own_len = length_of(grp_here)
    far_len = length_of((grp_here + half_cycle) % prompt_count)
    row_position = rep_here * span_rows + jnp.arange(span_rows, dtype=jnp.int32)
    local_ids = jnp.arange(decode_rows, dtype=jnp.int32)
    step_ids = local_ids % STEPS
    sample_ids = local_ids // STEPS
    positions = jnp.concatenate([row_position, own_len + step_ids, far_len + step_ids])
    cosine, sine_part = rope_tables(positions, HD)
    query_matrix = rotate(
        projected[:, :, :QPK], cosine[:, None, None, :], sine_part[:, None, None, :]
    ).astype(jnp.bfloat16)
    key_matrix_rows = rotate(
        projected[:, :, QPK], cosine[:, None, :], sine_part[:, None, :]
    ).astype(jnp.bfloat16)
    value_matrix = projected[:, :, QPK + 1].astype(jnp.bfloat16)
    cache_keys, cache_values = (
        lax.all_gather(key_matrix_rows[:span_rows], "rep", axis=0, tiled=True),
        lax.all_gather(value_matrix[:span_rows], "rep", axis=0, tiled=True),
    )
    key_pos = jnp.arange(cache_keys.shape[0], dtype=jnp.int32)
    allowed = ((key_pos[None, :] <= row_position[:, None]) & (key_pos[None, :] < own_len))[
        None, None
    ]
    scores = pair_scores(query_matrix[:span_rows], cache_keys, score_scale)
    highest = masked_max(scores, allowed)
    exponent = jnp.where(allowed, jnp.exp(scores - highest), 0.0)
    weight_matrix = exponent / jnp.sum(exponent, axis=-1, keepdims=True)
    attended = combine_values(weight_matrix, cache_values)
    prefill_out = attended.astype(jnp.bfloat16).reshape(1, span_rows, heads_here * QPK * HD)
    decode_queries = query_matrix[span_rows:].reshape(2, decode_rows, heads_here, QPK, HD)
    decode_keys = key_matrix_rows[span_rows:].reshape(2, decode_rows, heads_here, HD)
    decode_values = value_matrix[span_rows:].reshape(2, decode_rows, heads_here, HD)
    local_allowed = (
        (sample_ids[None, :] == sample_ids[:, None]) & (step_ids[None, :] <= step_ids[:, None])
    )[None, None]
    near_out = decode_pair(
        decode_queries[0],
        decode_keys[0],
        decode_values[0],
        cache_keys,
        cache_values,
        own_len,
        local_allowed,
        score_scale,
    )
    far_keys, far_values = shifted((cache_keys, cache_values), "grp", half_cycle)
    far_out = decode_pair(
        decode_queries[1],
        decode_keys[1],
        decode_values[1],
        far_keys,
        far_values,
        far_len,
        local_allowed,
        score_scale,
    )
    decode_out = (
        jnp.stack([near_out, far_out])
        .astype(jnp.bfloat16)
        .reshape(1, 1, 2, decode_rows, heads_here * QPK * HD)
    )
    return (prefill_out, decode_out)


MESH = pl.DeviceIdType.MESH
SUBS = 4
GROUPS = QPK // 2 + 1
WIDE = 2 * HD


def fused_kernel(
    len_ref, hidden_ref, decode_ref, gain_ref, w_ref, bias_ref, cos_ref, sin_ref,
    prefill_ref, out_decode_ref, wbuf_ref, land_ref,
    acc_ref, xh_ref, nv_ref, wt_ref, accp_ref, pb_ref, q_ref, k_ref, v_ref, m_ref, out_ref,
    wi_s, wo_s, wb_s, wy_s, w_r,
    xa_s, xb_s, xc_s, xd_s, xf_s, x_r,
    p_s, p_r, l_s, t_s, o_s, o_r, o_l,
):
    g = lax.axis_index("grp")
    r = lax.axis_index("rep")
    x = lax.axis_index("tp")
    z = g // 2
    y = g % 2
    hi = z // 2
    zin = z + 1 - 2 * hi
    zout = z - 1 + 2 * hi
    mid = (z == 1) | (z == 2)
    end = (z == 0) | (z == 3)
    mid_count = (z // 2 + z % 2) % 2
    home = r == y
    away = r != y
    span = hidden_ref.shape[1]
    drows = decode_ref.shape[3]
    share = w_ref.shape[0]
    cols = acc_ref.shape[1]
    head = cols // 2
    half = xh_ref.shape[2]
    quarter = half // 2
    rows_all = acc_ref.shape[0]
    sub = span // SUBS
    sides = 4

    barrier = pltpu.get_barrier_semaphore()

    def greet(grp, rep, tp):
        pl.semaphore_signal(
            barrier, inc=1, device_id={"grp": grp, "rep": rep, "tp": tp}, device_id_type=MESH
        )

    pair = 2 * z + 1 - y
    greet(g, 1 - r, x)
    greet(g, r, 1 - x)
    for c in (0, 1):
        greet(pair, c, x)
        greet((g + 4) % 8, c, x)
        greet((g + 4) % 8 + 1 - 2 * y, c, x)
        greet(2 * zin + y, c, x)

    @pl.when(mid)
    def _():
        for c in (0, 1):
            greet(2 * zout + y, c, x)
        pl.semaphore_wait(barrier, 12)

    @pl.when(end)
    def _():
        pl.semaphore_wait(barrier, 10)

    def offset(k):
        return ((k + GROUPS - 1) % GROUPS) * WIDE

    def own_cols(line, h, k):
        return w_ref.at[:, pl.ds(pl.multiple_of(line * cols + h * head + offset(k), 128), WIDE)]

    def remote(src, dst, ssem, rsem, **device):
        return pltpu.make_async_remote_copy(
            src, dst, ssem, rsem, device_id=device, device_id_type=MESH
        )

    def w_copy(o, k, own, kind):
        src = own_cols(y, r, k) if own else wbuf_ref.at[o, k, r]
        dst = wbuf_ref.at[o, k, r]
        if kind == 0:
            return remote(src, dst, wi_s.at[o, k], w_r.at[o, k, r], grp=2 * zin + y)
        if kind == 1:
            return remote(src, dst, wo_s.at[o, k], w_r.at[o, k, r], grp=2 * zout + y)
        return remote(src, dst, wb_s.at[o, k], w_r.at[o, k, r], rep=1 - r)

    def w_cross(k):
        return remote(own_cols(1 - y, r, k), wbuf_ref.at[g, k, r], wy_s.at[k], w_r.at[g, k, r], grp=pair)

    def w_arrived(o, k, h):
        remote(wbuf_ref.at[o, k, h], wbuf_ref.at[o, k, h], wb_s.at[o, k], w_r.at[o, k, h], rep=1 - r).wait_recv()

    def own_sends(k):
        @pl.when(mid)
        def _():
            w_copy(g, k, True, 1).start()

        @pl.when(end)
        def _():
            w_copy(g, k, True, 0).start()

    for k in (0, 1):
        own_sends(k)
    w_cross(0).start()

    @pl.when(mid)
    def _():
        w_copy(g, 0, True, 0).start()
        w_copy(g, 1, True, 0).start()

    raw = [
        pltpu.make_async_copy(decode_ref.at[0, 0, 1], nv_ref.at[pl.ds(span + drows, drows), :], l_s.at[0]),
        pltpu.make_async_copy(decode_ref.at[0, 0, 0], nv_ref.at[pl.ds(span, drows), :], l_s.at[1]),
        pltpu.make_async_copy(hidden_ref.at[0], nv_ref.at[pl.ds(0, span), :], l_s.at[2]),
    ]
    for copy in raw:
        copy.start()

    gain = gain_ref[...].astype(jnp.float32)

    def norm(first, n):
        @pl.loop(0, n // 16)
        def _(i):
            rows = pl.ds(pl.multiple_of(first + i * 16, 16), 16)
            wide = nv_ref[rows, :].astype(jnp.float32)
            factor = lax.rsqrt(jnp.mean(wide * wide, axis=-1, keepdims=True) + EPSILON)
            nv_ref[rows, :] = (wide * factor * gain).astype(jnp.bfloat16)

    def place(piece, rr):
        if piece < SUBS:
            return pl.multiple_of(rr * span + piece * sub, 16), sub
        return pl.multiple_of(2 * span + ((piece - SUBS) * 2 + rr) * drows, 16), drows

    def source(piece, k_half, part=None):
        start, n = (piece * sub, sub) if piece < SUBS else (span + (piece - SUBS) * drows, drows)
        if part is None:
            return nv_ref.at[pl.ds(start, n), pl.ds(pl.multiple_of(k_half * half, 128), half)]
        return nv_ref.at[pl.ds(start, n), pl.ds(pl.multiple_of(k_half * half + part * quarter, 128), quarter)]

    def spot(slot, piece, rr):
        start, n = place(piece, rr)
        return xh_ref.at[slot, pl.ds(start, n), :]

    def spot_part(part, piece, rr):
        start, n = place(piece, rr)
        return xh_ref.at[2, pl.ds(start, n), pl.ds(pl.multiple_of(part * quarter, 128), quarter)]

    near_half = hi
    far_half = 1 - hi

    def x_to_home(piece, slot, k_half):
        return remote(source(piece, k_half), spot(slot, piece, r), xa_s.at[slot, piece], x_r.at[slot, piece, r], rep=y)

    def x_local(piece, slot, k_half):
        return pltpu.make_async_copy(source(piece, k_half), spot(slot, piece, r), x_r.at[slot, piece, r])

    def x_to_away(piece):
        slot = jnp.where(mid, x, 0)
        k_half = hi + slot * (1 - 2 * hi)
        return remote(source(piece, k_half), spot(slot, piece, r), xb_s.at[piece], x_r.at[slot, piece, r], grp=pair, rep=y)

    def x_to_mid(piece):
        return remote(
            source(piece, far_half, x), spot_part(x, piece, r), xc_s.at[piece], x_r.at[2 + x, piece, r],
            grp=2 * zin + y, rep=y,
        )

    FAR = SUBS + 1
    NEAR = SUBS
    far_g = (g + 4) % 8

    def far_from_end():
        k_half = far_half + x * (1 - 2 * far_half)
        return remote(source(FAR, k_half), spot(x, FAR, r), xd_s.at[0], x_r.at[x, FAR, r], grp=far_g, rep=y)

    def far_to_end():
        return remote(source(FAR, far_half), spot(0, FAR, r), xd_s.at[0], x_r.at[0, FAR, r], grp=far_g, rep=y)

    def far_to_mid():
        return remote(
            source(FAR, near_half, x), spot_part(x, FAR, r), xd_s.at[1], x_r.at[2 + x, FAR, r],
            grp=2 * zin + y, rep=y,
        )

    def send_piece(piece):
        x_to_away(piece).start()

        @pl.when(end)
        def _():
            x_to_mid(piece).start()

        @pl.when(home)
        def _():
            x_local(piece, 0, near_half).start()

            @pl.when(mid)
            def _():
                x_local(piece, 1, far_half).start()

        @pl.when(away)
        def _():
            x_to_home(piece, 0, near_half).start()

            @pl.when(mid)
            def _():
                x_to_home(piece, 1, far_half).start()

    raw[0].wait()
    norm(span + drows, drows)

    @pl.when(mid)
    def _():
        far_to_end().start()
        far_to_mid().start()

    @pl.when(end)
    def _():
        far_from_end().start()

    @pl.when(mid)
    def _():
        for k in range(2, GROUPS):
            w_copy(g, k, True, 0).start()

    raw[1].wait()
    norm(span, drows)
    send_piece(NEAR)
    raw[2].wait()
    for s in range(SUBS):
        norm(s * sub, sub)
        send_piece(s)
    for k in (1, 2):
        w_cross(k).start()

    @pl.loop(0, rows_all // 16)
    def _(i):
        acc_ref[pl.ds(pl.multiple_of(i * 16, 16), 16), :] = jnp.zeros((16, cols), jnp.float32)

    across = {"grp": pair}
    beside = {"tp": 1 - x}
    MAIN = [NEAR] + list(range(SUBS))

    def x_forward(slot, piece, rr, way, device):
        where = spot(slot, piece, rr)
        return remote(where, where, xf_s.at[way, slot, piece, rr], x_r.at[slot, piece, rr], **device)

    def part_forward(part, piece, rr, way, device):
        where = spot_part(part, piece, rr)
        return remote(where, where, xf_s.at[way, 2 + part, piece, rr], x_r.at[2 + part, piece, rr], **device)

    def arrived(make, slot, piece, rr):
        make(slot, piece, rr, 0, {"rep": 1 - r}).wait_recv()

    def relay(make, slot, piece, ways):
        for rr in (0, 1):
            arrived(make, slot, piece, rr)
            for way in ways:
                make(slot, piece, rr, way, (across, beside)[way]).start()

    def settle(make, slot, piece, ways):
        for rr in (0, 1):
            for way in ways:
                make(slot, piece, rr, way, (across, beside)[way]).wait_send()

    EARLY = MAIN[:3]
    LATER = MAIN[3:]

    def forward_early(act):
        @pl.when(home & end)
        def _():
            act(x_forward, 0, FAR, (0,))

        @pl.when(home & mid)
        def _():
            act(x_forward, x, FAR, (0, 1))
            for piece in [FAR] + EARLY:
                act(part_forward, x, piece, (0, 1))

        @pl.when(away & mid)
        def _():
            for piece in EARLY:
                act(x_forward, x, piece, (1,))

    def forward_first(act):
        @pl.when(home & mid)
        def _():
            for piece in LATER:
                act(part_forward, x, piece, (0, 1))

        @pl.when(away & mid)
        def _():
            for piece in LATER[:-1]:
                act(x_forward, x, piece, (1,))

    def forward_late(act):
        @pl.when(away & mid)
        def _():
            act(x_forward, x, LATER[-1], (1,))
            act(x_forward, x, FAR, (1,))

    def forward_part(act, pieces):
        @pl.when(away & mid)
        def _():
            for piece in pieces:
                act(part_forward, x, piece, (1,))

    def wait_x():
        @pl.when(home)
        def _():
            def both(slot, k_half):
                for piece in MAIN:
                    x_local(piece, slot, k_half).wait()
                    arrived(x_forward, slot, piece, 1 - r)

            both(0, near_half)

            @pl.when(mid)
            def _():
                both(1, far_half)
                for rr in (0, 1):
                    arrived(x_forward, 1 - x, FAR, rr)

        @pl.when(away)
        def _():
            slot = jnp.where(mid, 1 - x, 0)
            for piece in MAIN + [FAR]:
                for rr in (0, 1):
                    arrived(x_forward, slot, piece, rr)

    def wait_part():
        @pl.when(mid)
        def _():
            for piece in MAIN + [FAR]:
                for rr in (0, 1):
                    arrived(part_forward, 1 - x, piece, rr)

    def pass_w(k):
        def outer(yy):
            o = 2 * zout + yy
            w_arrived(o, k, r)
            w_copy(o, k, False, 0).start()
            w_copy(o, k, False, 2).start()

        @pl.when(mid)
        def _():
            outer(y)

        w_arrived(pair, k, r)
        w_copy(pair, k, False, 0).start()

        @pl.when(mid)
        def _():
            w_copy(pair, k, False, 1).start()

        w_copy(pair, k, False, 2).start()

        @pl.when(mid)
        def _():
            outer(1 - y)

    def take_w(k):
        def over(layer):
            for yy in (y, 1 - y):
                o = 2 * layer + yy
                w_arrived(o, k, r)
                w_copy(o, k, False, 2).start()

        over(zin)

        @pl.when(mid)
        def _():
            over(zin + 1 - 2 * hi)
            for yy in (0, 1):
                w_arrived(2 * zout + yy, k, 1 - r)
            for i in range(sides):
                w_arrived(sides * (1 - hi) + i, k, 1 - r)

        @pl.when(end)
        def _():
            for yy in (0, 1):
                w_arrived(2 * zin + yy, k, 1 - r)

        w_arrived(pair, k, 1 - r)

    def p_copy(k):
        return remote(pb_ref.at[k % 2], land_ref.at[k], p_s.at[k], p_r.at[k], grp=2 * zout + y)

    def fetch(k, o, slot):
        for h in (0, 1):
            dst = wt_ref.at[slot, h]

            @pl.when(o == g)
            def _():
                pltpu.make_async_copy(own_cols(y, h, k), dst, t_s.at[slot, h]).start()

            @pl.when(o != g)
            def _():
                pltpu.make_async_copy(wbuf_ref.at[o, k, h], dst, t_s.at[slot, h]).start()

    def tile_done(slot):
        for h in (0, 1):
            pltpu.make_async_copy(wbuf_ref.at[0, 0, h], wt_ref.at[slot, h], t_s.at[slot, h]).wait()

    def slice_at(j):
        return (sides * (1 - hi) + j) % (2 * sides)

    def columns_of(o):
        return pl.ds(pl.multiple_of((o % sides) * share, 128), share)

    def compute(k):
        @pl.when(mid)
        def _():
            fetch(k, slice_at(0), 0)

        @pl.when(end)
        def _():
            fetch(k, slice_at(sides), 0)

        @pl.loop(0, 2 * sides)
        def _(j):
            o = slice_at(j)
            slot = j % 2

            @pl.when((j >= sides) | mid)
            def _():
                @pl.when(j + 1 < 2 * sides)
                def _():
                    fetch(k, slice_at(j + 1), (j + 1) % 2)

                tile_done(slot)
                for h in (0, 1):
                    place_h = pl.ds(pl.multiple_of(h * head + offset(k), 128), WIDE)
                    acc_ref[:, place_h] += jnp.dot(
                        xh_ref[1 - j // sides, :, columns_of(o)], wt_ref[slot, h], preferred_element_type=jnp.float32
                    )

    def partial(k):
        @pl.loop(0, rows_all // 16)
        def _(i):
            accp_ref[pl.ds(pl.multiple_of(i * 16, 16), 16), :] = jnp.zeros((16, 2 * WIDE), jnp.float32)

        fetch(k, slice_at(0), 0)

        @pl.loop(0, sides)
        def _(j):
            o = slice_at(j)
            slot = j % 2

            @pl.when(j + 1 < sides)
            def _():
                fetch(k, slice_at(j + 1), (j + 1) % 2)

            tile_done(slot)
            for h in (0, 1):
                accp_ref[:, h * WIDE:(h + 1) * WIDE] += jnp.dot(
                    xh_ref[2, :, columns_of(o)], wt_ref[slot, h], preferred_element_type=jnp.float32
                )

        @pl.when(k >= 2)
        def _():
            p_copy(k - 2).wait_send()

        @pl.loop(0, rows_all // 16)
        def _(i):
            rows = pl.ds(pl.multiple_of(i * 16, 16), 16)
            pb_ref[k % 2, rows, :] = accp_ref[rows, :].astype(jnp.bfloat16)

        p_copy(k).start()

    def add_partial(k):
        remote(pb_ref.at[0], land_ref.at[k], p_s.at[k], p_r.at[k], grp=2 * zin + y).wait_recv()
        take = pltpu.make_async_copy(land_ref.at[k], pb_ref.at[0], l_s.at[3])
        take.start()
        take.wait()

        @pl.loop(0, rows_all // 16)
        def _(i):
            rows = pl.ds(pl.multiple_of(i * 16, 16), 16)
            for h in (0, 1):
                place_h = pl.ds(pl.multiple_of(h * head + offset(k), 128), WIDE)
                acc_ref[rows, place_h] += pb_ref[0, rows, h * WIDE:(h + 1) * WIDE].astype(jnp.float32)

    prompt = g - y + r
    prompt_rows = 2 * span
    valid = len_ref[0]
    block = 256 if prompt_rows % 256 == 0 else prompt_rows
    blocks = [(prompt_rows, rows_all - prompt_rows, rows_all)]
    blocks += [(start, block, start + block) for start in range(0, prompt_rows, block)]
    starts = (0, prompt_rows, prompt_rows + 2 * drows)
    sizes = (span, drows, drows)
    width = QPK * HD

    def mask_place(index):
        top = 0
        for start, size, keys in blocks[:index]:
            top += size
        return slice(top, top + blocks[index][1]), slice(0, blocks[index][2])

    def make_masks():
        for index, (start, size, keys) in enumerate(blocks):
            shape = (size, keys)
            row = lax.broadcasted_iota(jnp.int32, shape, 0) + start
            col = lax.broadcasted_iota(jnp.int32, shape, 1)
            if start < prompt_rows:
                allowed = (col <= row) & (col < valid)
            else:
                same = ((row - prompt_rows) // STEPS == (col - prompt_rows) // STEPS) & (col <= row)
                allowed = (col < jnp.minimum(valid, prompt_rows)) | ((col >= prompt_rows) & same)
            m_ref[mask_place(index)] = jnp.where(allowed, 0.0, NEGATIVE)

    def target(f, h, c, line):
        at = pl.ds(pl.multiple_of((line * 2 + h) * width + offset(f), 128), WIDE)
        return (prefill_ref.at[0, :, at], out_decode_ref.at[0, 0, 0, :, at], out_decode_ref.at[0, 0, 1, :, at])[c]

    def out_piece(f, h, c, rr):
        start = pl.multiple_of(starts[c] + rr * sizes[c], 16)
        return out_ref.at[f - 1, h, pl.ds(start, sizes[c]), :]

    def out_send(f, h, c, rr):
        grp = (prompt + 4) % 8 if c == 2 else prompt
        return remote(
            out_piece(f, h, c, rr), target(f, h, c, y), o_s.at[f - 1, h, c, rr], o_r.at[f - 1, h, c, y],
            grp=grp, rep=rr,
        )

    def out_keep(f, h, c):
        return pltpu.make_async_copy(out_piece(f, h, c, r), target(f, h, c, y), o_l.at[f - 1, h, c])

    def out_receive(f, h, c, line):
        remote(
            out_piece(f, h, c, 0), target(f, h, c, line), o_s.at[f - 1, h, c, 0], o_r.at[f - 1, h, c, line], rep=1 - r
        ).wait_recv()

    def each_out(f, h, c, act, keep_act):
        if c == 2:
            act(out_send(f, h, c, 0))
            act(out_send(f, h, c, 1))
            return

        @pl.when(home)
        def _():
            keep_act(out_keep(f, h, c))
            act(out_send(f, h, c, 1 - r))

        @pl.when(away)
        def _():
            act(out_send(f, h, c, 0))
            act(out_send(f, h, c, 1))

    def begin(copy):
        copy.start()

    def sent(copy):
        copy.wait_send()

    def kept(copy):
        copy.wait()

    def finish(f):
        factor = HD ** (-0.5) * math.log2(math.e)

        def part(h, first):
            at = pl.ds(pl.multiple_of(h * head + first, 128), HD)
            return acc_ref[:, at] + bias_ref[:, at]

        def turned(v):
            return v * cos_ref[...] + pltpu.roll(v, HD // 2, 1) * sin_ref[...]

        @pl.when(f == 0)
        def _():
            for h in (0, 1):
                k_ref[h] = turned(part(h, QPK * HD)).astype(jnp.bfloat16)
                v_ref[h] = part(h, (QPK + 1) * HD).astype(jnp.bfloat16)

        @pl.when(f > 0)
        def _():
            @pl.loop(0, 2)
            def _(h):
                for j in (0, 1):
                    q_ref[j] = (turned(part(h, offset(f) + j * HD)) * factor).astype(jnp.bfloat16)
                for index, (start, size, keys) in enumerate(blocks):
                    for j in (0, 1):
                        s = lax.dot_general(
                            q_ref[j, start:start + size, :], k_ref[h, :keys, :], (((1,), (1,)), ((), ())),
                            preferred_element_type=jnp.float32,
                        ) + m_ref[mask_place(index)]
                        top = jnp.max(s, axis=-1, keepdims=True)
                        p = jnp.exp2(s - top)
                        total = jnp.sum(p, axis=-1, keepdims=True)
                        o = jnp.dot(p.astype(jnp.bfloat16), v_ref[h, :keys, :], preferred_element_type=jnp.float32)
                        out_ref[f - 1, h, start:start + size, j * HD:(j + 1) * HD] = (o / total).astype(jnp.bfloat16)
                    if index == 0:
                        each_out(f, h, 2, begin, begin)
                        each_out(f, h, 1, begin, begin)
                each_out(f, h, 0, begin, begin)

    @pl.loop(0, GROUPS + 4)
    def _(t):
        @pl.when(t == 0)
        def _():
            forward_early(relay)

        @pl.when(t < GROUPS)
        def _():
            pass_w(t)

        @pl.when(t + 2 < GROUPS)
        def _():
            own_sends(t + 2)

        @pl.when(t == 0)
        def _():
            forward_first(relay)
            for k in range(3, GROUPS):
                w_cross(k).start()
            make_masks()

        @pl.when(t == 1)
        def _():
            forward_late(relay)

        @pl.when(t == 2)
        def _():
            wait_x()

        @pl.when(t == 3)
        def _():
            forward_part(relay, [FAR] + EARLY)

        @pl.when((t >= 2) & (t < GROUPS + 2))
        def _():
            take_w(t - 2)

            @pl.when(mid & ((home & (t == 3)) | (away & (t == 4))))
            def _():
                wait_part()

            @pl.loop(0, GROUPS)
            def _(k):
                due = ((t >= 4) & (k == t - 2)) | (home & (t == 3) & (k <= 1)) | (away & (t == 4) & (k <= 1))

                @pl.when(mid & due)
                def _():
                    partial(k)

            compute(t - 2)

        @pl.when(t == 3)
        def _():
            forward_part(relay, LATER)

        f = t - 4 + 2 * mid_count

        @pl.when((f >= 0) & (f < GROUPS))
        def _():
            @pl.when(end)
            def _():
                add_partial(f)

            finish(f)

    @pl.loop(1, GROUPS)
    def _(f):
        for h in (0, 1):
            for c in range(3):
                each_out(f, h, c, sent, kept)
                if c == 2:
                    out_receive(f, h, c, 0)
                    out_receive(f, h, c, 1)
                else:
                    out_receive(f, h, c, 1 - y)

                    @pl.when(away)
                    def _():
                        out_receive(f, h, c, y)

    @pl.when(mid)
    def _():
        p_copy(GROUPS - 2).wait_send()
        p_copy(GROUPS - 1).wait_send()

    @pl.when(mid)
    def _():
        far_to_end().wait_send()
        far_to_mid().wait_send()

    @pl.when(end)
    def _():
        far_from_end().wait_send()

    for piece in [NEAR] + list(range(SUBS)):
        x_to_away(piece).wait_send()

        @pl.when(end)
        def _():
            x_to_mid(piece).wait_send()

        @pl.when(away)
        def _():
            x_to_home(piece, 0, near_half).wait_send()

            @pl.when(mid)
            def _():
                x_to_home(piece, 1, far_half).wait_send()

    forward_early(settle)
    forward_first(settle)
    forward_late(settle)
    forward_part(settle, [FAR] + MAIN)

    @pl.loop(0, GROUPS)
    def _(k):
        w_cross(k).wait_send()
        for o in (g, pair):
            w_copy(o, k, False, 0).wait_send()

            @pl.when(mid)
            def _():
                w_copy(o, k, False, 1).wait_send()

        w_copy(pair, k, False, 2).wait_send()

        @pl.when(mid)
        def _():
            for yy in (0, 1):
                w_copy(2 * zout + yy, k, False, 0).wait_send()
                w_copy(2 * zout + yy, k, False, 2).wait_send()
            for i in range(sides):
                w_copy(sides * (1 - hi) + i, k, False, 2).wait_send()

        @pl.when(end)
        def _():
            for yy in (0, 1):
                w_copy(2 * zin + yy, k, False, 2).wait_send()


def fused(hidden, decode_hidden, norm_gain, qkv_weight, bias_row, cosine, sine, valid):
    count = lax.axis_size("grp")
    own_rows = hidden.shape[1] + 2 * decode_hidden.shape[3]
    rows = 2 * own_rows
    share = qkv_weight.shape[0]
    width = hidden.shape[2]
    cols = qkv_weight.shape[1] // 2
    out_width = 4 * QPK * HD
    pieces = SUBS + 2
    hbm = pl.BlockSpec(memory_space=pl.ANY)
    vmem = pl.BlockSpec(memory_space=pltpu.VMEM)
    smem = pl.BlockSpec(memory_space=pltpu.SMEM)
    dma = pltpu.SemaphoreType.DMA
    outs = GROUPS - 1
    return pl.pallas_call(
        fused_kernel,
        out_shape=(
            jax.ShapeDtypeStruct(hidden.shape[:2] + (out_width,), jnp.bfloat16),
            jax.ShapeDtypeStruct(decode_hidden.shape[:4] + (out_width,), jnp.bfloat16),
            jax.ShapeDtypeStruct((count, GROUPS, 2, share, WIDE), jnp.bfloat16),
            jax.ShapeDtypeStruct((GROUPS, rows, 2 * WIDE), jnp.bfloat16),
        ),
        in_specs=[smem, hbm, hbm, vmem, hbm, vmem, vmem, vmem],
        out_specs=(hbm, hbm, hbm, hbm),
        scratch_shapes=[
            pltpu.VMEM((rows, cols), jnp.float32),
            pltpu.VMEM((3, rows, width // 2), jnp.bfloat16),
            pltpu.VMEM((own_rows, width), jnp.bfloat16),
            pltpu.VMEM((2, 2, share, WIDE), jnp.bfloat16),
            pltpu.VMEM((rows, 2 * WIDE), jnp.float32),
            pltpu.VMEM((2, rows, 2 * WIDE), jnp.bfloat16),
            pltpu.VMEM((2, rows, HD), jnp.bfloat16),
            pltpu.VMEM((2, rows, HD), jnp.bfloat16),
            pltpu.VMEM((2, rows, HD), jnp.bfloat16),
            pltpu.VMEM((rows, rows), jnp.float32),
            pltpu.VMEM((outs, 2, rows, WIDE), jnp.bfloat16),
            dma((count, GROUPS)), dma((count, GROUPS)), dma((count, GROUPS)), dma((GROUPS,)),
            dma((count, GROUPS, 2)),
            dma((2, SUBS + 1)), dma((SUBS + 1,)), dma((SUBS + 1,)), dma((2,)),
            dma((2, 4, pieces, 2)), dma((4, pieces, 2)),
            dma((GROUPS,)), dma((GROUPS,)), dma((4,)), dma((2, 2)),
            dma((outs, 2, 3, 2)), dma((outs, 2, 3, 2)), dma((outs, 2, 3)),
        ],
        compiler_params=pltpu.CompilerParams(
            collective_id=0, has_side_effects=True, vmem_limit_bytes=60 << 20
        ),
        name="fused",
    )(valid.reshape(1), hidden, decode_hidden, norm_gain.reshape(1, width), qkv_weight, bias_row, cosine, sine)[:2]


def on_device(hidden, decode_hidden, norm_gain, qkv_weight, qkv_bias, lengths):
    count = lax.axis_size("grp")
    reps = lax.axis_size("rep")
    head_block = (QPK + 2) * HD
    heads_here = qkv_bias.shape[0] // head_block
    if reps != 2 or count != 8 or lax.axis_size("tp") != 2 or heads_here != 4 or decode_hidden.shape[1] != 1:
        return plain_device(hidden, decode_hidden, norm_gain, qkv_weight, qkv_bias, lengths)
    g = lax.axis_index("grp")
    r = lax.axis_index("rep")
    y = g % 2
    prompt = g - y + r
    cols = qkv_weight.shape[1] // 2
    drows = decode_hidden.shape[3]
    prompt_rows = reps * hidden.shape[1]
    index_table = jnp.arange(count, dtype=jnp.int32)
    own_len = jnp.sum(jnp.where(index_table == prompt, lengths, 0))
    steps = jnp.arange(2 * reps * drows, dtype=jnp.int32) % STEPS
    positions = jnp.concatenate([jnp.arange(prompt_rows, dtype=jnp.int32), own_len + steps])
    cosine, sine = rope_tables(positions, HD)
    cosine = jnp.concatenate([cosine, cosine], axis=-1)
    sine = jnp.concatenate([-sine, sine], axis=-1)
    bias_row = lax.dynamic_slice_in_dim(qkv_bias, y * cols, cols, 0).astype(jnp.float32).reshape(1, cols)
    return fused(hidden, decode_hidden, norm_gain, qkv_weight, bias_row, cosine, sine, own_len)


def solution(mesh):
    return jax.shard_map(
        on_device,
        mesh=mesh,
        in_specs=(
            P("grp", "rep", None),
            P("grp", "rep", None, None, None),
            P(),
            P("grp", "tp"),
            P("tp"),
            P(),
        ),
        out_specs=(P("grp", "rep", "tp"), P("grp", "rep", None, None, "tp")),
        check_vma=False,
    )
```

```python
import jax
import jax.numpy as jnp
from jax import lax
from jax.experimental import pallas as pl
from jax.experimental.pallas import tpu as pltpu
from jax.sharding import PartitionSpec as P
import functools
import math
import numpy as np

HD = 128
QPK = 8
STEPS = 4


THETA = 1000000.0
EPSILON = 1e-06
NEGATIVE = -1e30


def shifted(block, axis, distance):
    devices = range(lax.axis_size(axis))
    route = [((i - distance) % len(devices), i) for i in devices]
    return lax.ppermute(block, axis, route)


def normalize(row_block, gain_row):
    widened = row_block.astype(jnp.float32)
    factor = lax.rsqrt(jnp.mean(widened * widened, axis=-1, keepdims=True) + EPSILON)
    return (widened * factor * gain_row.astype(jnp.float32)).astype(jnp.bfloat16)


def rope_tables(positions, head_size):
    half_size = head_size // 2
    frequency = THETA ** (-(jnp.arange(half_size, dtype=jnp.float32) * 2.0 / head_size))
    angle = positions.astype(jnp.float32)[:, None] * frequency[None, :]
    return (jnp.cos(angle), jnp.sin(angle))


def rotate(vector, cosine, sine_part):
    half_size = vector.shape[-1] // 2
    first_half = vector[..., :half_size]
    second = vector[..., half_size:]
    return jnp.concatenate(
        [first_half * cosine - second * sine_part, second * cosine + first_half * sine_part],
        axis=-1,
    )


def masked_max(scores, allowed):
    return jnp.max(jnp.where(allowed, scores, NEGATIVE), axis=-1, keepdims=True)


def combine_values(weight_matrix, value_matrix):
    return jnp.einsum(
        "aprk,kaz->rapz",
        weight_matrix.astype(jnp.bfloat16),
        value_matrix,
        preferred_element_type=jnp.float32,
    )


def pair_scores(query_matrix, key_matrix_rows, score_scale):
    return (
        jnp.einsum(
            "wjro,ujo->jrwu", query_matrix, key_matrix_rows, preferred_element_type=jnp.float32
        )
        * score_scale
    )


def decode_pair(
    query_matrix,
    own_keys,
    own_values,
    prompt_keys,
    prompt_values,
    valid_len,
    local_allowed,
    score_scale,
):
    key_slot_index = jnp.arange(prompt_keys.shape[0], dtype=jnp.int32)
    prompt_allowed = (key_slot_index < valid_len)[None, None, None, :]
    far_scores = pair_scores(query_matrix, prompt_keys, score_scale)
    near_scores = pair_scores(query_matrix, own_keys, score_scale)
    highest = jnp.maximum(
        masked_max(far_scores, prompt_allowed), masked_max(near_scores, local_allowed)
    )
    far_exp = jnp.where(prompt_allowed, jnp.exp(far_scores - highest), 0.0)
    near_exp = jnp.where(local_allowed, jnp.exp(near_scores - highest), 0.0)
    running = jnp.sum(far_exp, axis=-1, keepdims=True) + jnp.sum(near_exp, axis=-1, keepdims=True)
    return combine_values(far_exp / running, prompt_values) + combine_values(
        near_exp / running, own_values
    )


def plain_device(hidden, decode_hidden, norm_gain, qkv_weight, qkv_bias, lengths):
    prompt_count = lax.axis_size("grp")
    rep_count = lax.axis_size("rep")
    half_cycle = prompt_count // 2
    grp_here = lax.axis_index("grp")
    rep_here = lax.axis_index("rep")
    span_rows = hidden.shape[1]
    model_width = hidden.shape[2]
    head_block = (QPK + 2) * HD
    heads_here = qkv_bias.shape[0] // head_block
    decode_rows = decode_hidden.shape[3]
    score_scale = HD ** (-0.5)
    prefill_normed = normalize(hidden[0], norm_gain)
    decode_normed = normalize(decode_hidden.reshape(2 * decode_rows, model_width), norm_gain)
    normed = jnp.concatenate([prefill_normed, decode_normed], axis=0)
    share_cols = qkv_weight.shape[1] // rep_count
    own_cols = lax.dynamic_slice_in_dim(qkv_weight, rep_here * share_cols, share_cols, 1)
    columns = lax.all_gather(own_cols, "grp", axis=0, tiled=True)
    complete = lax.all_gather(columns, "rep", axis=1, tiled=True)
    projected = jnp.dot(normed, complete, preferred_element_type=jnp.float32)
    projected = (projected + qkv_bias.astype(jnp.float32)).reshape(
        normed.shape[0], heads_here, QPK + 2, HD
    )
    index_table = jnp.arange(prompt_count, dtype=jnp.int32)

    def length_of(prompt):
        return jnp.sum(jnp.where(index_table == prompt, lengths, 0))

    own_len = length_of(grp_here)
    far_len = length_of((grp_here + half_cycle) % prompt_count)
    row_position = rep_here * span_rows + jnp.arange(span_rows, dtype=jnp.int32)
    local_ids = jnp.arange(decode_rows, dtype=jnp.int32)
    step_ids = local_ids % STEPS
    sample_ids = local_ids // STEPS
    positions = jnp.concatenate([row_position, own_len + step_ids, far_len + step_ids])
    cosine, sine_part = rope_tables(positions, HD)
    query_matrix = rotate(
        projected[:, :, :QPK], cosine[:, None, None, :], sine_part[:, None, None, :]
    ).astype(jnp.bfloat16)
    key_matrix_rows = rotate(
        projected[:, :, QPK], cosine[:, None, :], sine_part[:, None, :]
    ).astype(jnp.bfloat16)
    value_matrix = projected[:, :, QPK + 1].astype(jnp.bfloat16)
    cache_keys, cache_values = (
        lax.all_gather(key_matrix_rows[:span_rows], "rep", axis=0, tiled=True),
        lax.all_gather(value_matrix[:span_rows], "rep", axis=0, tiled=True),
    )
    key_pos = jnp.arange(cache_keys.shape[0], dtype=jnp.int32)
    allowed = ((key_pos[None, :] <= row_position[:, None]) & (key_pos[None, :] < own_len))[
        None, None
    ]
    scores = pair_scores(query_matrix[:span_rows], cache_keys, score_scale)
    highest = masked_max(scores, allowed)
    exponent = jnp.where(allowed, jnp.exp(scores - highest), 0.0)
    weight_matrix = exponent / jnp.sum(exponent, axis=-1, keepdims=True)
    attended = combine_values(weight_matrix, cache_values)
    prefill_out = attended.astype(jnp.bfloat16).reshape(1, span_rows, heads_here * QPK * HD)
    decode_queries = query_matrix[span_rows:].reshape(2, decode_rows, heads_here, QPK, HD)
    decode_keys = key_matrix_rows[span_rows:].reshape(2, decode_rows, heads_here, HD)
    decode_values = value_matrix[span_rows:].reshape(2, decode_rows, heads_here, HD)
    local_allowed = (
        (sample_ids[None, :] == sample_ids[:, None]) & (step_ids[None, :] <= step_ids[:, None])
    )[None, None]
    near_out = decode_pair(
        decode_queries[0],
        decode_keys[0],
        decode_values[0],
        cache_keys,
        cache_values,
        own_len,
        local_allowed,
        score_scale,
    )
    far_keys, far_values = shifted((cache_keys, cache_values), "grp", half_cycle)
    far_out = decode_pair(
        decode_queries[1],
        decode_keys[1],
        decode_values[1],
        far_keys,
        far_values,
        far_len,
        local_allowed,
        score_scale,
    )
    decode_out = (
        jnp.stack([near_out, far_out])
        .astype(jnp.bfloat16)
        .reshape(1, 1, 2, decode_rows, heads_here * QPK * HD)
    )
    return (prefill_out, decode_out)


MESH = pl.DeviceIdType.MESH
SUBS = 4
GROUPS = QPK // 2 + 1
WIDE = 2 * HD
BROAD = GROUPS - 1
ALL = GROUPS + 1


def fused_kernel(
    len_ref, hidden_ref, decode_ref, aux_ref, w_ref, cos_tab_ref, sin_tab_ref,
    prefill_ref, out_decode_ref, wbuf_ref, land_ref, wnar_ref, landn_ref,
    acc_ref, xh_ref, nv_ref, wt_ref, pb_ref, pbn_ref, cos_ref, sin_ref, q_ref, k_ref, v_ref, m_ref, out_ref,
    wi_s, wo_s, wb_s, wy_s, w_r,
    xa_s, xb_s, xc_s, xd_s, xf_s, x_r,
    p_s, p_r, l_s, t_s, o_s, o_r, o_l,
):
    g = lax.axis_index("grp")
    r = lax.axis_index("rep")
    x = lax.axis_index("tp")
    z = g // 2
    y = g % 2
    hi = z // 2
    zin = z + 1 - 2 * hi
    zout = z - 1 + 2 * hi
    mid = (z == 1) | (z == 2)
    end = (z == 0) | (z == 3)
    mid_count = (z // 2 + z % 2) % 2
    home = r == y
    away = r != y
    span = hidden_ref.shape[1]
    drows = decode_ref.shape[3]
    share = w_ref.shape[0]
    cols = acc_ref.shape[1]
    head = cols // 2
    half = xh_ref.shape[2]
    quarter = half // 2
    rows_all = acc_ref.shape[0]
    sub = span // SUBS
    sides = 4

    barrier = pltpu.get_barrier_semaphore()

    def greet(grp, rep, tp):
        pl.semaphore_signal(
            barrier, inc=1, device_id={"grp": grp, "rep": rep, "tp": tp}, device_id_type=MESH
        )

    pair = 2 * z + 1 - y
    greet(g, 1 - r, x)
    greet(g, r, 1 - x)
    for c in (0, 1):
        greet(pair, c, x)
        greet((g + 4) % 8, c, x)
        greet((g + 4) % 8 + 1 - 2 * y, c, x)
        greet(2 * zin + y, c, x)

    @pl.when(mid)
    def _():
        for c in (0, 1):
            greet(2 * zout + y, c, x)
        pl.semaphore_wait(barrier, 12)

    @pl.when(end)
    def _():
        pl.semaphore_wait(barrier, 10)

    def offset(k, slim=False):
        if slim:
            return (QPK - 2 + k - BROAD) * HD
        return ((k + GROUPS - 1) % GROUPS) * WIDE

    def own_cols(line, h, k, slim=False):
        first = pl.multiple_of(line * cols + h * head + offset(k, slim), 128)
        return w_ref.at[:, pl.ds(first, HD if slim else WIDE)]

    def landing(o, k, h, slim):
        return wnar_ref.at[o, k - BROAD, h] if slim else wbuf_ref.at[o, k, h]

    def remote(src, dst, ssem, rsem, **device):
        return pltpu.make_async_remote_copy(
            src, dst, ssem, rsem, device_id=device, device_id_type=MESH
        )

    def w_copy(o, k, own, kind, slim=False):
        dst = landing(o, k, r, slim)
        src = own_cols(y, r, k, slim) if own else dst
        if kind == 0:
            return remote(src, dst, wi_s.at[o, k], w_r.at[o, k, r], grp=2 * zin + y)
        if kind == 1:
            return remote(src, dst, wo_s.at[o, k], w_r.at[o, k, r], grp=2 * zout + y)
        return remote(src, dst, wb_s.at[o, k], w_r.at[o, k, r], rep=1 - r)

    def w_cross(k, slim=False):
        return remote(own_cols(1 - y, r, k, slim), landing(g, k, r, slim), wy_s.at[k], w_r.at[g, k, r], grp=pair)

    def w_arrived(o, k, h, slim=False):
        where = landing(o, k, h, slim)
        remote(where, where, wb_s.at[o, k], w_r.at[o, k, h], rep=1 - r).wait_recv()

    def own_sends(k, slim=False):
        @pl.when(end)
        def _():
            w_copy(g, k, True, 0, slim).start()

    w_cross(0).start()
    for k in (0, 1):
        w_copy(g, k, True, 0).start()
    w_cross(1).start()

    @pl.when(mid)
    def _():
        for k in range(ALL):
            w_copy(g, k, True, 1, k >= BROAD).start()

    raw = [
        pltpu.make_async_copy(decode_ref.at[0, 0, 1], nv_ref.at[pl.ds(span + drows, drows), :], l_s.at[0]),
        pltpu.make_async_copy(decode_ref.at[0, 0, 0], nv_ref.at[pl.ds(span, drows), :], l_s.at[1]),
        pltpu.make_async_copy(hidden_ref.at[0], nv_ref.at[pl.ds(0, span), :], l_s.at[2]),
    ]
    for copy in raw:
        copy.start()

    gain = aux_ref[:, :hidden_ref.shape[2]]

    def norm(first, n):
        @pl.loop(0, n // 16)
        def _(i):
            rows = pl.ds(pl.multiple_of(first + i * 16, 16), 16)
            wide = nv_ref[rows, :].astype(jnp.float32)
            factor = lax.rsqrt(jnp.mean(wide * wide, axis=-1, keepdims=True) + EPSILON)
            nv_ref[rows, :] = (wide * factor * gain).astype(jnp.bfloat16)

    def place(piece, rr):
        if piece < SUBS:
            return pl.multiple_of(rr * span + piece * sub, 16), sub
        return pl.multiple_of(2 * span + ((piece - SUBS) * 2 + rr) * drows, 16), drows

    def source(piece, k_half, part=None):
        start, n = (piece * sub, sub) if piece < SUBS else (span + (piece - SUBS) * drows, drows)
        if part is None:
            return nv_ref.at[pl.ds(start, n), pl.ds(pl.multiple_of(k_half * half, 128), half)]
        return nv_ref.at[pl.ds(start, n), pl.ds(pl.multiple_of(k_half * half + part * quarter, 128), quarter)]

    def spot(slot, piece, rr):
        start, n = place(piece, rr)
        return xh_ref.at[slot, pl.ds(start, n), :]

    def spot_part(part, piece, rr):
        start, n = place(piece, rr)
        return xh_ref.at[2, pl.ds(start, n), pl.ds(pl.multiple_of(part * quarter, 128), quarter)]

    near_half = hi
    far_half = 1 - hi

    def x_to_home(piece, slot, k_half):
        return remote(source(piece, k_half), spot(slot, piece, r), xa_s.at[slot, piece], x_r.at[slot, piece, r], rep=y)

    def x_local(piece, slot, k_half):
        return pltpu.make_async_copy(source(piece, k_half), spot(slot, piece, r), x_r.at[slot, piece, r])

    def x_to_away(piece):
        slot = jnp.where(mid, x, 0)
        k_half = hi + slot * (1 - 2 * hi)
        return remote(source(piece, k_half), spot(slot, piece, r), xb_s.at[piece], x_r.at[slot, piece, r], grp=pair, rep=y)

    def x_to_mid(piece):
        return remote(
            source(piece, far_half, x), spot_part(x, piece, r), xc_s.at[piece], x_r.at[2 + x, piece, r],
            grp=2 * zin + y, rep=y,
        )

    FAR = SUBS + 1
    NEAR = SUBS
    far_g = (g + 4) % 8

    def far_from_end():
        k_half = far_half + x * (1 - 2 * far_half)
        return remote(source(FAR, k_half), spot(x, FAR, r), xd_s.at[0], x_r.at[x, FAR, r], grp=far_g, rep=y)

    def far_to_end():
        return remote(source(FAR, far_half), spot(0, FAR, r), xd_s.at[0], x_r.at[0, FAR, r], grp=far_g, rep=y)

    def far_to_mid():
        return remote(
            source(FAR, near_half, x), spot_part(x, FAR, r), xd_s.at[1], x_r.at[2 + x, FAR, r],
            grp=2 * zin + y, rep=y,
        )

    def send_piece(piece):
        x_to_away(piece).start()

        @pl.when(end)
        def _():
            x_to_mid(piece).start()

        @pl.when(home)
        def _():
            x_local(piece, 0, near_half).start()

            @pl.when(mid)
            def _():
                x_local(piece, 1, far_half).start()

        @pl.when(away)
        def _():
            x_to_home(piece, 0, near_half).start()

            @pl.when(mid)
            def _():
                x_to_home(piece, 1, far_half).start()

    raw[0].wait()
    norm(span + drows, drows)

    @pl.when(mid)
    def _():
        far_to_end().start()
        far_to_mid().start()

    @pl.when(end)
    def _():
        far_from_end().start()

    @pl.when(mid)
    def _():
        for k in range(2, ALL):
            w_copy(g, k, True, 0, k >= BROAD).start()

    raw[1].wait()
    norm(span, drows)
    send_piece(NEAR)
    raw[2].wait()
    for s in range(SUBS):
        norm(s * sub, sub)
        send_piece(s)
    for k in (2,):
        w_cross(k).start()

    @pl.loop(0, rows_all // 16)
    def _(i):
        acc_ref[pl.ds(pl.multiple_of(i * 16, 16), 16), :] = jnp.zeros((16, cols), jnp.float32)

    across = {"grp": pair}
    beside = {"tp": 1 - x}
    MAIN = [NEAR] + list(range(SUBS))

    def x_forward(slot, piece, rr, way, device):
        where = spot(slot, piece, rr)
        return remote(where, where, xf_s.at[way, slot, piece, rr], x_r.at[slot, piece, rr], **device)

    def part_forward(part, piece, rr, way, device):
        where = spot_part(part, piece, rr)
        return remote(where, where, xf_s.at[way, 2 + part, piece, rr], x_r.at[2 + part, piece, rr], **device)

    def arrived(make, slot, piece, rr):
        make(slot, piece, rr, 0, {"rep": 1 - r}).wait_recv()

    def relay(make, slot, piece, ways):
        for rr in (0, 1):
            arrived(make, slot, piece, rr)
            for way in ways:
                make(slot, piece, rr, way, (across, beside)[way]).start()

    def settle(make, slot, piece, ways):
        for rr in (0, 1):
            for way in ways:
                make(slot, piece, rr, way, (across, beside)[way]).wait_send()

    EARLY = MAIN[:3]
    LATER = MAIN[3:]

    def forward_early(act):
        @pl.when(home & end)
        def _():
            act(x_forward, 0, FAR, (0,))

        @pl.when(home & mid)
        def _():
            act(x_forward, x, FAR, (0, 1))
            for piece in [FAR] + EARLY:
                act(part_forward, x, piece, (0, 1))

        @pl.when(away & mid)
        def _():
            for piece in EARLY:
                act(x_forward, x, piece, (1,))

    def forward_first(act):
        @pl.when(home & mid)
        def _():
            for piece in LATER:
                act(part_forward, x, piece, (0, 1))

        @pl.when(away & mid)
        def _():
            for piece in LATER[:-1]:
                act(x_forward, x, piece, (1,))

    def forward_late(act):
        @pl.when(away & mid)
        def _():
            act(x_forward, x, LATER[-1], (1,))
            act(x_forward, x, FAR, (1,))

    def forward_part(act, pieces):
        @pl.when(away & mid)
        def _():
            for piece in pieces:
                act(part_forward, x, piece, (1,))

    def wait_x():
        @pl.when(home)
        def _():
            def both(slot, k_half):
                for piece in MAIN:
                    x_local(piece, slot, k_half).wait()
                    arrived(x_forward, slot, piece, 1 - r)

            both(0, near_half)

            @pl.when(mid)
            def _():
                both(1, far_half)
                for rr in (0, 1):
                    arrived(x_forward, 1 - x, FAR, rr)

        @pl.when(away)
        def _():
            slot = jnp.where(mid, 1 - x, 0)
            for piece in MAIN + [FAR]:
                for rr in (0, 1):
                    arrived(x_forward, slot, piece, rr)

    def wait_part():
        @pl.when(mid)
        def _():
            for piece in MAIN + [FAR]:
                for rr in (0, 1):
                    arrived(part_forward, 1 - x, piece, rr)

    def pass_w(k, slim=False, first=True, second=True):
        def outer(yy):
            o = 2 * zout + yy
            w_arrived(o, k, r, slim)
            w_copy(o, k, False, 0, slim).start()
            w_copy(o, k, False, 2, slim).start()

        if first:
            @pl.when(mid)
            def _():
                outer(y)

            w_arrived(pair, k, r, slim)
            w_copy(pair, k, False, 0, slim).start()

            @pl.when(mid)
            def _():
                w_copy(pair, k, False, 1, slim).start()

            w_copy(pair, k, False, 2, slim).start()

        if second:
            @pl.when(mid)
            def _():
                outer(1 - y)

    def take_w(k, slim=False):
        def over(layer):
            for yy in (y, 1 - y):
                o = 2 * layer + yy
                w_arrived(o, k, r, slim)
                w_copy(o, k, False, 2, slim).start()

        over(zin)

        @pl.when(mid)
        def _():
            over(zin + 1 - 2 * hi)
            for yy in (0, 1):
                w_arrived(2 * zout + yy, k, 1 - r, slim)
            for i in range(sides):
                w_arrived(sides * (1 - hi) + i, k, 1 - r, slim)

        @pl.when(end)
        def _():
            for yy in (0, 1):
                w_arrived(2 * zin + yy, k, 1 - r, slim)

        w_arrived(pair, k, 1 - r, slim)

    def p_copy(k, slim=False):
        if slim:
            src, dst = pbn_ref.at[k - BROAD], landn_ref.at[k - BROAD]
        else:
            src, dst = pb_ref.at[k], land_ref.at[k]
        return remote(src, dst, p_s.at[k], p_r.at[k], grp=2 * zout + y)

    def tile(slot, i, h, slim):
        rows = pl.ds(i * share, share)
        return wt_ref.at[slot, rows, pl.ds(h * HD, HD)] if slim else wt_ref.at[slot, rows, :]

    def fetch(k, base, h, slot, slim):
        heads = (0, 1) if slim else (h,)
        for i in range(sides):
            o = base + i
            for c, hh in enumerate(heads):
                dst = tile(slot, i, c, slim)

                @pl.when(o == g)
                def _():
                    pltpu.make_async_copy(own_cols(y, hh, k, slim), dst, t_s.at[slot, i, c]).start()

                @pl.when(o != g)
                def _():
                    pltpu.make_async_copy(landing(o, k, hh, slim), dst, t_s.at[slot, i, c]).start()

    def fetched(slot, slim):
        for i in range(sides):
            for c in range(2 if slim else 1):
                dst = tile(slot, i, c, slim)
                pltpu.make_async_copy(dst, dst, t_s.at[slot, i, c]).wait()

    far_base = sides * (1 - hi)
    near_base = sides * hi

    def compute(k, slim=False):
        per = 1 if slim else 2
        steps = 2 * per

        @pl.when(mid)
        def _():
            fetch(k, far_base, 0, 0, slim)

        @pl.when(end)
        def _():
            fetch(k, near_base, 0, per % 2, slim)

        @pl.loop(0, steps)
        def _(j):
            slot = j % 2
            n = j + 1

            @pl.when((j >= per) | mid)
            def _():
                @pl.when(n < steps)
                def _():
                    side = n // per
                    fetch(k, far_base + side * (near_base - far_base), n % per, n % 2, slim)

                fetched(slot, slim)
                product = jnp.dot(xh_ref[1 - j // per], wt_ref[slot], preferred_element_type=jnp.float32)
                if slim:
                    for h in (0, 1):
                        at = pl.ds(pl.multiple_of(h * head + offset(k, slim), 128), HD)
                        acc_ref[:, at] += product[:, h * HD:(h + 1) * HD]
                else:
                    acc_ref[:, pl.ds(pl.multiple_of((j % 2) * head + offset(k), 128), WIDE)] += product

    def partial(k, slim=False):
        per = 1 if slim else 2
        fetch(k, far_base, 0, 0, slim)

        @pl.loop(0, per)
        def _(j):
            @pl.when(j + 1 < per)
            def _():
                fetch(k, far_base, 1, 1, slim)

            fetched(j, slim)
            value = jnp.dot(xh_ref[2], wt_ref[j], preferred_element_type=jnp.float32).astype(jnp.bfloat16)
            if slim:
                pbn_ref[k - BROAD] = value
            else:
                pb_ref[k, :, pl.ds(pl.multiple_of(j * WIDE, 128), WIDE)] = value

        p_copy(k, slim).start()

    def add_partial(k, slim=False):
        w = HD if slim else WIDE
        if slim:
            src, dst = landn_ref.at[k - BROAD], pbn_ref.at[0]
        else:
            src, dst = land_ref.at[k], pb_ref.at[0]
        remote(dst, src, p_s.at[k], p_r.at[k], grp=2 * zin + y).wait_recv()
        take = pltpu.make_async_copy(src, dst, l_s.at[3])
        take.start()
        take.wait()

        @pl.loop(0, rows_all // 16)
        def _(i):
            rows = pl.ds(pl.multiple_of(i * 16, 16), 16)
            for h in (0, 1):
                place_h = pl.ds(pl.multiple_of(h * head + offset(k, slim), 128), w)
                value = pbn_ref[0, rows, h * w:(h + 1) * w] if slim else pb_ref[0, rows, h * w:(h + 1) * w]
                acc_ref[rows, place_h] += value.astype(jnp.float32)

    prompt = g - y + r
    prompt_rows = 2 * span
    valid = len_ref[prompt]
    block = 256 if prompt_rows % 256 == 0 else prompt_rows
    blocks = [(prompt_rows, rows_all - prompt_rows, rows_all)]
    blocks += [(start, block, start + block) for start in range(0, prompt_rows, block)]
    starts = (0, prompt_rows, prompt_rows + 2 * drows)
    sizes = (span, drows, drows)
    width = QPK * HD

    def mask_place(index):
        top = 0
        for start, size, keys in blocks[:index]:
            top += size
        return slice(top, top + blocks[index][1]), slice(0, blocks[index][2])

    def make_tables():
        step = lax.broadcasted_iota(jnp.int32, (rows_all - prompt_rows, HD), 0) % STEPS
        for table, out in ((cos_tab_ref, cos_ref), (sin_tab_ref, sin_ref)):
            out[:prompt_rows, :] = table[:prompt_rows, :]
            picked = jnp.zeros((rows_all - prompt_rows, HD), jnp.float32)
            for i in range(STEPS):
                picked = jnp.where(step == i, table[pl.ds(valid + i, 1), :], picked)
            out[prompt_rows:, :] = picked

    def make_masks():
        for index, (start, size, keys) in enumerate(blocks):
            shape = (size, keys)
            row = lax.broadcasted_iota(jnp.int32, shape, 0) + start
            col = lax.broadcasted_iota(jnp.int32, shape, 1)
            if start < prompt_rows:
                allowed = (col <= row) & (col < valid)
            else:
                same = ((row - prompt_rows) // STEPS == (col - prompt_rows) // STEPS) & (col <= row)
                allowed = (col < jnp.minimum(valid, prompt_rows)) | ((col >= prompt_rows) & same)
            m_ref[mask_place(index)] = jnp.where(allowed, 0.0, NEGATIVE)

    def target(f, h, c, line, slim):
        at = pl.ds(pl.multiple_of((line * 2 + h) * width + offset(f, slim), 128), HD if slim else WIDE)
        return (prefill_ref.at[0, :, at], out_decode_ref.at[0, 0, 0, :, at], out_decode_ref.at[0, 0, 1, :, at])[c]

    def out_piece(f, h, c, rr, slim):
        start = pl.multiple_of(starts[c] + rr * sizes[c], 16)
        rows = pl.ds(start, sizes[c])
        if slim:
            return out_ref.at[BROAD - 1, h, rows, pl.ds(pl.multiple_of((f - BROAD) * HD, 128), HD)]
        return out_ref.at[f - 1, h, rows, :]

    def out_send(f, h, c, rr, slim):
        grp = (prompt + 4) % 8 if c == 2 else prompt
        return remote(
            out_piece(f, h, c, rr, slim), target(f, h, c, y, slim), o_s.at[f - 1, h, c, rr], o_r.at[f - 1, h, c, y],
            grp=grp, rep=rr,
        )

    def out_keep(f, h, c, slim):
        return pltpu.make_async_copy(out_piece(f, h, c, r, slim), target(f, h, c, y, slim), o_l.at[f - 1, h, c])

    def out_receive(f, h, c, line, slim):
        remote(
            out_piece(f, h, c, 0, slim), target(f, h, c, line, slim), o_s.at[f - 1, h, c, 0],
            o_r.at[f - 1, h, c, line], rep=1 - r,
        ).wait_recv()

    def each_out(f, h, c, act, keep_act, slim):
        if c == 2:
            act(out_send(f, h, c, 0, slim))
            act(out_send(f, h, c, 1, slim))
            return

        @pl.when(home)
        def _():
            keep_act(out_keep(f, h, c, slim))
            act(out_send(f, h, c, 1 - r, slim))

        @pl.when(away)
        def _():
            act(out_send(f, h, c, 0, slim))
            act(out_send(f, h, c, 1, slim))

    def begin(copy):
        copy.start()

    def sent(copy):
        copy.wait_send()

    def kept(copy):
        copy.wait()

    factor = HD ** (-0.5) * math.log2(math.e)

    def part(h, first):
        at = pl.ds(pl.multiple_of(h * head + first, 128), HD)
        bias_at = pl.ds(pl.multiple_of(hidden_ref.shape[2] + y * cols + h * head + first, 128), HD)
        return acc_ref[:, at] + aux_ref[:, bias_at]

    def turned(v):
        return v * cos_ref[...] + pltpu.roll(v, HD // 2, 1) * sin_ref[...]

    def keys_values():
        for h in (0, 1):
            k_ref[h] = turned(part(h, QPK * HD)).astype(jnp.bfloat16)
            v_ref[h] = part(h, (QPK + 1) * HD).astype(jnp.bfloat16)

    def attend(f, slim=False):
        here = (0,) if slim else (0, 1)

        @pl.loop(0, 2)
        def _(h):
            for j in here:
                q_ref[j] = (turned(part(h, offset(f, slim) + j * HD)) * factor).astype(jnp.bfloat16)
            for index, (start, size, keys) in enumerate(blocks):
                for j in here:
                    s = lax.dot_general(
                        q_ref[j, start:start + size, :], k_ref[h, :keys, :], (((1,), (1,)), ((), ())),
                        preferred_element_type=jnp.float32,
                    ) + m_ref[mask_place(index)]
                    top = jnp.max(s, axis=-1, keepdims=True)
                    p = jnp.exp2(s - top)
                    total = jnp.sum(p, axis=-1, keepdims=True)
                    o = jnp.dot(p.astype(jnp.bfloat16), v_ref[h, :keys, :], preferred_element_type=jnp.float32)
                    o = (o / total).astype(jnp.bfloat16)
                    if slim:
                        out_ref[BROAD - 1, h, start:start + size, pl.ds(pl.multiple_of((f - BROAD) * HD, 128), HD)] = o
                    else:
                        out_ref[f - 1, h, start:start + size, j * HD:(j + 1) * HD] = o
                if index == 0:
                    each_out(f, h, 2, begin, begin, slim)
                    each_out(f, h, 1, begin, begin, slim)
            each_out(f, h, 0, begin, begin, slim)

    @pl.loop(0, BROAD + 6)
    def _(t):
        k = t - 2

        @pl.when(t < BROAD)
        def _():
            pass_w(t, second=False)

        @pl.when(t == 0)
        def _():
            forward_early(relay)

        @pl.when(t < BROAD)
        def _():
            pass_w(t, first=False)

        @pl.when(t < BROAD - 2)
        def _():
            own_sends(t + 2)

        @pl.when((t >= BROAD - 2) & (t < BROAD))
        def _():
            own_sends(t + 2, True)

        @pl.when(t == 0)
        def _():
            forward_first(relay)
            for kk in range(3, ALL):
                w_cross(kk, kk >= BROAD).start()
            make_masks()
            make_tables()

        @pl.when(t == 1)
        def _():
            forward_late(relay)

        @pl.when(t == 2)
        def _():
            wait_x()

        @pl.when(t == 3)
        def _():
            forward_part(relay, [FAR] + EARLY)

        @pl.when((k >= 0) & (k < BROAD))
        def _():
            take_w(k)

            @pl.when(mid & ((home & (t == 3)) | (away & (t == 4))))
            def _():
                wait_part()

            @pl.loop(0, BROAD)
            def _(kk):
                due = (home & ((t == 3) & (kk <= k) | (t > 3) & (kk == k))) | (away & ((t == 4) & (kk <= k) | (t > 4) & (kk == k)))

                @pl.when(mid & due)
                def _():
                    partial(kk)

            compute(k)

        @pl.when((k >= BROAD) & (k < ALL))
        def _():
            take_w(k, True)

            @pl.when(mid)
            def _():
                partial(k, True)

            compute(k, True)

        @pl.when(t == 3)
        def _():
            forward_part(relay, LATER)

        f = t - 4 + 2 * mid_count

        @pl.when(end & (f >= 0) & (f < BROAD))
        def _():
            add_partial(f)

        @pl.when(end & (f >= BROAD) & (f < ALL))
        def _():
            add_partial(f, True)

        @pl.when(f == 0)
        def _():
            keys_values()

        @pl.when((f > 0) & (f < BROAD))
        def _():
            attend(f)

        @pl.when((f >= BROAD) & (f < ALL))
        def _():
            attend(f, True)

        @pl.when(t == 3)
        def _():
            pass_w(BROAD, True)

        @pl.when(((t == 3) & end) | ((t == 4) & mid))
        def _():
            pass_w(BROAD + 1, True)

    def close_out(f, slim):
        for h in (0, 1):
            for c in range(3):
                each_out(f, h, c, sent, kept, slim)
                if c == 2:
                    out_receive(f, h, c, 0, slim)
                    out_receive(f, h, c, 1, slim)
                else:
                    out_receive(f, h, c, 1 - y, slim)

                    @pl.when(away)
                    def _():
                        out_receive(f, h, c, y, slim)

    @pl.loop(1, BROAD)
    def _(f):
        close_out(f, False)

    @pl.loop(BROAD, ALL)
    def _(f):
        close_out(f, True)

    @pl.when(mid)
    def _():
        for k in range(ALL):
            p_copy(k, k >= BROAD).wait_send()

    @pl.when(mid)
    def _():
        far_to_end().wait_send()
        far_to_mid().wait_send()

    @pl.when(end)
    def _():
        far_from_end().wait_send()

    for piece in [NEAR] + list(range(SUBS)):
        x_to_away(piece).wait_send()

        @pl.when(end)
        def _():
            x_to_mid(piece).wait_send()

        @pl.when(away)
        def _():
            x_to_home(piece, 0, near_half).wait_send()

            @pl.when(mid)
            def _():
                x_to_home(piece, 1, far_half).wait_send()

    forward_early(settle)
    forward_first(settle)
    forward_late(settle)
    forward_part(settle, [FAR] + MAIN)

    def close_w(k, slim):
        w_cross(k, slim).wait_send()
        for o in (g, pair):
            w_copy(o, k, False, 0, slim).wait_send()

            @pl.when(mid)
            def _():
                w_copy(o, k, False, 1, slim).wait_send()

        w_copy(pair, k, False, 2, slim).wait_send()

        @pl.when(mid)
        def _():
            for yy in (0, 1):
                w_copy(2 * zout + yy, k, False, 0, slim).wait_send()
                w_copy(2 * zout + yy, k, False, 2, slim).wait_send()
            for i in range(sides):
                w_copy(sides * (1 - hi) + i, k, False, 2, slim).wait_send()

        @pl.when(end)
        def _():
            for yy in (0, 1):
                w_copy(2 * zin + yy, k, False, 2, slim).wait_send()

    @pl.loop(0, BROAD)
    def _(k):
        close_w(k, False)

    @pl.loop(BROAD, ALL)
    def _(k):
        close_w(k, True)


def rope_rows(count):
    half_size = HD // 2
    frequency = np.float32(THETA) ** (-(np.arange(half_size, dtype=np.float32) * np.float32(2.0) / np.float32(HD)))
    angle = np.arange(count, dtype=np.float32)[:, None] * frequency.astype(np.float32)[None, :]
    cosine, sine = np.cos(angle), np.sin(angle)
    return np.concatenate([cosine, cosine], axis=-1), np.concatenate([-sine, sine], axis=-1)


def fused(hidden, decode_hidden, norm_gain, qkv_weight, qkv_bias, lengths):
    count = lax.axis_size("grp")
    own_rows = hidden.shape[1] + 2 * decode_hidden.shape[3]
    rows = 2 * own_rows
    positions = 2 * hidden.shape[1] + STEPS
    cosine, sine = rope_rows(positions + (-positions) % 8)
    aux = jnp.concatenate([norm_gain, qkv_bias]).astype(jnp.float32).reshape(1, -1)
    share = qkv_weight.shape[0]
    width = hidden.shape[2]
    cols = qkv_weight.shape[1] // 2
    out_width = 4 * QPK * HD
    pieces = SUBS + 2
    hbm = pl.BlockSpec(memory_space=pl.ANY)
    vmem = pl.BlockSpec(memory_space=pltpu.VMEM)
    smem = pl.BlockSpec(memory_space=pltpu.SMEM)
    dma = pltpu.SemaphoreType.DMA
    outs = BROAD
    return pl.pallas_call(
        fused_kernel,
        out_shape=(
            jax.ShapeDtypeStruct(hidden.shape[:2] + (out_width,), jnp.bfloat16),
            jax.ShapeDtypeStruct(decode_hidden.shape[:4] + (out_width,), jnp.bfloat16),
            jax.ShapeDtypeStruct((count, BROAD, 2, share, WIDE), jnp.bfloat16),
            jax.ShapeDtypeStruct((BROAD, rows, 2 * WIDE), jnp.bfloat16),
            jax.ShapeDtypeStruct((count, 2, 2, share, HD), jnp.bfloat16),
            jax.ShapeDtypeStruct((2, rows, WIDE), jnp.bfloat16),
        ),
        in_specs=[smem, hbm, hbm, vmem, hbm, vmem, vmem],
        out_specs=(hbm,) * 6,
        scratch_shapes=[
            pltpu.VMEM((rows, cols), jnp.float32),
            pltpu.VMEM((3, rows, width // 2), jnp.bfloat16),
            pltpu.VMEM((own_rows, width), jnp.bfloat16),
            pltpu.VMEM((2, width // 2, WIDE), jnp.bfloat16),
            pltpu.VMEM((BROAD, rows, 2 * WIDE), jnp.bfloat16),
            pltpu.VMEM((2, rows, WIDE), jnp.bfloat16),
            pltpu.VMEM((rows, HD), jnp.float32),
            pltpu.VMEM((rows, HD), jnp.float32),
            pltpu.VMEM((2, rows, HD), jnp.bfloat16),
            pltpu.VMEM((2, rows, HD), jnp.bfloat16),
            pltpu.VMEM((2, rows, HD), jnp.bfloat16),
            pltpu.VMEM((rows, rows), jnp.float32),
            pltpu.VMEM((outs, 2, rows, WIDE), jnp.bfloat16),
            dma((count, ALL)), dma((count, ALL)), dma((count, ALL)), dma((ALL,)),
            dma((count, ALL, 2)),
            dma((2, SUBS + 1)), dma((SUBS + 1,)), dma((SUBS + 1,)), dma((2,)),
            dma((2, 4, pieces, 2)), dma((4, pieces, 2)),
            dma((ALL,)), dma((ALL,)), dma((4,)), dma((2, 4, 2)),
            dma((GROUPS, 2, 3, 2)), dma((GROUPS, 2, 3, 2)), dma((GROUPS, 2, 3)),
        ],
        compiler_params=pltpu.CompilerParams(
            collective_id=0, has_side_effects=True, vmem_limit_bytes=60 << 20
        ),
        name="fused",
    )(lengths, hidden, decode_hidden, aux, qkv_weight, jnp.asarray(cosine), jnp.asarray(sine))[:2]


def on_device(hidden, decode_hidden, norm_gain, qkv_weight, qkv_bias, lengths):
    count = lax.axis_size("grp")
    reps = lax.axis_size("rep")
    head_block = (QPK + 2) * HD
    heads_here = qkv_bias.shape[0] // head_block
    if reps != 2 or count != 8 or lax.axis_size("tp") != 2 or heads_here != 4 or decode_hidden.shape[1] != 1:
        return plain_device(hidden, decode_hidden, norm_gain, qkv_weight, qkv_bias, lengths)
    return fused(hidden, decode_hidden, norm_gain, qkv_weight, qkv_bias, lengths)


def solution(mesh):
    return jax.shard_map(
        on_device,
        mesh=mesh,
        in_specs=(
            P("grp", "rep", None),
            P("grp", "rep", None, None, None),
            P(),
            P("grp", "tp"),
            P("tp"),
            P(),
        ),
        out_specs=(P("grp", "rep", "tp"), P("grp", "rep", None, None, "tp")),
        check_vma=False,
    )
```

```python
import jax
import jax.numpy as jnp
from jax import lax
from jax.experimental import pallas as pl
from jax.experimental.pallas import tpu as pltpu
from jax.sharding import PartitionSpec as P
import functools
import math
import numpy as np

HD = 128
QPK = 8
STEPS = 4


THETA = 1000000.0
EPSILON = 1e-06
NEGATIVE = -1e30


def shifted(block, axis, distance):
    devices = range(lax.axis_size(axis))
    route = [((i - distance) % len(devices), i) for i in devices]
    return lax.ppermute(block, axis, route)


def normalize(row_block, gain_row):
    widened = row_block.astype(jnp.float32)
    factor = lax.rsqrt(jnp.mean(widened * widened, axis=-1, keepdims=True) + EPSILON)
    return (widened * factor * gain_row.astype(jnp.float32)).astype(jnp.bfloat16)


def rope_tables(positions, head_size):
    half_size = head_size // 2
    frequency = THETA ** (-(jnp.arange(half_size, dtype=jnp.float32) * 2.0 / head_size))
    angle = positions.astype(jnp.float32)[:, None] * frequency[None, :]
    return (jnp.cos(angle), jnp.sin(angle))


def rotate(vector, cosine, sine_part):
    half_size = vector.shape[-1] // 2
    first_half = vector[..., :half_size]
    second = vector[..., half_size:]
    return jnp.concatenate(
        [first_half * cosine - second * sine_part, second * cosine + first_half * sine_part],
        axis=-1,
    )


def masked_max(scores, allowed):
    return jnp.max(jnp.where(allowed, scores, NEGATIVE), axis=-1, keepdims=True)


def combine_values(weight_matrix, value_matrix):
    return jnp.einsum(
        "aprk,kaz->rapz",
        weight_matrix.astype(jnp.bfloat16),
        value_matrix,
        preferred_element_type=jnp.float32,
    )


def pair_scores(query_matrix, key_matrix_rows, score_scale):
    return (
        jnp.einsum(
            "wjro,ujo->jrwu", query_matrix, key_matrix_rows, preferred_element_type=jnp.float32
        )
        * score_scale
    )


def decode_pair(
    query_matrix,
    own_keys,
    own_values,
    prompt_keys,
    prompt_values,
    valid_len,
    local_allowed,
    score_scale,
):
    key_slot_index = jnp.arange(prompt_keys.shape[0], dtype=jnp.int32)
    prompt_allowed = (key_slot_index < valid_len)[None, None, None, :]
    far_scores = pair_scores(query_matrix, prompt_keys, score_scale)
    near_scores = pair_scores(query_matrix, own_keys, score_scale)
    highest = jnp.maximum(
        masked_max(far_scores, prompt_allowed), masked_max(near_scores, local_allowed)
    )
    far_exp = jnp.where(prompt_allowed, jnp.exp(far_scores - highest), 0.0)
    near_exp = jnp.where(local_allowed, jnp.exp(near_scores - highest), 0.0)
    running = jnp.sum(far_exp, axis=-1, keepdims=True) + jnp.sum(near_exp, axis=-1, keepdims=True)
    return combine_values(far_exp / running, prompt_values) + combine_values(
        near_exp / running, own_values
    )


def plain_device(hidden, decode_hidden, norm_gain, qkv_weight, qkv_bias, lengths):
    prompt_count = lax.axis_size("grp")
    rep_count = lax.axis_size("rep")
    half_cycle = prompt_count // 2
    grp_here = lax.axis_index("grp")
    rep_here = lax.axis_index("rep")
    span_rows = hidden.shape[1]
    model_width = hidden.shape[2]
    head_block = (QPK + 2) * HD
    heads_here = qkv_bias.shape[0] // head_block
    decode_rows = decode_hidden.shape[3]
    score_scale = HD ** (-0.5)
    prefill_normed = normalize(hidden[0], norm_gain)
    decode_normed = normalize(decode_hidden.reshape(2 * decode_rows, model_width), norm_gain)
    normed = jnp.concatenate([prefill_normed, decode_normed], axis=0)
    share_cols = qkv_weight.shape[1] // rep_count
    own_cols = lax.dynamic_slice_in_dim(qkv_weight, rep_here * share_cols, share_cols, 1)
    columns = lax.all_gather(own_cols, "grp", axis=0, tiled=True)
    complete = lax.all_gather(columns, "rep", axis=1, tiled=True)
    projected = jnp.dot(normed, complete, preferred_element_type=jnp.float32)
    projected = (projected + qkv_bias.astype(jnp.float32)).reshape(
        normed.shape[0], heads_here, QPK + 2, HD
    )
    index_table = jnp.arange(prompt_count, dtype=jnp.int32)

    def length_of(prompt):
        return jnp.sum(jnp.where(index_table == prompt, lengths, 0))

    own_len = length_of(grp_here)
    far_len = length_of((grp_here + half_cycle) % prompt_count)
    row_position = rep_here * span_rows + jnp.arange(span_rows, dtype=jnp.int32)
    local_ids = jnp.arange(decode_rows, dtype=jnp.int32)
    step_ids = local_ids % STEPS
    sample_ids = local_ids // STEPS
    positions = jnp.concatenate([row_position, own_len + step_ids, far_len + step_ids])
    cosine, sine_part = rope_tables(positions, HD)
    query_matrix = rotate(
        projected[:, :, :QPK], cosine[:, None, None, :], sine_part[:, None, None, :]
    ).astype(jnp.bfloat16)
    key_matrix_rows = rotate(
        projected[:, :, QPK], cosine[:, None, :], sine_part[:, None, :]
    ).astype(jnp.bfloat16)
    value_matrix = projected[:, :, QPK + 1].astype(jnp.bfloat16)
    cache_keys, cache_values = (
        lax.all_gather(key_matrix_rows[:span_rows], "rep", axis=0, tiled=True),
        lax.all_gather(value_matrix[:span_rows], "rep", axis=0, tiled=True),
    )
    key_pos = jnp.arange(cache_keys.shape[0], dtype=jnp.int32)
    allowed = ((key_pos[None, :] <= row_position[:, None]) & (key_pos[None, :] < own_len))[
        None, None
    ]
    scores = pair_scores(query_matrix[:span_rows], cache_keys, score_scale)
    highest = masked_max(scores, allowed)
    exponent = jnp.where(allowed, jnp.exp(scores - highest), 0.0)
    weight_matrix = exponent / jnp.sum(exponent, axis=-1, keepdims=True)
    attended = combine_values(weight_matrix, cache_values)
    prefill_out = attended.astype(jnp.bfloat16).reshape(1, span_rows, heads_here * QPK * HD)
    decode_queries = query_matrix[span_rows:].reshape(2, decode_rows, heads_here, QPK, HD)
    decode_keys = key_matrix_rows[span_rows:].reshape(2, decode_rows, heads_here, HD)
    decode_values = value_matrix[span_rows:].reshape(2, decode_rows, heads_here, HD)
    local_allowed = (
        (sample_ids[None, :] == sample_ids[:, None]) & (step_ids[None, :] <= step_ids[:, None])
    )[None, None]
    near_out = decode_pair(
        decode_queries[0],
        decode_keys[0],
        decode_values[0],
        cache_keys,
        cache_values,
        own_len,
        local_allowed,
        score_scale,
    )
    far_keys, far_values = shifted((cache_keys, cache_values), "grp", half_cycle)
    far_out = decode_pair(
        decode_queries[1],
        decode_keys[1],
        decode_values[1],
        far_keys,
        far_values,
        far_len,
        local_allowed,
        score_scale,
    )
    decode_out = (
        jnp.stack([near_out, far_out])
        .astype(jnp.bfloat16)
        .reshape(1, 1, 2, decode_rows, heads_here * QPK * HD)
    )
    return (prefill_out, decode_out)


MESH = pl.DeviceIdType.MESH
SUBS = 4
GROUPS = QPK // 2 + 1
WIDE = 2 * HD
BROAD = GROUPS - 1
ALL = GROUPS + 1


def fused_kernel(
    len_ref, hidden_ref, decode_ref, aux_ref, w_ref, cos_tab_ref, sin_tab_ref,
    prefill_ref, out_decode_ref, wbuf_ref, land_ref, wnar_ref, landn_ref,
    acc_ref, xh_ref, nv_ref, wt_ref, pb_ref, pbn_ref, cos_ref, sin_ref, q_ref, k_ref, v_ref, m_ref, out_ref,
    wi_s, wo_s, wb_s, wy_s, w_r,
    xa_s, xb_s, xc_s, xd_s, xf_s, x_r,
    p_s, p_r, l_s, t_s, o_s, o_r, o_l,
):
    g = lax.axis_index("grp")
    r = lax.axis_index("rep")
    x = lax.axis_index("tp")
    z = g // 2
    y = g % 2
    hi = z // 2
    zin = z + 1 - 2 * hi
    zout = z - 1 + 2 * hi
    mid = (z == 1) | (z == 2)
    end = (z == 0) | (z == 3)
    mid_count = (z // 2 + z % 2) % 2
    home = r == y
    away = r != y
    span = hidden_ref.shape[1]
    drows = decode_ref.shape[3]
    share = w_ref.shape[0]
    cols = acc_ref.shape[1]
    head = cols // 2
    half = xh_ref.shape[2]
    quarter = half // 2
    rows_all = acc_ref.shape[0]
    sub = span // SUBS
    sides = 4

    barrier = pltpu.get_barrier_semaphore()

    def greet(grp, rep, tp):
        pl.semaphore_signal(
            barrier, inc=1, device_id={"grp": grp, "rep": rep, "tp": tp}, device_id_type=MESH
        )

    pair = 2 * z + 1 - y
    greet(g, 1 - r, x)
    greet(g, r, 1 - x)
    for c in (0, 1):
        greet(pair, c, x)
        greet((g + 4) % 8, c, x)
        greet((g + 4) % 8 + 1 - 2 * y, c, x)
        greet(2 * zin + y, c, x)

    @pl.when(mid)
    def _():
        for c in (0, 1):
            greet(2 * zout + y, c, x)
        pl.semaphore_wait(barrier, 12)

    @pl.when(end)
    def _():
        pl.semaphore_wait(barrier, 10)

    def offset(k, slim=False):
        if slim:
            return (QPK - 2 + k - BROAD) * HD
        return ((k + GROUPS - 1) % GROUPS) * WIDE

    def own_cols(line, h, k, slim=False):
        first = pl.multiple_of(line * cols + h * head + offset(k, slim), 128)
        return w_ref.at[:, pl.ds(first, HD if slim else WIDE)]

    def landing(o, k, h, slim):
        return wnar_ref.at[o, k - BROAD, h] if slim else wbuf_ref.at[o, k, h]

    def remote(src, dst, ssem, rsem, **device):
        return pltpu.make_async_remote_copy(
            src, dst, ssem, rsem, device_id=device, device_id_type=MESH
        )

    def w_copy(o, k, own, kind, slim=False):
        dst = landing(o, k, r, slim)
        src = own_cols(y, r, k, slim) if own else dst
        if kind == 0:
            return remote(src, dst, wi_s.at[o, k], w_r.at[o, k, r], grp=2 * zin + y)
        if kind == 1:
            return remote(src, dst, wo_s.at[o, k], w_r.at[o, k, r], grp=2 * zout + y)
        return remote(src, dst, wb_s.at[o, k], w_r.at[o, k, r], rep=1 - r)

    def w_cross(k, slim=False):
        return remote(own_cols(1 - y, r, k, slim), landing(g, k, r, slim), wy_s.at[k], w_r.at[g, k, r], grp=pair)

    def w_arrived(o, k, h, slim=False):
        where = landing(o, k, h, slim)
        remote(where, where, wb_s.at[o, k], w_r.at[o, k, h], rep=1 - r).wait_recv()

    def own_sends(k, slim=False):
        @pl.when(end)
        def _():
            w_copy(g, k, True, 0, slim).start()

    w_cross(0).start()
    for k in (0, 1):
        w_copy(g, k, True, 0).start()
    w_cross(1).start()

    @pl.when(mid)
    def _():
        for k in range(ALL):
            w_copy(g, k, True, 1, k >= BROAD).start()

    raw = [
        pltpu.make_async_copy(decode_ref.at[0, 0, 1], nv_ref.at[pl.ds(span + drows, drows), :], l_s.at[0]),
        pltpu.make_async_copy(decode_ref.at[0, 0, 0], nv_ref.at[pl.ds(span, drows), :], l_s.at[1]),
        pltpu.make_async_copy(hidden_ref.at[0], nv_ref.at[pl.ds(0, span), :], l_s.at[2]),
    ]
    for copy in raw:
        copy.start()

    gain = aux_ref[:, :hidden_ref.shape[2]]

    def norm(first, n):
        @pl.loop(0, n // 16)
        def _(i):
            rows = pl.ds(pl.multiple_of(first + i * 16, 16), 16)
            wide = nv_ref[rows, :].astype(jnp.float32)
            factor = lax.rsqrt(jnp.mean(wide * wide, axis=-1, keepdims=True) + EPSILON)
            nv_ref[rows, :] = (wide * factor * gain).astype(jnp.bfloat16)

    def place(piece, rr):
        if piece < SUBS:
            return pl.multiple_of(rr * span + piece * sub, 16), sub
        return pl.multiple_of(2 * span + ((piece - SUBS) * 2 + rr) * drows, 16), drows

    def source(piece, k_half, part=None):
        start, n = (piece * sub, sub) if piece < SUBS else (span + (piece - SUBS) * drows, drows)
        if part is None:
            return nv_ref.at[pl.ds(start, n), pl.ds(pl.multiple_of(k_half * half, 128), half)]
        return nv_ref.at[pl.ds(start, n), pl.ds(pl.multiple_of(k_half * half + part * quarter, 128), quarter)]

    def spot(slot, piece, rr):
        start, n = place(piece, rr)
        return xh_ref.at[slot, pl.ds(start, n), :]

    def spot_part(part, piece, rr):
        start, n = place(piece, rr)
        return xh_ref.at[2, pl.ds(start, n), pl.ds(pl.multiple_of(part * quarter, 128), quarter)]

    near_half = hi
    far_half = 1 - hi

    def x_to_home(piece, slot, k_half):
        return remote(source(piece, k_half), spot(slot, piece, r), xa_s.at[slot, piece], x_r.at[slot, piece, r], rep=y)

    def x_local(piece, slot, k_half):
        return pltpu.make_async_copy(source(piece, k_half), spot(slot, piece, r), x_r.at[slot, piece, r])

    def x_to_away(piece):
        slot = jnp.where(mid, x, 0)
        k_half = hi + slot * (1 - 2 * hi)
        return remote(source(piece, k_half), spot(slot, piece, r), xb_s.at[piece], x_r.at[slot, piece, r], grp=pair, rep=y)

    def x_to_mid(piece):
        return remote(
            source(piece, far_half, x), spot_part(x, piece, r), xc_s.at[piece], x_r.at[2 + x, piece, r],
            grp=2 * zin + y, rep=y,
        )

    FAR = SUBS + 1
    NEAR = SUBS
    far_g = (g + 4) % 8

    def far_from_end():
        k_half = far_half + x * (1 - 2 * far_half)
        return remote(source(FAR, k_half), spot(x, FAR, r), xd_s.at[0], x_r.at[x, FAR, r], grp=far_g, rep=y)

    def far_to_end():
        return remote(source(FAR, far_half), spot(0, FAR, r), xd_s.at[0], x_r.at[0, FAR, r], grp=far_g, rep=y)

    def far_to_mid():
        return remote(
            source(FAR, near_half, x), spot_part(x, FAR, r), xd_s.at[1], x_r.at[2 + x, FAR, r],
            grp=2 * zin + y, rep=y,
        )

    def send_piece(piece):
        x_to_away(piece).start()

        @pl.when(end)
        def _():
            x_to_mid(piece).start()

        @pl.when(home)
        def _():
            x_local(piece, 0, near_half).start()

            @pl.when(mid)
            def _():
                x_local(piece, 1, far_half).start()

        @pl.when(away)
        def _():
            x_to_home(piece, 0, near_half).start()

            @pl.when(mid)
            def _():
                x_to_home(piece, 1, far_half).start()

    raw[0].wait()
    norm(span + drows, drows)

    @pl.when(mid)
    def _():
        far_to_end().start()
        far_to_mid().start()

    @pl.when(end)
    def _():
        far_from_end().start()

    @pl.when(mid)
    def _():
        for k in range(2, ALL):
            w_copy(g, k, True, 0, k >= BROAD).start()

    raw[1].wait()
    norm(span, drows)
    send_piece(NEAR)
    raw[2].wait()
    for s in range(SUBS):
        norm(s * sub, sub)
        send_piece(s)
    for k in (2, 3):
        w_cross(k).start()

    @pl.loop(0, rows_all // 16)
    def _(i):
        acc_ref[pl.ds(pl.multiple_of(i * 16, 16), 16), :] = jnp.zeros((16, cols), jnp.float32)

    across = {"grp": pair}
    beside = {"tp": 1 - x}
    MAIN = [NEAR] + list(range(SUBS))

    def x_forward(slot, piece, rr, way, device):
        where = spot(slot, piece, rr)
        return remote(where, where, xf_s.at[way, slot, piece, rr], x_r.at[slot, piece, rr], **device)

    def part_forward(part, piece, rr, way, device):
        where = spot_part(part, piece, rr)
        return remote(where, where, xf_s.at[way, 2 + part, piece, rr], x_r.at[2 + part, piece, rr], **device)

    def arrived(make, slot, piece, rr):
        make(slot, piece, rr, 0, {"rep": 1 - r}).wait_recv()

    def relay(make, slot, piece, ways):
        for rr in (0, 1):
            arrived(make, slot, piece, rr)
            for way in ways:
                make(slot, piece, rr, way, (across, beside)[way]).start()

    def settle(make, slot, piece, ways):
        for rr in (0, 1):
            for way in ways:
                make(slot, piece, rr, way, (across, beside)[way]).wait_send()

    EARLY = MAIN[:3]
    LATER = MAIN[3:]

    def forward_early(act):
        @pl.when(home & end)
        def _():
            act(x_forward, 0, FAR, (0,))

        @pl.when(home & mid)
        def _():
            act(x_forward, x, FAR, (0, 1))
            for piece in [FAR] + EARLY:
                act(part_forward, x, piece, (0, 1))

        @pl.when(away & mid)
        def _():
            for piece in EARLY:
                act(x_forward, x, piece, (1,))

    def forward_first(act):
        @pl.when(home & mid)
        def _():
            for piece in LATER:
                act(part_forward, x, piece, (0, 1))

        @pl.when(away & mid)
        def _():
            for piece in LATER[:-1]:
                act(x_forward, x, piece, (1,))

    def forward_late(act):
        @pl.when(away & mid)
        def _():
            act(x_forward, x, LATER[-1], (1,))
            act(x_forward, x, FAR, (1,))

    def forward_part(act, pieces):
        @pl.when(away & mid)
        def _():
            for piece in pieces:
                act(part_forward, x, piece, (1,))

    def wait_x():
        @pl.when(home)
        def _():
            def both(slot, k_half):
                for piece in MAIN:
                    x_local(piece, slot, k_half).wait()
                    arrived(x_forward, slot, piece, 1 - r)

            both(0, near_half)

            @pl.when(mid)
            def _():
                both(1, far_half)
                for rr in (0, 1):
                    arrived(x_forward, 1 - x, FAR, rr)

        @pl.when(away)
        def _():
            slot = jnp.where(mid, 1 - x, 0)
            for piece in MAIN + [FAR]:
                for rr in (0, 1):
                    arrived(x_forward, slot, piece, rr)

    def wait_part():
        @pl.when(mid)
        def _():
            for piece in MAIN + [FAR]:
                for rr in (0, 1):
                    arrived(part_forward, 1 - x, piece, rr)

    def pass_w(k, slim=False, first=True, second=True):
        def outer(yy):
            o = 2 * zout + yy
            w_arrived(o, k, r, slim)
            w_copy(o, k, False, 0, slim).start()
            w_copy(o, k, False, 2, slim).start()

        if first:
            @pl.when(mid)
            def _():
                outer(y)

            w_arrived(pair, k, r, slim)
            w_copy(pair, k, False, 0, slim).start()

            @pl.when(mid)
            def _():
                w_copy(pair, k, False, 1, slim).start()

            w_copy(pair, k, False, 2, slim).start()

        if second:
            @pl.when(mid)
            def _():
                outer(1 - y)

    def take_w(k, slim=False):
        def over(layer):
            for yy in (y, 1 - y):
                o = 2 * layer + yy
                w_arrived(o, k, r, slim)
                w_copy(o, k, False, 2, slim).start()

        over(zin)

        @pl.when(mid)
        def _():
            over(zin + 1 - 2 * hi)
            for yy in (0, 1):
                w_arrived(2 * zout + yy, k, 1 - r, slim)
            for i in range(sides):
                w_arrived(sides * (1 - hi) + i, k, 1 - r, slim)

        @pl.when(end)
        def _():
            for yy in (0, 1):
                w_arrived(2 * zin + yy, k, 1 - r, slim)

        w_arrived(pair, k, 1 - r, slim)

    def p_copy(k, slim=False):
        if slim:
            src, dst = pbn_ref.at[k - BROAD], landn_ref.at[k - BROAD]
        else:
            src, dst = pb_ref.at[k], land_ref.at[k]
        return remote(src, dst, p_s.at[k], p_r.at[k], grp=2 * zout + y)

    def tile(slot, i, h, slim):
        rows = pl.ds(i * share, share)
        return wt_ref.at[slot, rows, pl.ds(h * HD, HD)] if slim else wt_ref.at[slot, rows, :]

    def fetch(k, base, h, slot, slim):
        heads = (0, 1) if slim else (h,)
        for i in range(sides):
            o = base + i
            for c, hh in enumerate(heads):
                dst = tile(slot, i, c, slim)

                @pl.when(o == g)
                def _():
                    pltpu.make_async_copy(own_cols(y, hh, k, slim), dst, t_s.at[slot, i, c]).start()

                @pl.when(o != g)
                def _():
                    pltpu.make_async_copy(landing(o, k, hh, slim), dst, t_s.at[slot, i, c]).start()

    def fetched(slot, slim):
        for i in range(sides):
            for c in range(2 if slim else 1):
                dst = tile(slot, i, c, slim)
                pltpu.make_async_copy(dst, dst, t_s.at[slot, i, c]).wait()

    far_base = sides * (1 - hi)
    near_base = sides * hi

    def compute(k, slim=False):
        per = 1 if slim else 2
        steps = 2 * per

        @pl.when(mid)
        def _():
            fetch(k, far_base, 0, 0, slim)

        @pl.when(end)
        def _():
            fetch(k, near_base, 0, per % 2, slim)

        @pl.loop(0, steps)
        def _(j):
            slot = j % 2
            n = j + 1

            @pl.when((j >= per) | mid)
            def _():
                @pl.when(n < steps)
                def _():
                    side = n // per
                    fetch(k, far_base + side * (near_base - far_base), n % per, n % 2, slim)

                fetched(slot, slim)
                product = jnp.dot(xh_ref[1 - j // per], wt_ref[slot], preferred_element_type=jnp.float32)
                if slim:
                    for h in (0, 1):
                        at = pl.ds(pl.multiple_of(h * head + offset(k, slim), 128), HD)
                        acc_ref[:, at] += product[:, h * HD:(h + 1) * HD]
                else:
                    acc_ref[:, pl.ds(pl.multiple_of((j % 2) * head + offset(k), 128), WIDE)] += product

    def partial(k, slim=False):
        per = 1 if slim else 2
        fetch(k, far_base, 0, 0, slim)

        @pl.loop(0, per)
        def _(j):
            @pl.when(j + 1 < per)
            def _():
                fetch(k, far_base, 1, 1, slim)

            fetched(j, slim)
            value = jnp.dot(xh_ref[2], wt_ref[j], preferred_element_type=jnp.float32).astype(jnp.bfloat16)
            if slim:
                pbn_ref[k - BROAD] = value
            else:
                pb_ref[k, :, pl.ds(pl.multiple_of(j * WIDE, 128), WIDE)] = value

        p_copy(k, slim).start()

    def add_partial(k, slim=False):
        w = HD if slim else WIDE
        if slim:
            src, dst = landn_ref.at[k - BROAD], pbn_ref.at[0]
        else:
            src, dst = land_ref.at[k], pb_ref.at[0]
        remote(dst, src, p_s.at[k], p_r.at[k], grp=2 * zin + y).wait_recv()
        take = pltpu.make_async_copy(src, dst, l_s.at[3])
        take.start()
        take.wait()

        @pl.loop(0, rows_all // 16)
        def _(i):
            rows = pl.ds(pl.multiple_of(i * 16, 16), 16)
            for h in (0, 1):
                place_h = pl.ds(pl.multiple_of(h * head + offset(k, slim), 128), w)
                value = pbn_ref[0, rows, h * w:(h + 1) * w] if slim else pb_ref[0, rows, h * w:(h + 1) * w]
                acc_ref[rows, place_h] += value.astype(jnp.float32)

    prompt = g - y + r
    prompt_rows = 2 * span
    valid = len_ref[prompt]
    block = 256 if prompt_rows % 256 == 0 else prompt_rows
    blocks = [(prompt_rows, rows_all - prompt_rows, rows_all)]
    blocks += [(start, block, start + block) for start in range(0, prompt_rows, block)]
    starts = (0, prompt_rows, prompt_rows + 2 * drows)
    sizes = (span, drows, drows)
    width = QPK * HD

    def mask_place(index):
        top = 0
        for start, size, keys in blocks[:index]:
            top += size
        return slice(top, top + blocks[index][1]), slice(0, blocks[index][2])

    def make_tables():
        step = lax.broadcasted_iota(jnp.int32, (rows_all - prompt_rows, HD), 0) % STEPS
        for table, out in ((cos_tab_ref, cos_ref), (sin_tab_ref, sin_ref)):
            out[:prompt_rows, :] = table[:prompt_rows, :]
            picked = jnp.zeros((rows_all - prompt_rows, HD), jnp.float32)
            for i in range(STEPS):
                picked = jnp.where(step == i, table[pl.ds(valid + i, 1), :], picked)
            out[prompt_rows:, :] = picked

    def make_masks():
        for index, (start, size, keys) in enumerate(blocks):
            shape = (size, keys)
            row = lax.broadcasted_iota(jnp.int32, shape, 0) + start
            col = lax.broadcasted_iota(jnp.int32, shape, 1)
            if start < prompt_rows:
                allowed = (col <= row) & (col < valid)
            else:
                same = ((row - prompt_rows) // STEPS == (col - prompt_rows) // STEPS) & (col <= row)
                allowed = (col < jnp.minimum(valid, prompt_rows)) | ((col >= prompt_rows) & same)
            m_ref[mask_place(index)] = jnp.where(allowed, 0.0, NEGATIVE)

    def target(f, h, c, line, slim):
        at = pl.ds(pl.multiple_of((line * 2 + h) * width + offset(f, slim), 128), HD if slim else WIDE)
        return (prefill_ref.at[0, :, at], out_decode_ref.at[0, 0, 0, :, at], out_decode_ref.at[0, 0, 1, :, at])[c]

    def out_piece(f, h, c, rr, slim):
        start = pl.multiple_of(starts[c] + rr * sizes[c], 16)
        rows = pl.ds(start, sizes[c])
        if slim:
            return out_ref.at[BROAD - 1, h, rows, pl.ds(pl.multiple_of((f - BROAD) * HD, 128), HD)]
        return out_ref.at[f - 1, h, rows, :]

    def out_send(f, h, c, rr, slim):
        grp = (prompt + 4) % 8 if c == 2 else prompt
        return remote(
            out_piece(f, h, c, rr, slim), target(f, h, c, y, slim), o_s.at[f - 1, h, c, rr], o_r.at[f - 1, h, c, y],
            grp=grp, rep=rr,
        )

    def out_keep(f, h, c, slim):
        return pltpu.make_async_copy(out_piece(f, h, c, r, slim), target(f, h, c, y, slim), o_l.at[f - 1, h, c])

    def out_receive(f, h, c, line, slim):
        remote(
            out_piece(f, h, c, 0, slim), target(f, h, c, line, slim), o_s.at[f - 1, h, c, 0],
            o_r.at[f - 1, h, c, line], rep=1 - r,
        ).wait_recv()

    def each_out(f, h, c, act, keep_act, slim):
        if c == 2:
            act(out_send(f, h, c, 0, slim))
            act(out_send(f, h, c, 1, slim))
            return

        @pl.when(home)
        def _():
            keep_act(out_keep(f, h, c, slim))
            act(out_send(f, h, c, 1 - r, slim))

        @pl.when(away)
        def _():
            act(out_send(f, h, c, 0, slim))
            act(out_send(f, h, c, 1, slim))

    def begin(copy):
        copy.start()

    def sent(copy):
        copy.wait_send()

    def kept(copy):
        copy.wait()

    factor = HD ** (-0.5) * math.log2(math.e)

    def part(h, first):
        at = pl.ds(pl.multiple_of(h * head + first, 128), HD)
        bias_at = pl.ds(pl.multiple_of(hidden_ref.shape[2] + y * cols + h * head + first, 128), HD)
        return acc_ref[:, at] + aux_ref[:, bias_at]

    def turned(v):
        return v * cos_ref[...] + pltpu.roll(v, HD // 2, 1) * sin_ref[...]

    def keys_values():
        for h in (0, 1):
            k_ref[h] = turned(part(h, QPK * HD)).astype(jnp.bfloat16)
            v_ref[h] = part(h, (QPK + 1) * HD).astype(jnp.bfloat16)

    def attend(f, slim=False):
        here = (0,) if slim else (0, 1)

        @pl.loop(0, 2)
        def _(h):
            for j in here:
                q_ref[j] = (turned(part(h, offset(f, slim) + j * HD)) * factor).astype(jnp.bfloat16)
            for index, (start, size, keys) in enumerate(blocks):
                for j in here:
                    s = lax.dot_general(
                        q_ref[j, start:start + size, :], k_ref[h, :keys, :], (((1,), (1,)), ((), ())),
                        preferred_element_type=jnp.float32,
                    ) + m_ref[mask_place(index)]
                    top = jnp.max(s, axis=-1, keepdims=True)
                    p = jnp.exp2(s - top)
                    total = jnp.sum(p, axis=-1, keepdims=True)
                    o = jnp.dot(p.astype(jnp.bfloat16), v_ref[h, :keys, :], preferred_element_type=jnp.float32)
                    o = (o / total).astype(jnp.bfloat16)
                    if slim:
                        out_ref[BROAD - 1, h, start:start + size, pl.ds(pl.multiple_of((f - BROAD) * HD, 128), HD)] = o
                    else:
                        out_ref[f - 1, h, start:start + size, j * HD:(j + 1) * HD] = o
                if index == 0:
                    each_out(f, h, 2, begin, begin, slim)
                    each_out(f, h, 1, begin, begin, slim)
            each_out(f, h, 0, begin, begin, slim)

    @pl.loop(0, BROAD + 6)
    def _(t):
        k = t - 2

        @pl.when(t < BROAD)
        def _():
            pass_w(t, second=False)

        @pl.when(t == 0)
        def _():
            forward_early(relay)

        @pl.when(t < BROAD)
        def _():
            pass_w(t, first=False)

        @pl.when(t < BROAD - 2)
        def _():
            own_sends(t + 2)

        @pl.when((t >= BROAD - 2) & (t < BROAD))
        def _():
            own_sends(t + 2, True)

        @pl.when(t == 0)
        def _():
            forward_first(relay)
            for kk in range(BROAD, ALL):
                w_cross(kk, True).start()
            make_masks()
            make_tables()

        @pl.when(t == 1)
        def _():
            forward_late(relay)

        @pl.when(t == 2)
        def _():
            wait_x()

        @pl.when(t == 3)
        def _():
            forward_part(relay, [FAR] + EARLY)

        @pl.when((k >= 0) & (k < BROAD))
        def _():
            take_w(k)

            @pl.when(mid & ((home & (t == 3)) | (away & (t == 4))))
            def _():
                wait_part()

            @pl.loop(0, BROAD)
            def _(kk):
                due = (home & ((t == 3) & (kk <= k) | (t > 3) & (kk == k))) | (away & ((t == 4) & (kk <= k) | (t > 4) & (kk == k)))

                @pl.when(mid & due)
                def _():
                    partial(kk)

            compute(k)

        @pl.when((k >= BROAD) & (k < ALL))
        def _():
            take_w(k, True)

            @pl.when(mid)
            def _():
                partial(k, True)

            compute(k, True)

        @pl.when(t == 3)
        def _():
            forward_part(relay, LATER)

        f = t - 4 + 2 * mid_count

        @pl.when(end & (f >= 0) & (f < BROAD))
        def _():
            add_partial(f)

        @pl.when(end & (f >= BROAD) & (f < ALL))
        def _():
            add_partial(f, True)

        @pl.when(f == 0)
        def _():
            keys_values()

        @pl.when((f > 0) & (f < BROAD))
        def _():
            attend(f)

        @pl.when((f >= BROAD) & (f < ALL))
        def _():
            attend(f, True)

        @pl.when(t == 3)
        def _():
            pass_w(BROAD, True)

        @pl.when(t == 3)
        def _():
            pass_w(BROAD + 1, True)

    def close_out(f, slim):
        for h in (0, 1):
            for c in range(3):
                each_out(f, h, c, sent, kept, slim)
                if c == 2:
                    out_receive(f, h, c, 0, slim)
                    out_receive(f, h, c, 1, slim)
                else:
                    out_receive(f, h, c, 1 - y, slim)

                    @pl.when(away)
                    def _():
                        out_receive(f, h, c, y, slim)

    @pl.loop(1, BROAD)
    def _(f):
        close_out(f, False)

    @pl.loop(BROAD, ALL)
    def _(f):
        close_out(f, True)

    @pl.when(mid)
    def _():
        for k in range(ALL):
            p_copy(k, k >= BROAD).wait_send()

    @pl.when(mid)
    def _():
        far_to_end().wait_send()
        far_to_mid().wait_send()

    @pl.when(end)
    def _():
        far_from_end().wait_send()

    for piece in [NEAR] + list(range(SUBS)):
        x_to_away(piece).wait_send()

        @pl.when(end)
        def _():
            x_to_mid(piece).wait_send()

        @pl.when(away)
        def _():
            x_to_home(piece, 0, near_half).wait_send()

            @pl.when(mid)
            def _():
                x_to_home(piece, 1, far_half).wait_send()

    forward_early(settle)
    forward_first(settle)
    forward_late(settle)
    forward_part(settle, [FAR] + MAIN)

    def close_w(k, slim):
        w_cross(k, slim).wait_send()
        for o in (g, pair):
            w_copy(o, k, False, 0, slim).wait_send()

            @pl.when(mid)
            def _():
                w_copy(o, k, False, 1, slim).wait_send()

        w_copy(pair, k, False, 2, slim).wait_send()

        @pl.when(mid)
        def _():
            for yy in (0, 1):
                w_copy(2 * zout + yy, k, False, 0, slim).wait_send()
                w_copy(2 * zout + yy, k, False, 2, slim).wait_send()
            for i in range(sides):
                w_copy(sides * (1 - hi) + i, k, False, 2, slim).wait_send()

        @pl.when(end)
        def _():
            for yy in (0, 1):
                w_copy(2 * zin + yy, k, False, 2, slim).wait_send()

    @pl.loop(0, BROAD)
    def _(k):
        close_w(k, False)

    @pl.loop(BROAD, ALL)
    def _(k):
        close_w(k, True)


def rope_rows(count):
    half_size = HD // 2
    frequency = np.float32(THETA) ** (-(np.arange(half_size, dtype=np.float32) * np.float32(2.0) / np.float32(HD)))
    angle = np.arange(count, dtype=np.float32)[:, None] * frequency.astype(np.float32)[None, :]
    cosine, sine = np.cos(angle), np.sin(angle)
    return np.concatenate([cosine, cosine], axis=-1), np.concatenate([-sine, sine], axis=-1)


def fused(hidden, decode_hidden, norm_gain, qkv_weight, qkv_bias, lengths):
    count = lax.axis_size("grp")
    own_rows = hidden.shape[1] + 2 * decode_hidden.shape[3]
    rows = 2 * own_rows
    positions = 2 * hidden.shape[1] + STEPS
    cosine, sine = rope_rows(positions + (-positions) % 8)
    aux = jnp.concatenate([norm_gain, qkv_bias]).astype(jnp.float32).reshape(1, -1)
    share = qkv_weight.shape[0]
    width = hidden.shape[2]
    cols = qkv_weight.shape[1] // 2
    out_width = 4 * QPK * HD
    pieces = SUBS + 2
    hbm = pl.BlockSpec(memory_space=pl.ANY)
    vmem = pl.BlockSpec(memory_space=pltpu.VMEM)
    smem = pl.BlockSpec(memory_space=pltpu.SMEM)
    dma = pltpu.SemaphoreType.DMA
    outs = BROAD
    return pl.pallas_call(
        fused_kernel,
        out_shape=(
            jax.ShapeDtypeStruct(hidden.shape[:2] + (out_width,), jnp.bfloat16),
            jax.ShapeDtypeStruct(decode_hidden.shape[:4] + (out_width,), jnp.bfloat16),
            jax.ShapeDtypeStruct((count, BROAD, 2, share, WIDE), jnp.bfloat16),
            jax.ShapeDtypeStruct((BROAD, rows, 2 * WIDE), jnp.bfloat16),
            jax.ShapeDtypeStruct((count, 2, 2, share, HD), jnp.bfloat16),
            jax.ShapeDtypeStruct((2, rows, WIDE), jnp.bfloat16),
        ),
        in_specs=[smem, hbm, hbm, vmem, hbm, vmem, vmem],
        out_specs=(hbm,) * 6,
        scratch_shapes=[
            pltpu.VMEM((rows, cols), jnp.float32),
            pltpu.VMEM((3, rows, width // 2), jnp.bfloat16),
            pltpu.VMEM((own_rows, width), jnp.bfloat16),
            pltpu.VMEM((2, width // 2, WIDE), jnp.bfloat16),
            pltpu.VMEM((BROAD, rows, 2 * WIDE), jnp.bfloat16),
            pltpu.VMEM((2, rows, WIDE), jnp.bfloat16),
            pltpu.VMEM((rows, HD), jnp.float32),
            pltpu.VMEM((rows, HD), jnp.float32),
            pltpu.VMEM((2, rows, HD), jnp.bfloat16),
            pltpu.VMEM((2, rows, HD), jnp.bfloat16),
            pltpu.VMEM((2, rows, HD), jnp.bfloat16),
            pltpu.VMEM((rows, rows), jnp.float32),
            pltpu.VMEM((outs, 2, rows, WIDE), jnp.bfloat16),
            dma((count, ALL)), dma((count, ALL)), dma((count, ALL)), dma((ALL,)),
            dma((count, ALL, 2)),
            dma((2, SUBS + 1)), dma((SUBS + 1,)), dma((SUBS + 1,)), dma((2,)),
            dma((2, 4, pieces, 2)), dma((4, pieces, 2)),
            dma((ALL,)), dma((ALL,)), dma((4,)), dma((2, 4, 2)),
            dma((GROUPS, 2, 3, 2)), dma((GROUPS, 2, 3, 2)), dma((GROUPS, 2, 3)),
        ],
        compiler_params=pltpu.CompilerParams(
            collective_id=0, has_side_effects=True, vmem_limit_bytes=60 << 20
        ),
        name="fused",
    )(lengths, hidden, decode_hidden, aux, qkv_weight, jnp.asarray(cosine), jnp.asarray(sine))[:2]


def on_device(hidden, decode_hidden, norm_gain, qkv_weight, qkv_bias, lengths):
    count = lax.axis_size("grp")
    reps = lax.axis_size("rep")
    head_block = (QPK + 2) * HD
    heads_here = qkv_bias.shape[0] // head_block
    if reps != 2 or count != 8 or lax.axis_size("tp") != 2 or heads_here != 4 or decode_hidden.shape[1] != 1:
        return plain_device(hidden, decode_hidden, norm_gain, qkv_weight, qkv_bias, lengths)
    return fused(hidden, decode_hidden, norm_gain, qkv_weight, qkv_bias, lengths)


def solution(mesh):
    return jax.shard_map(
        on_device,
        mesh=mesh,
        in_specs=(
            P("grp", "rep", None),
            P("grp", "rep", None, None, None),
            P(),
            P("grp", "tp"),
            P("tp"),
            P(),
        ),
        out_specs=(P("grp", "rep", "tp"), P("grp", "rep", None, None, "tp")),
        check_vma=False,
    )
```

```python
import jax
import jax.numpy as jnp
from jax import lax
from jax.experimental import pallas as pl
from jax.experimental.pallas import tpu as pltpu
from jax.sharding import PartitionSpec as P
import functools
import math
import numpy as np

HD = 128
QPK = 8
STEPS = 4


THETA = 1000000.0
EPSILON = 1e-06
NEGATIVE = -1e30


def shifted(block, axis, distance):
    devices = range(lax.axis_size(axis))
    route = [((i - distance) % len(devices), i) for i in devices]
    return lax.ppermute(block, axis, route)


def normalize(row_block, gain_row):
    widened = row_block.astype(jnp.float32)
    factor = lax.rsqrt(jnp.mean(widened * widened, axis=-1, keepdims=True) + EPSILON)
    return (widened * factor * gain_row.astype(jnp.float32)).astype(jnp.bfloat16)


def rope_tables(positions, head_size):
    half_size = head_size // 2
    frequency = THETA ** (-(jnp.arange(half_size, dtype=jnp.float32) * 2.0 / head_size))
    angle = positions.astype(jnp.float32)[:, None] * frequency[None, :]
    return (jnp.cos(angle), jnp.sin(angle))


def rotate(vector, cosine, sine_part):
    half_size = vector.shape[-1] // 2
    first_half = vector[..., :half_size]
    second = vector[..., half_size:]
    return jnp.concatenate(
        [first_half * cosine - second * sine_part, second * cosine + first_half * sine_part],
        axis=-1,
    )


def masked_max(scores, allowed):
    return jnp.max(jnp.where(allowed, scores, NEGATIVE), axis=-1, keepdims=True)


def combine_values(weight_matrix, value_matrix):
    return jnp.einsum(
        "aprk,kaz->rapz",
        weight_matrix.astype(jnp.bfloat16),
        value_matrix,
        preferred_element_type=jnp.float32,
    )


def pair_scores(query_matrix, key_matrix_rows, score_scale):
    return (
        jnp.einsum(
            "wjro,ujo->jrwu", query_matrix, key_matrix_rows, preferred_element_type=jnp.float32
        )
        * score_scale
    )


def decode_pair(
    query_matrix,
    own_keys,
    own_values,
    prompt_keys,
    prompt_values,
    valid_len,
    local_allowed,
    score_scale,
):
    key_slot_index = jnp.arange(prompt_keys.shape[0], dtype=jnp.int32)
    prompt_allowed = (key_slot_index < valid_len)[None, None, None, :]
    far_scores = pair_scores(query_matrix, prompt_keys, score_scale)
    near_scores = pair_scores(query_matrix, own_keys, score_scale)
    highest = jnp.maximum(
        masked_max(far_scores, prompt_allowed), masked_max(near_scores, local_allowed)
    )
    far_exp = jnp.where(prompt_allowed, jnp.exp(far_scores - highest), 0.0)
    near_exp = jnp.where(local_allowed, jnp.exp(near_scores - highest), 0.0)
    running = jnp.sum(far_exp, axis=-1, keepdims=True) + jnp.sum(near_exp, axis=-1, keepdims=True)
    return combine_values(far_exp / running, prompt_values) + combine_values(
        near_exp / running, own_values
    )


def plain_device(hidden, decode_hidden, norm_gain, qkv_weight, qkv_bias, lengths):
    prompt_count = lax.axis_size("grp")
    rep_count = lax.axis_size("rep")
    half_cycle = prompt_count // 2
    grp_here = lax.axis_index("grp")
    rep_here = lax.axis_index("rep")
    span_rows = hidden.shape[1]
    model_width = hidden.shape[2]
    head_block = (QPK + 2) * HD
    heads_here = qkv_bias.shape[0] // head_block
    decode_rows = decode_hidden.shape[3]
    score_scale = HD ** (-0.5)
    prefill_normed = normalize(hidden[0], norm_gain)
    decode_normed = normalize(decode_hidden.reshape(2 * decode_rows, model_width), norm_gain)
    normed = jnp.concatenate([prefill_normed, decode_normed], axis=0)
    share_cols = qkv_weight.shape[1] // rep_count
    own_cols = lax.dynamic_slice_in_dim(qkv_weight, rep_here * share_cols, share_cols, 1)
    columns = lax.all_gather(own_cols, "grp", axis=0, tiled=True)
    complete = lax.all_gather(columns, "rep", axis=1, tiled=True)
    projected = jnp.dot(normed, complete, preferred_element_type=jnp.float32)
    projected = (projected + qkv_bias.astype(jnp.float32)).reshape(
        normed.shape[0], heads_here, QPK + 2, HD
    )
    index_table = jnp.arange(prompt_count, dtype=jnp.int32)

    def length_of(prompt):
        return jnp.sum(jnp.where(index_table == prompt, lengths, 0))

    own_len = length_of(grp_here)
    far_len = length_of((grp_here + half_cycle) % prompt_count)
    row_position = rep_here * span_rows + jnp.arange(span_rows, dtype=jnp.int32)
    local_ids = jnp.arange(decode_rows, dtype=jnp.int32)
    step_ids = local_ids % STEPS
    sample_ids = local_ids // STEPS
    positions = jnp.concatenate([row_position, own_len + step_ids, far_len + step_ids])
    cosine, sine_part = rope_tables(positions, HD)
    query_matrix = rotate(
        projected[:, :, :QPK], cosine[:, None, None, :], sine_part[:, None, None, :]
    ).astype(jnp.bfloat16)
    key_matrix_rows = rotate(
        projected[:, :, QPK], cosine[:, None, :], sine_part[:, None, :]
    ).astype(jnp.bfloat16)
    value_matrix = projected[:, :, QPK + 1].astype(jnp.bfloat16)
    cache_keys, cache_values = (
        lax.all_gather(key_matrix_rows[:span_rows], "rep", axis=0, tiled=True),
        lax.all_gather(value_matrix[:span_rows], "rep", axis=0, tiled=True),
    )
    key_pos = jnp.arange(cache_keys.shape[0], dtype=jnp.int32)
    allowed = ((key_pos[None, :] <= row_position[:, None]) & (key_pos[None, :] < own_len))[
        None, None
    ]
    scores = pair_scores(query_matrix[:span_rows], cache_keys, score_scale)
    highest = masked_max(scores, allowed)
    exponent = jnp.where(allowed, jnp.exp(scores - highest), 0.0)
    weight_matrix = exponent / jnp.sum(exponent, axis=-1, keepdims=True)
    attended = combine_values(weight_matrix, cache_values)
    prefill_out = attended.astype(jnp.bfloat16).reshape(1, span_rows, heads_here * QPK * HD)
    decode_queries = query_matrix[span_rows:].reshape(2, decode_rows, heads_here, QPK, HD)
    decode_keys = key_matrix_rows[span_rows:].reshape(2, decode_rows, heads_here, HD)
    decode_values = value_matrix[span_rows:].reshape(2, decode_rows, heads_here, HD)
    local_allowed = (
        (sample_ids[None, :] == sample_ids[:, None]) & (step_ids[None, :] <= step_ids[:, None])
    )[None, None]
    near_out = decode_pair(
        decode_queries[0],
        decode_keys[0],
        decode_values[0],
        cache_keys,
        cache_values,
        own_len,
        local_allowed,
        score_scale,
    )
    far_keys, far_values = shifted((cache_keys, cache_values), "grp", half_cycle)
    far_out = decode_pair(
        decode_queries[1],
        decode_keys[1],
        decode_values[1],
        far_keys,
        far_values,
        far_len,
        local_allowed,
        score_scale,
    )
    decode_out = (
        jnp.stack([near_out, far_out])
        .astype(jnp.bfloat16)
        .reshape(1, 1, 2, decode_rows, heads_here * QPK * HD)
    )
    return (prefill_out, decode_out)


MESH = pl.DeviceIdType.MESH
SUBS = 4
GROUPS = QPK // 2 + 1
WIDE = 2 * HD
BROAD = GROUPS - 1
ALL = GROUPS + 1


def fused_kernel(
    len_ref, hidden_ref, decode_ref, aux_ref, w_ref, cos_tab_ref, sin_tab_ref,
    prefill_ref, out_decode_ref, wbuf_ref, land_ref, wnar_ref, landn_ref,
    acc_ref, xh_ref, nv_ref, wt_ref, pb_ref, pbn_ref, cos_ref, sin_ref, q_ref, k_ref, v_ref, m_ref, out_ref,
    wi_s, wo_s, wb_s, wy_s, w_r,
    xa_s, xb_s, xc_s, xd_s, xf_s, x_r,
    p_s, p_r, l_s, t_s, o_s, o_r, o_l,
):
    g = lax.axis_index("grp")
    r = lax.axis_index("rep")
    x = lax.axis_index("tp")
    z = g // 2
    y = g % 2
    hi = z // 2
    zin = z + 1 - 2 * hi
    zout = z - 1 + 2 * hi
    mid = (z == 1) | (z == 2)
    end = (z == 0) | (z == 3)
    mid_count = (z // 2 + z % 2) % 2
    home = r == y
    away = r != y
    span = hidden_ref.shape[1]
    drows = decode_ref.shape[3]
    share = w_ref.shape[0]
    cols = acc_ref.shape[1]
    head = cols // 2
    half = xh_ref.shape[2]
    quarter = half // 2
    rows_all = acc_ref.shape[0]
    sub = span // SUBS
    sides = 4

    barrier = pltpu.get_barrier_semaphore()

    def greet(grp, rep, tp):
        pl.semaphore_signal(
            barrier, inc=1, device_id={"grp": grp, "rep": rep, "tp": tp}, device_id_type=MESH
        )

    pair = 2 * z + 1 - y
    greet(g, 1 - r, x)
    greet(g, r, 1 - x)
    for c in (0, 1):
        greet(pair, c, x)
        greet((g + 4) % 8, c, x)
        greet((g + 4) % 8 + 1 - 2 * y, c, x)
        greet(2 * zin + y, c, x)

    @pl.when(mid)
    def _():
        for c in (0, 1):
            greet(2 * zout + y, c, x)
        pl.semaphore_wait(barrier, 12)

    @pl.when(end)
    def _():
        pl.semaphore_wait(barrier, 10)

    def offset(k, slim=False):
        if slim:
            return (QPK - 2 + k - BROAD) * HD
        return ((k + GROUPS - 1) % GROUPS) * WIDE

    def own_cols(line, h, k, slim=False):
        first = pl.multiple_of(line * cols + h * head + offset(k, slim), 128)
        return w_ref.at[:, pl.ds(first, HD if slim else WIDE)]

    def landing(o, k, h, slim):
        return wnar_ref.at[o, k - BROAD, h] if slim else wbuf_ref.at[o, k, h]

    def remote(src, dst, ssem, rsem, **device):
        return pltpu.make_async_remote_copy(
            src, dst, ssem, rsem, device_id=device, device_id_type=MESH
        )

    def w_copy(o, k, own, kind, slim=False):
        dst = landing(o, k, r, slim)
        src = own_cols(y, r, k, slim) if own else dst
        if kind == 0:
            return remote(src, dst, wi_s.at[o, k], w_r.at[o, k, r], grp=2 * zin + y)
        if kind == 1:
            return remote(src, dst, wo_s.at[o, k], w_r.at[o, k, r], grp=2 * zout + y)
        return remote(src, dst, wb_s.at[o, k], w_r.at[o, k, r], rep=1 - r)

    def w_cross(k, slim=False):
        return remote(own_cols(1 - y, r, k, slim), landing(g, k, r, slim), wy_s.at[k], w_r.at[g, k, r], grp=pair)

    def w_arrived(o, k, h, slim=False):
        where = landing(o, k, h, slim)
        remote(where, where, wb_s.at[o, k], w_r.at[o, k, h], rep=1 - r).wait_recv()

    def own_sends(k, slim=False):
        @pl.when(end)
        def _():
            w_copy(g, k, True, 0, slim).start()

    w_cross(0).start()
    for k in (0, 1):
        w_copy(g, k, True, 0).start()
    w_cross(1).start()

    @pl.when(mid)
    def _():
        for k in range(ALL):
            w_copy(g, k, True, 1, k >= BROAD).start()

    raw = [
        pltpu.make_async_copy(decode_ref.at[0, 0, 1], nv_ref.at[pl.ds(span + drows, drows), :], l_s.at[0]),
        pltpu.make_async_copy(decode_ref.at[0, 0, 0], nv_ref.at[pl.ds(span, drows), :], l_s.at[1]),
        pltpu.make_async_copy(hidden_ref.at[0], nv_ref.at[pl.ds(0, span), :], l_s.at[2]),
    ]
    for copy in raw:
        copy.start()

    gain = aux_ref[:, :hidden_ref.shape[2]]

    def norm(first, n):
        @pl.loop(0, n // 16)
        def _(i):
            rows = pl.ds(pl.multiple_of(first + i * 16, 16), 16)
            wide = nv_ref[rows, :].astype(jnp.float32)
            factor = lax.rsqrt(jnp.mean(wide * wide, axis=-1, keepdims=True) + EPSILON)
            nv_ref[rows, :] = (wide * factor * gain).astype(jnp.bfloat16)

    def place(piece, rr):
        if piece < SUBS:
            return pl.multiple_of(rr * span + piece * sub, 16), sub
        return pl.multiple_of(2 * span + ((piece - SUBS) * 2 + rr) * drows, 16), drows

    def source(piece, k_half, part=None):
        start, n = (piece * sub, sub) if piece < SUBS else (span + (piece - SUBS) * drows, drows)
        if part is None:
            return nv_ref.at[pl.ds(start, n), pl.ds(pl.multiple_of(k_half * half, 128), half)]
        return nv_ref.at[pl.ds(start, n), pl.ds(pl.multiple_of(k_half * half + part * quarter, 128), quarter)]

    def spot(slot, piece, rr):
        start, n = place(piece, rr)
        return xh_ref.at[slot, pl.ds(start, n), :]

    def spot_part(part, piece, rr):
        start, n = place(piece, rr)
        return xh_ref.at[2, pl.ds(start, n), pl.ds(pl.multiple_of(part * quarter, 128), quarter)]

    near_half = hi
    far_half = 1 - hi

    def x_to_home(piece, slot, k_half):
        return remote(source(piece, k_half), spot(slot, piece, r), xa_s.at[slot, piece], x_r.at[slot, piece, r], rep=y)

    def x_local(piece, slot, k_half):
        return pltpu.make_async_copy(source(piece, k_half), spot(slot, piece, r), x_r.at[slot, piece, r])

    def x_to_away(piece):
        slot = jnp.where(mid, x, 0)
        k_half = hi + slot * (1 - 2 * hi)
        return remote(source(piece, k_half), spot(slot, piece, r), xb_s.at[piece], x_r.at[slot, piece, r], grp=pair, rep=y)

    def x_to_mid(piece):
        return remote(
            source(piece, far_half, x), spot_part(x, piece, r), xc_s.at[piece], x_r.at[2 + x, piece, r],
            grp=2 * zin + y, rep=y,
        )

    FAR = SUBS + 1
    NEAR = SUBS
    far_g = (g + 4) % 8

    def far_from_end():
        k_half = far_half + x * (1 - 2 * far_half)
        return remote(source(FAR, k_half), spot(x, FAR, r), xd_s.at[0], x_r.at[x, FAR, r], grp=far_g, rep=y)

    def far_to_end():
        return remote(source(FAR, far_half), spot(0, FAR, r), xd_s.at[0], x_r.at[0, FAR, r], grp=far_g, rep=y)

    def far_to_mid():
        return remote(
            source(FAR, near_half, x), spot_part(x, FAR, r), xd_s.at[1], x_r.at[2 + x, FAR, r],
            grp=2 * zin + y, rep=y,
        )

    def send_piece(piece):
        x_to_away(piece).start()

        @pl.when(end)
        def _():
            x_to_mid(piece).start()

        @pl.when(home)
        def _():
            x_local(piece, 0, near_half).start()

            @pl.when(mid)
            def _():
                x_local(piece, 1, far_half).start()

        @pl.when(away)
        def _():
            x_to_home(piece, 0, near_half).start()

            @pl.when(mid)
            def _():
                x_to_home(piece, 1, far_half).start()

    raw[0].wait()
    norm(span + drows, drows)

    @pl.when(mid)
    def _():
        far_to_end().start()
        far_to_mid().start()

    @pl.when(end)
    def _():
        far_from_end().start()

    @pl.when(mid)
    def _():
        for k in range(2, ALL):
            w_copy(g, k, True, 0, k >= BROAD).start()

    raw[1].wait()
    norm(span, drows)
    send_piece(NEAR)
    raw[2].wait()
    for s in range(SUBS):
        norm(s * sub, sub)
        send_piece(s)
    for k in range(2, ALL):
        w_cross(k, k >= BROAD).start()

    @pl.loop(0, rows_all // 16)
    def _(i):
        acc_ref[pl.ds(pl.multiple_of(i * 16, 16), 16), :] = jnp.zeros((16, cols), jnp.float32)

    across = {"grp": pair}
    beside = {"tp": 1 - x}
    MAIN = [NEAR] + list(range(SUBS))

    def x_forward(slot, piece, rr, way, device):
        where = spot(slot, piece, rr)
        return remote(where, where, xf_s.at[way, slot, piece, rr], x_r.at[slot, piece, rr], **device)

    def part_forward(part, piece, rr, way, device):
        where = spot_part(part, piece, rr)
        return remote(where, where, xf_s.at[way, 2 + part, piece, rr], x_r.at[2 + part, piece, rr], **device)

    def arrived(make, slot, piece, rr):
        make(slot, piece, rr, 0, {"rep": 1 - r}).wait_recv()

    def relay(make, slot, piece, ways):
        for rr in (0, 1):
            arrived(make, slot, piece, rr)
            for way in ways:
                make(slot, piece, rr, way, (across, beside)[way]).start()

    def settle(make, slot, piece, ways):
        for rr in (0, 1):
            for way in ways:
                make(slot, piece, rr, way, (across, beside)[way]).wait_send()

    EARLY = MAIN[:3]
    LATER = MAIN[3:]

    def forward_early(act):
        @pl.when(home & end)
        def _():
            act(x_forward, 0, FAR, (0,))

        @pl.when(home & mid)
        def _():
            act(x_forward, x, FAR, (0, 1))
            for piece in [FAR] + EARLY:
                act(part_forward, x, piece, (0, 1))

        @pl.when(away & mid)
        def _():
            for piece in EARLY:
                act(x_forward, x, piece, (1,))

    def forward_first(act):
        @pl.when(home & mid)
        def _():
            for piece in LATER:
                act(part_forward, x, piece, (0, 1))

        @pl.when(away & mid)
        def _():
            for piece in LATER[:-1]:
                act(x_forward, x, piece, (1,))

    def forward_late(act):
        @pl.when(away & mid)
        def _():
            act(x_forward, x, LATER[-1], (1,))
            act(x_forward, x, FAR, (1,))

    def forward_part(act, pieces):
        @pl.when(away & mid)
        def _():
            for piece in pieces:
                act(part_forward, x, piece, (1,))

    def wait_x():
        @pl.when(home)
        def _():
            def both(slot, k_half):
                for piece in MAIN:
                    x_local(piece, slot, k_half).wait()
                    arrived(x_forward, slot, piece, 1 - r)

            both(0, near_half)

            @pl.when(mid)
            def _():
                both(1, far_half)
                for rr in (0, 1):
                    arrived(x_forward, 1 - x, FAR, rr)

        @pl.when(away)
        def _():
            slot = jnp.where(mid, 1 - x, 0)
            for piece in MAIN + [FAR]:
                for rr in (0, 1):
                    arrived(x_forward, slot, piece, rr)

    def wait_part():
        @pl.when(mid)
        def _():
            for piece in MAIN + [FAR]:
                for rr in (0, 1):
                    arrived(part_forward, 1 - x, piece, rr)

    def pass_w(k, slim=False, first=True, second=True):
        def outer(yy):
            o = 2 * zout + yy
            w_arrived(o, k, r, slim)
            w_copy(o, k, False, 0, slim).start()
            w_copy(o, k, False, 2, slim).start()

        if first:
            @pl.when(mid)
            def _():
                outer(y)

            w_arrived(pair, k, r, slim)
            w_copy(pair, k, False, 0, slim).start()

            @pl.when(mid)
            def _():
                w_copy(pair, k, False, 1, slim).start()

            w_copy(pair, k, False, 2, slim).start()

        if second:
            @pl.when(mid)
            def _():
                outer(1 - y)

    def take_w(k, slim=False):
        def over(layer):
            for yy in (y, 1 - y):
                o = 2 * layer + yy
                w_arrived(o, k, r, slim)
                w_copy(o, k, False, 2, slim).start()

        over(zin)

        @pl.when(mid)
        def _():
            over(zin + 1 - 2 * hi)
            for yy in (0, 1):
                w_arrived(2 * zout + yy, k, 1 - r, slim)
            for i in range(sides):
                w_arrived(sides * (1 - hi) + i, k, 1 - r, slim)

        @pl.when(end)
        def _():
            for yy in (0, 1):
                w_arrived(2 * zin + yy, k, 1 - r, slim)

        w_arrived(pair, k, 1 - r, slim)

    def p_copy(k, slim=False):
        if slim:
            src, dst = pbn_ref.at[k - BROAD], landn_ref.at[k - BROAD]
        else:
            src, dst = pb_ref.at[k], land_ref.at[k]
        return remote(src, dst, p_s.at[k], p_r.at[k], grp=2 * zout + y)

    def tile(slot, i, h, slim):
        rows = pl.ds(i * share, share)
        return wt_ref.at[slot, rows, pl.ds(h * HD, HD)] if slim else wt_ref.at[slot, rows, :]

    def fetch(k, base, h, slot, slim):
        heads = (0, 1) if slim else (h,)
        for i in range(sides):
            o = base + i
            for c, hh in enumerate(heads):
                dst = tile(slot, i, c, slim)

                @pl.when(o == g)
                def _():
                    pltpu.make_async_copy(own_cols(y, hh, k, slim), dst, t_s.at[slot, i, c]).start()

                @pl.when(o != g)
                def _():
                    pltpu.make_async_copy(landing(o, k, hh, slim), dst, t_s.at[slot, i, c]).start()

    def fetched(slot, slim):
        for i in range(sides):
            for c in range(2 if slim else 1):
                dst = tile(slot, i, c, slim)
                pltpu.make_async_copy(dst, dst, t_s.at[slot, i, c]).wait()

    far_base = sides * (1 - hi)
    near_base = sides * hi

    def compute(k, slim=False):
        per = 1 if slim else 2
        steps = 2 * per

        @pl.when(mid)
        def _():
            fetch(k, far_base, 0, 0, slim)

        @pl.when(end)
        def _():
            fetch(k, near_base, 0, per % 2, slim)

        @pl.loop(0, steps)
        def _(j):
            slot = j % 2
            n = j + 1

            @pl.when((j >= per) | mid)
            def _():
                @pl.when(n < steps)
                def _():
                    side = n // per
                    fetch(k, far_base + side * (near_base - far_base), n % per, n % 2, slim)

                fetched(slot, slim)
                product = jnp.dot(xh_ref[1 - j // per], wt_ref[slot], preferred_element_type=jnp.float32)
                if slim:
                    for h in (0, 1):
                        at = pl.ds(pl.multiple_of(h * head + offset(k, slim), 128), HD)
                        acc_ref[:, at] += product[:, h * HD:(h + 1) * HD]
                else:
                    acc_ref[:, pl.ds(pl.multiple_of((j % 2) * head + offset(k), 128), WIDE)] += product

    def partial(k, slim=False):
        per = 1 if slim else 2
        fetch(k, far_base, 0, 0, slim)

        @pl.loop(0, per)
        def _(j):
            @pl.when(j + 1 < per)
            def _():
                fetch(k, far_base, 1, 1, slim)

            fetched(j, slim)
            value = jnp.dot(xh_ref[2], wt_ref[j], preferred_element_type=jnp.float32).astype(jnp.bfloat16)
            if slim:
                pbn_ref[k - BROAD] = value
            else:
                pb_ref[k, :, pl.ds(pl.multiple_of(j * WIDE, 128), WIDE)] = value

        p_copy(k, slim).start()

    def add_partial(k, slim=False):
        w = HD if slim else WIDE
        if slim:
            src, dst = landn_ref.at[k - BROAD], pbn_ref.at[0]
        else:
            src, dst = land_ref.at[k], pb_ref.at[0]
        remote(dst, src, p_s.at[k], p_r.at[k], grp=2 * zin + y).wait_recv()
        take = pltpu.make_async_copy(src, dst, l_s.at[3])
        take.start()
        take.wait()

        @pl.loop(0, rows_all // 16)
        def _(i):
            rows = pl.ds(pl.multiple_of(i * 16, 16), 16)
            for h in (0, 1):
                place_h = pl.ds(pl.multiple_of(h * head + offset(k, slim), 128), w)
                value = pbn_ref[0, rows, h * w:(h + 1) * w] if slim else pb_ref[0, rows, h * w:(h + 1) * w]
                acc_ref[rows, place_h] += value.astype(jnp.float32)

    prompt = g - y + r
    prompt_rows = 2 * span
    valid = len_ref[prompt]
    block = 256 if prompt_rows % 256 == 0 else prompt_rows
    blocks = [(prompt_rows, rows_all - prompt_rows, rows_all)]
    blocks += [(start, block, start + block) for start in range(0, prompt_rows, block)]
    starts = (0, prompt_rows, prompt_rows + 2 * drows)
    sizes = (span, drows, drows)
    width = QPK * HD

    def mask_place(index):
        top = 0
        for start, size, keys in blocks[:index]:
            top += size
        return slice(top, top + blocks[index][1]), slice(0, blocks[index][2])

    def make_tables():
        step = lax.broadcasted_iota(jnp.int32, (rows_all - prompt_rows, HD), 0) % STEPS
        for table, out in ((cos_tab_ref, cos_ref), (sin_tab_ref, sin_ref)):
            out[:prompt_rows, :] = table[:prompt_rows, :]
            picked = jnp.zeros((rows_all - prompt_rows, HD), jnp.float32)
            for i in range(STEPS):
                picked = jnp.where(step == i, table[pl.ds(valid + i, 1), :], picked)
            out[prompt_rows:, :] = picked

    def make_masks():
        for index, (start, size, keys) in enumerate(blocks):
            shape = (size, keys)
            row = lax.broadcasted_iota(jnp.int32, shape, 0) + start
            col = lax.broadcasted_iota(jnp.int32, shape, 1)
            if start < prompt_rows:
                allowed = (col <= row) & (col < valid)
            else:
                same = ((row - prompt_rows) // STEPS == (col - prompt_rows) // STEPS) & (col <= row)
                allowed = (col < jnp.minimum(valid, prompt_rows)) | ((col >= prompt_rows) & same)
            m_ref[mask_place(index)] = jnp.where(allowed, 0.0, NEGATIVE)

    def target(f, h, c, line, slim):
        at = pl.ds(pl.multiple_of((line * 2 + h) * width + offset(f, slim), 128), HD if slim else WIDE)
        return (prefill_ref.at[0, :, at], out_decode_ref.at[0, 0, 0, :, at], out_decode_ref.at[0, 0, 1, :, at])[c]

    def out_piece(f, h, c, rr, slim):
        start = pl.multiple_of(starts[c] + rr * sizes[c], 16)
        rows = pl.ds(start, sizes[c])
        if slim:
            return out_ref.at[BROAD - 1, h, rows, pl.ds(pl.multiple_of((f - BROAD) * HD, 128), HD)]
        return out_ref.at[f - 1, h, rows, :]

    def out_send(f, h, c, rr, slim):
        grp = (prompt + 4) % 8 if c == 2 else prompt
        return remote(
            out_piece(f, h, c, rr, slim), target(f, h, c, y, slim), o_s.at[f - 1, h, c, rr], o_r.at[f - 1, h, c, y],
            grp=grp, rep=rr,
        )

    def out_keep(f, h, c, slim):
        return pltpu.make_async_copy(out_piece(f, h, c, r, slim), target(f, h, c, y, slim), o_l.at[f - 1, h, c])

    def out_receive(f, h, c, line, slim):
        remote(
            out_piece(f, h, c, 0, slim), target(f, h, c, line, slim), o_s.at[f - 1, h, c, 0],
            o_r.at[f - 1, h, c, line], rep=1 - r,
        ).wait_recv()

    def each_out(f, h, c, act, keep_act, slim):
        if c == 2:
            act(out_send(f, h, c, 0, slim))
            act(out_send(f, h, c, 1, slim))
            return

        @pl.when(home)
        def _():
            keep_act(out_keep(f, h, c, slim))
            act(out_send(f, h, c, 1 - r, slim))

        @pl.when(away)
        def _():
            act(out_send(f, h, c, 0, slim))
            act(out_send(f, h, c, 1, slim))

    def begin(copy):
        copy.start()

    def sent(copy):
        copy.wait_send()

    def kept(copy):
        copy.wait()

    factor = HD ** (-0.5) * math.log2(math.e)

    def part(h, first):
        at = pl.ds(pl.multiple_of(h * head + first, 128), HD)
        bias_at = pl.ds(pl.multiple_of(hidden_ref.shape[2] + y * cols + h * head + first, 128), HD)
        return acc_ref[:, at] + aux_ref[:, bias_at]

    def turned(v):
        return v * cos_ref[...] + pltpu.roll(v, HD // 2, 1) * sin_ref[...]

    def keys_values():
        for h in (0, 1):
            k_ref[h] = turned(part(h, QPK * HD)).astype(jnp.bfloat16)
            v_ref[h] = part(h, (QPK + 1) * HD).astype(jnp.bfloat16)

    def attend(f, slim=False):
        here = (0,) if slim else (0, 1)

        @pl.loop(0, 2)
        def _(h):
            for j in here:
                q_ref[j] = (turned(part(h, offset(f, slim) + j * HD)) * factor).astype(jnp.bfloat16)
            for index, (start, size, keys) in enumerate(blocks):
                for j in here:
                    s = lax.dot_general(
                        q_ref[j, start:start + size, :], k_ref[h, :keys, :], (((1,), (1,)), ((), ())),
                        preferred_element_type=jnp.float32,
                    ) + m_ref[mask_place(index)]
                    top = jnp.max(s, axis=-1, keepdims=True)
                    p = jnp.exp2(s - top)
                    total = jnp.sum(p, axis=-1, keepdims=True)
                    o = jnp.dot(p.astype(jnp.bfloat16), v_ref[h, :keys, :], preferred_element_type=jnp.float32)
                    o = (o / total).astype(jnp.bfloat16)
                    if slim:
                        out_ref[BROAD - 1, h, start:start + size, pl.ds(pl.multiple_of((f - BROAD) * HD, 128), HD)] = o
                    else:
                        out_ref[f - 1, h, start:start + size, j * HD:(j + 1) * HD] = o
                if index == 0:
                    each_out(f, h, 2, begin, begin, slim)
                    each_out(f, h, 1, begin, begin, slim)
            each_out(f, h, 0, begin, begin, slim)

    @pl.loop(0, BROAD + 6)
    def _(t):
        k = t - 2

        @pl.when(t < BROAD)
        def _():
            pass_w(t, second=False)

        @pl.when(t == 0)
        def _():
            forward_early(relay)

        @pl.when(t < BROAD)
        def _():
            pass_w(t, first=False)

        @pl.when(t < BROAD - 2)
        def _():
            own_sends(t + 2)

        @pl.when((t >= BROAD - 2) & (t < BROAD))
        def _():
            own_sends(t + 2, True)

        @pl.when(t == 0)
        def _():
            forward_first(relay)
            make_masks()
            make_tables()

        @pl.when(t == 1)
        def _():
            forward_late(relay)

        @pl.when(t == 2)
        def _():
            wait_x()

        @pl.when(t == 3)
        def _():
            forward_part(relay, [FAR] + EARLY)

        @pl.when((k >= 0) & (k < BROAD))
        def _():
            take_w(k)

            @pl.when(mid & ((home & (t == 3)) | (away & (t == 4))))
            def _():
                wait_part()

            @pl.loop(0, BROAD)
            def _(kk):
                due = (home & ((t == 3) & (kk <= k) | (t > 3) & (kk == k))) | (away & ((t == 4) & (kk <= k) | (t > 4) & (kk == k)))

                @pl.when(mid & due)
                def _():
                    partial(kk)

            compute(k)

        @pl.when((k >= BROAD) & (k < ALL))
        def _():
            take_w(k, True)

            @pl.when(mid)
            def _():
                partial(k, True)

            compute(k, True)

        @pl.when(t == 3)
        def _():
            forward_part(relay, LATER)

        f = t - 4 + 2 * mid_count

        @pl.when(end & (f >= 0) & (f < BROAD))
        def _():
            add_partial(f)

        @pl.when(end & (f >= BROAD) & (f < ALL))
        def _():
            add_partial(f, True)

        @pl.when(f == 0)
        def _():
            keys_values()

        @pl.when((f > 0) & (f < BROAD))
        def _():
            attend(f)

        @pl.when((f >= BROAD) & (f < ALL))
        def _():
            attend(f, True)

        @pl.when(t == 3)
        def _():
            pass_w(BROAD, True)

        @pl.when(t == 3)
        def _():
            pass_w(BROAD + 1, True)

    def close_out(f, slim):
        for h in (0, 1):
            for c in range(3):
                each_out(f, h, c, sent, kept, slim)
                if c == 2:
                    out_receive(f, h, c, 0, slim)
                    out_receive(f, h, c, 1, slim)
                else:
                    out_receive(f, h, c, 1 - y, slim)

                    @pl.when(away)
                    def _():
                        out_receive(f, h, c, y, slim)

    @pl.loop(1, BROAD)
    def _(f):
        close_out(f, False)

    @pl.loop(BROAD, ALL)
    def _(f):
        close_out(f, True)

    @pl.when(mid)
    def _():
        for k in range(ALL):
            p_copy(k, k >= BROAD).wait_send()

    @pl.when(mid)
    def _():
        far_to_end().wait_send()
        far_to_mid().wait_send()

    @pl.when(end)
    def _():
        far_from_end().wait_send()

    for piece in [NEAR] + list(range(SUBS)):
        x_to_away(piece).wait_send()

        @pl.when(end)
        def _():
            x_to_mid(piece).wait_send()

        @pl.when(away)
        def _():
            x_to_home(piece, 0, near_half).wait_send()

            @pl.when(mid)
            def _():
                x_to_home(piece, 1, far_half).wait_send()

    forward_early(settle)
    forward_first(settle)
    forward_late(settle)
    forward_part(settle, [FAR] + MAIN)

    def close_w(k, slim):
        w_cross(k, slim).wait_send()
        for o in (g, pair):
            w_copy(o, k, False, 0, slim).wait_send()

            @pl.when(mid)
            def _():
                w_copy(o, k, False, 1, slim).wait_send()

        w_copy(pair, k, False, 2, slim).wait_send()

        @pl.when(mid)
        def _():
            for yy in (0, 1):
                w_copy(2 * zout + yy, k, False, 0, slim).wait_send()
                w_copy(2 * zout + yy, k, False, 2, slim).wait_send()
            for i in range(sides):
                w_copy(sides * (1 - hi) + i, k, False, 2, slim).wait_send()

        @pl.when(end)
        def _():
            for yy in (0, 1):
                w_copy(2 * zin + yy, k, False, 2, slim).wait_send()

    @pl.loop(0, BROAD)
    def _(k):
        close_w(k, False)

    @pl.loop(BROAD, ALL)
    def _(k):
        close_w(k, True)


def rope_rows(count):
    half_size = HD // 2
    frequency = np.float32(THETA) ** (-(np.arange(half_size, dtype=np.float32) * np.float32(2.0) / np.float32(HD)))
    angle = np.arange(count, dtype=np.float32)[:, None] * frequency.astype(np.float32)[None, :]
    cosine, sine = np.cos(angle), np.sin(angle)
    return np.concatenate([cosine, cosine], axis=-1), np.concatenate([-sine, sine], axis=-1)


def fused(hidden, decode_hidden, norm_gain, qkv_weight, qkv_bias, lengths):
    count = lax.axis_size("grp")
    own_rows = hidden.shape[1] + 2 * decode_hidden.shape[3]
    rows = 2 * own_rows
    positions = 2 * hidden.shape[1] + STEPS
    cosine, sine = rope_rows(positions + (-positions) % 8)
    aux = jnp.concatenate([norm_gain, qkv_bias]).astype(jnp.float32).reshape(1, -1)
    share = qkv_weight.shape[0]
    width = hidden.shape[2]
    cols = qkv_weight.shape[1] // 2
    out_width = 4 * QPK * HD
    pieces = SUBS + 2
    hbm = pl.BlockSpec(memory_space=pl.ANY)
    vmem = pl.BlockSpec(memory_space=pltpu.VMEM)
    smem = pl.BlockSpec(memory_space=pltpu.SMEM)
    dma = pltpu.SemaphoreType.DMA
    outs = BROAD
    return pl.pallas_call(
        fused_kernel,
        out_shape=(
            jax.ShapeDtypeStruct(hidden.shape[:2] + (out_width,), jnp.bfloat16),
            jax.ShapeDtypeStruct(decode_hidden.shape[:4] + (out_width,), jnp.bfloat16),
            jax.ShapeDtypeStruct((count, BROAD, 2, share, WIDE), jnp.bfloat16),
            jax.ShapeDtypeStruct((BROAD, rows, 2 * WIDE), jnp.bfloat16),
            jax.ShapeDtypeStruct((count, 2, 2, share, HD), jnp.bfloat16),
            jax.ShapeDtypeStruct((2, rows, WIDE), jnp.bfloat16),
        ),
        in_specs=[smem, hbm, hbm, vmem, hbm, vmem, vmem],
        out_specs=(hbm,) * 6,
        scratch_shapes=[
            pltpu.VMEM((rows, cols), jnp.float32),
            pltpu.VMEM((3, rows, width // 2), jnp.bfloat16),
            pltpu.VMEM((own_rows, width), jnp.bfloat16),
            pltpu.VMEM((2, width // 2, WIDE), jnp.bfloat16),
            pltpu.VMEM((BROAD, rows, 2 * WIDE), jnp.bfloat16),
            pltpu.VMEM((2, rows, WIDE), jnp.bfloat16),
            pltpu.VMEM((rows, HD), jnp.float32),
            pltpu.VMEM((rows, HD), jnp.float32),
            pltpu.VMEM((2, rows, HD), jnp.bfloat16),
            pltpu.VMEM((2, rows, HD), jnp.bfloat16),
            pltpu.VMEM((2, rows, HD), jnp.bfloat16),
            pltpu.VMEM((rows, rows), jnp.float32),
            pltpu.VMEM((outs, 2, rows, WIDE), jnp.bfloat16),
            dma((count, ALL)), dma((count, ALL)), dma((count, ALL)), dma((ALL,)),
            dma((count, ALL, 2)),
            dma((2, SUBS + 1)), dma((SUBS + 1,)), dma((SUBS + 1,)), dma((2,)),
            dma((2, 4, pieces, 2)), dma((4, pieces, 2)),
            dma((ALL,)), dma((ALL,)), dma((4,)), dma((2, 4, 2)),
            dma((GROUPS, 2, 3, 2)), dma((GROUPS, 2, 3, 2)), dma((GROUPS, 2, 3)),
        ],
        compiler_params=pltpu.CompilerParams(
            collective_id=0, has_side_effects=True, vmem_limit_bytes=60 << 20
        ),
        name="fused",
    )(lengths, hidden, decode_hidden, aux, qkv_weight, jnp.asarray(cosine), jnp.asarray(sine))[:2]


def on_device(hidden, decode_hidden, norm_gain, qkv_weight, qkv_bias, lengths):
    count = lax.axis_size("grp")
    reps = lax.axis_size("rep")
    head_block = (QPK + 2) * HD
    heads_here = qkv_bias.shape[0] // head_block
    if reps != 2 or count != 8 or lax.axis_size("tp") != 2 or heads_here != 4 or decode_hidden.shape[1] != 1:
        return plain_device(hidden, decode_hidden, norm_gain, qkv_weight, qkv_bias, lengths)
    return fused(hidden, decode_hidden, norm_gain, qkv_weight, qkv_bias, lengths)


def solution(mesh):
    return jax.shard_map(
        on_device,
        mesh=mesh,
        in_specs=(
            P("grp", "rep", None),
            P("grp", "rep", None, None, None),
            P(),
            P("grp", "tp"),
            P("tp"),
            P(),
        ),
        out_specs=(P("grp", "rep", "tp"), P("grp", "rep", None, None, "tp")),
        check_vma=False,
    )
```
